256 devices in a mesh: section: 4 (over y), task: 4 (over x), mp: 16 (over z, core).
Axes of the slice: x: 4, y: 4, z: 8, core: 2. Of those that a mesh axis runs over, the one named last changes fastest.
Arguments:
- hidden_in: bfloat16 [4, 256, 3584], P('task', 'mp'), may hold values from -6 to 6
- lengths: int32 [4], P('task'), may hold values from 128 to 256
- layer_targets: bfloat16 [4, 4, 256, 3584], P('section', 'task', 'mp'), may hold values from -27 to 27
- task_weights: float32 [4], replicated, may hold values from 0.25 to 1
- norm_gains: float32 [4, 2, 3584], P('section'), may hold values from 0.5 to 1.5
- query_weight: bfloat16 [4, 4, 3584, 4096], P('task', 'section', None, 'mp'), may hold values from -0.40089186 to 0.40089186
- key_weight: bfloat16 [4, 4, 3584, 2048], P('task', 'section', None, 'mp'), may hold values from -0.40089186 to 0.40089186
- value_weight: bfloat16 [4, 4, 3584, 2048], P('task', 'section', None, 'mp'), may hold values from -0.09375 to 0.09375
- output_weight: bfloat16 [4, 4, 4096, 3584], P('task', 'section', 'mp'), may hold values from -0.09375 to 0.09375
- query_fisher: bfloat16 [4, 4, 3584, 4096], P('task', 'section', None, 'mp'), may hold values from 0.0099487305 to 10
- key_fisher: bfloat16 [4, 4, 3584, 2048], P('task', 'section', None, 'mp'), may hold values from 0.0099487305 to 10
- value_fisher: bfloat16 [4, 4, 3584, 2048], P('task', 'section', None, 'mp'), may hold values from 0.0099487305 to 10
- output_fisher: bfloat16 [4, 4, 4096, 3584], P('task', 'section', 'mp'), may hold values from 0.0099487305 to 10
Outputs:
- hidden_out: bfloat16 [4, 4, 256, 3584], P('section', 'task', 'mp')
- losses: float32 [4, 4], P('section', 'task')
The draws below stay inside these ranges and needn't reach their ends.
All inputs are finite; a program needn't handle non-finite values.
Results may differ from the reference program's by a relative error of at most 0.04.
Values may be sent and summed in bfloat16 or wider, within the bound.
No kernel may reach another device: no remote copies, remote signals or barrier semaphores. Data moves between devices by JAX's collectives and lax.ppermute only.
A program may use at most 128 MiB of HBM per device.

```python
import math
import jax
import jax.numpy as jnp
from jax import lax

D = 3584
HEADS = 16
KV_HEADS = 8
HEAD_DIM = 256
LENGTH = 256
TASKS = 4
LAYERS = 4
SEQS = 4
N_MP = 16


def draw_layer_targets(key, part):
    positions = jnp.arange(LENGTH, dtype=jnp.float32) / LENGTH
    scale_key = jax.random.fold_in(key, 77)
    row_scales = jnp.exp(jax.random.uniform(scale_key, (LAYERS, SEQS), jnp.float32, -1.204, 1.0986))
    values = jax.random.truncated_normal(key, -4.0, 4.0, (LAYERS, SEQS, LENGTH, D), jnp.float32)
    values = values * (0.6 + 1.6 * positions)[None, None, :, None]
    values = values * row_scales[:, :, None, None]
    return values.astype(jnp.bfloat16)


def head_factors(key, seed_offset, head_count):
    factor_key = jax.random.fold_in(key, seed_offset)
    return jnp.exp(jax.random.uniform(factor_key, (LAYERS, head_count), jnp.float32, 0.0, 0.693147))


def projection_draw(key, seed_offset, head_count):
    array_shape = (TASKS, LAYERS, D, head_count * HEAD_DIM)
    entry_key = jax.random.fold_in(key, seed_offset)
    values = jax.random.truncated_normal(entry_key, -4.0, 4.0, array_shape, jnp.float32)
    factors = jnp.repeat(head_factors(key, seed_offset + 100, head_count), HEAD_DIM, axis=1)
    return (values * factors[None, :, None, :] * D ** (-0.5)).astype(jnp.bfloat16)


def draw_query_weight(key, part):
    return projection_draw(key, 11, HEADS)


def draw_key_weight(key, part):
    return projection_draw(key, 13, KV_HEADS)


def with_ends(result, rng, smallest, high):
    longest = result.shape.index(max(result.shape))
    spots = []
    for shift in (0, 1):
        where = [jax.random.randint(jax.random.fold_in(rng, axis), (), 0, length) for axis, length in enumerate(result.shape)]
        where[longest] = (where[longest] + shift) % result.shape[longest]
        spots.append(tuple(where))
    return result.at[spots[0]].set(smallest).at[spots[1]].set(high)


def levels(rng, shape, shards, smallest, high):
    gain = 1.0
    for axis_at, parts in shards:
        draws = jax.random.uniform(jax.random.fold_in(jax.random.fold_in(rng, 6), axis_at), (parts,), jnp.float32, smallest / len(shards), high / len(shards))
        gain = gain * jnp.repeat(jnp.exp(draws), shape[axis_at] // parts).reshape((-1,) + (1,) * (len(shape) - 1 - axis_at))
    return gain


def noise(own_key, shape, deviation, limit, pieces=(), kind=jnp.bfloat16):
    result = jax.random.normal(own_key, shape, jnp.float32) * deviation
    if len(pieces) > 0:
        result = levels(own_key, shape, pieces, -0.22, 0.18) * result
    return jnp.clip(result, min=-limit, max=limit).astype(kind)


def setup_inputs(seed: int = 0) -> dict:
    arg_keys = jax.random.split(jax.random.key(seed), 14)
    hidden_in = noise(arg_keys[0], (SEQS, LENGTH, D), 1.0, 6.0, ((0, 4), (1, 16)))
    lengths = with_ends(jax.random.randint(arg_keys[1], (SEQS,), LENGTH // 2, LENGTH + 1), jax.random.fold_in(arg_keys[1], 1), LENGTH // 2, LENGTH).astype(jnp.int32)
    layer_targets = draw_layer_targets(jax.random.fold_in(arg_keys[13], 71), 0)
    task_weights = jnp.clip(jnp.exp(jax.random.uniform(arg_keys[3], (TASKS,), jnp.float32, math.log(0.25), math.log(1.0))), 0.25, 1.0)
    norm_gains = jnp.clip(1.0 + 0.1 * jax.random.normal(arg_keys[4], (LAYERS, 2, D), jnp.float32), 0.5, 1.5)
    query_weight = draw_query_weight(jax.random.fold_in(arg_keys[13], 71), 0)
    key_weight = draw_key_weight(jax.random.fold_in(arg_keys[13], 71), 0)
    value_weight = noise(arg_keys[7], (TASKS, LAYERS, D, KV_HEADS * HEAD_DIM), D ** -0.5, 0.09375, ((0, 4), (1, 4), (3, 16)))
    output_weight = noise(arg_keys[8], (TASKS, LAYERS, HEADS * HEAD_DIM, D), (HEADS * HEAD_DIM) ** -0.5, 0.09375, ((0, 4), (1, 4), (2, 16)))
    query_fisher = jnp.clip(jnp.exp(math.log(10.0) - 6.912895 * jax.random.uniform(arg_keys[9], (TASKS, LAYERS, D, HEADS * HEAD_DIM), jnp.float32) ** levels(arg_keys[9], (TASKS, LAYERS, D, HEADS * HEAD_DIM), ((0, 4), (1, 4), (3, 16)), -0.2, 0.2)), 0.0099487305, 10.0).astype(jnp.bfloat16)
    key_fisher = jnp.clip(jnp.exp(math.log(10.0) - 6.912895 * jax.random.uniform(arg_keys[10], (TASKS, LAYERS, D, KV_HEADS * HEAD_DIM), jnp.float32) ** levels(arg_keys[10], (TASKS, LAYERS, D, KV_HEADS * HEAD_DIM), ((0, 4), (1, 4), (3, 16)), -0.2, 0.2)), 0.0099487305, 10.0).astype(jnp.bfloat16)
    value_fisher = jnp.clip(jnp.exp(math.log(10.0) - 6.912895 * jax.random.uniform(arg_keys[11], (TASKS, LAYERS, D, KV_HEADS * HEAD_DIM), jnp.float32) ** levels(arg_keys[11], (TASKS, LAYERS, D, KV_HEADS * HEAD_DIM), ((0, 4), (1, 4), (3, 16)), -0.2, 0.2)), 0.0099487305, 10.0).astype(jnp.bfloat16)
    output_fisher = jnp.clip(jnp.exp(math.log(10.0) - 6.912895 * jax.random.uniform(arg_keys[12], (TASKS, LAYERS, HEADS * HEAD_DIM, D), jnp.float32) ** levels(arg_keys[12], (TASKS, LAYERS, HEADS * HEAD_DIM, D), ((0, 4), (1, 4), (2, 16)), -0.2, 0.2)), 0.0099487305, 10.0).astype(jnp.bfloat16)
    return {"hidden_in": hidden_in, "lengths": lengths, "layer_targets": layer_targets, "task_weights": task_weights, "norm_gains": norm_gains, "query_weight": query_weight, "key_weight": key_weight, "value_weight": value_weight, "output_weight": output_weight, "query_fisher": query_fisher, "key_fisher": key_fisher, "value_fisher": value_fisher, "output_fisher": output_fisher}


def rounded(values):
    return lax.optimization_barrier(values.astype(jnp.bfloat16)).astype(jnp.float32)

def merge_one(weight, fisher, task_scale):
    scaled = fisher.astype(jnp.float32) * task_scale[:, None, None, None]
    numerator = lax.optimization_barrier(jnp.sum(rounded(scaled * weight.astype(jnp.float32)), axis=0))
    denominator = lax.optimization_barrier(jnp.sum(rounded(scaled), axis=0))
    return (numerator / denominator).astype(jnp.bfloat16)

def normalize(values, gain_row):
    widened = values.astype(jnp.float32)
    return widened * lax.rsqrt(lax.optimization_barrier(jnp.mean(widened * widened, axis=-1, keepdims=True)) + 1e-06) * gain_row

def rotate(values):
    half_width = values.shape[-1] // 2
    frequency = 10000.0 ** (-2.0 * jnp.arange(half_width, dtype=jnp.float32) / values.shape[-1])
    angles = jnp.arange(values.shape[0], dtype=jnp.float32)[:, None] * frequency[None, :]
    cosine = jnp.cos(angles)[:, None, :]
    sine_wave = jnp.sin(angles)[:, None, :]
    first_half = values[..., :half_width]
    second_half = values[..., half_width:]
    return jnp.concatenate([first_half * cosine - second_half * sine_wave, second_half * cosine + first_half * sine_wave], axis=-1)

def sequence_layer(states, length, target, gain_pair, merged_query, merged_key, merged_value, merged_output):
    seq_len = states.shape[0]
    normed = normalize(states, gain_pair[0]).astype(jnp.bfloat16)
    queries = rotate(jnp.dot(normed, merged_query, preferred_element_type=jnp.float32).reshape(seq_len, HEADS, HEAD_DIM)).astype(jnp.bfloat16)
    key_raw = jnp.dot(normed, merged_key, preferred_element_type=jnp.float32).astype(jnp.bfloat16)
    key_rows = rotate(key_raw.astype(jnp.float32).reshape(seq_len, KV_HEADS, HEAD_DIM)).astype(jnp.bfloat16)
    value_rows = jnp.dot(normed, merged_value, preferred_element_type=jnp.float32).astype(jnp.bfloat16).reshape(seq_len, KV_HEADS, HEAD_DIM)
    group_size = HEADS // KV_HEADS
    key_rows = jnp.repeat(key_rows, group_size, axis=1)
    value_rows = jnp.repeat(value_rows, group_size, axis=1)
    scores = jnp.einsum('qhd,khd->hqk', queries.astype(jnp.float32), key_rows.astype(jnp.float32)) * HEAD_DIM ** (-0.5)
    capped = 50.0 * jnp.tanh(scores / 50.0)
    positions = jnp.arange(seq_len, dtype=jnp.int32)
    allowed = (positions[None, :] <= positions[:, None]) & (positions[None, :] < length)
    numerators = jnp.where(allowed[None], jnp.exp(capped), 0.0)
    probs = (numerators / lax.optimization_barrier(jnp.sum(numerators, axis=-1, keepdims=True))).astype(jnp.bfloat16)
    context = jnp.einsum('hqk,khd->qhd', probs.astype(jnp.float32), value_rows.astype(jnp.float32)).astype(jnp.bfloat16)
    shard_cols = HEADS * HEAD_DIM // N_MP
    context = context.reshape(seq_len, N_MP, shard_cols).astype(jnp.float32)
    partial_out = jnp.einsum('lgc,gcd->gld', context, merged_output.reshape(N_MP, shard_cols, D).astype(jnp.float32))
    attention_out = lax.optimization_barrier(jnp.sum(rounded(partial_out), axis=0))
    layer_out = (states.astype(jnp.float32) + normalize(attention_out, gain_pair[1])).astype(jnp.bfloat16)
    mismatch = layer_out.astype(jnp.float32) - target.astype(jnp.float32)
    live_rows = positions < length
    total = jnp.sum(jnp.where(live_rows[:, None], mismatch * mismatch, 0.0))
    return (layer_out, total / (length.astype(jnp.float32) * D))

def reference(hidden_in, lengths, layer_targets, task_weights, norm_gains, query_weight, key_weight, value_weight, output_weight, query_fisher, key_fisher, value_fisher, output_fisher):
    merged_query = merge_one(query_weight, query_fisher, task_weights)
    merged_key = merge_one(key_weight, key_fisher, task_weights)
    merged_value = merge_one(value_weight, value_fisher, task_weights)
    merged_output = merge_one(output_weight, output_fisher, task_weights)
    states = hidden_in
    outputs = []
    loss_list = []
    for layer_index in range(LAYERS):

        def apply_layer(items, layer_index=layer_index):
            return sequence_layer(items[0], items[1], items[2], norm_gains[layer_index], merged_query[layer_index], merged_key[layer_index], merged_value[layer_index], merged_output[layer_index])
        states, layer_loss = lax.map(apply_layer, (states, lengths, layer_targets[layer_index]))
        outputs.append(states)
        loss_list.append(layer_loss)
    return (jnp.stack(outputs), jnp.stack(loss_list))
```

```python
import functools

import jax
import jax.numpy as jnp
from jax import lax
from jax.experimental import pallas as pl
from jax.experimental.pallas import tpu as pltpu
from jax.sharding import PartitionSpec as P

HEAD_DIM = 256
F32 = jnp.float32
BF16 = jnp.bfloat16
VMEM_BYTES = 56 * 1024 * 1024


def exchanged(array, axis, mask):
    return lax.ppermute(array, axis, [(i, i ^ mask) for i in range(lax.axis_size(axis))])


def params():
    return pltpu.CompilerParams(vmem_limit_bytes=VMEM_BYTES)


def share_call(idx, scale, weights, fishers, lane_block, blocks, count, received, finish):
    rows = weights[0].shape[1]
    sub = 224 if rows % 224 == 0 else rows
    widths = [w.shape[2] if lane_block is None else w.shape[2] // 2 for w in weights]
    lane = 0 if lane_block is None else lane_block
    total = sum(widths)
    n = len(weights)

    def own_map(j, r, s):
        return (s[blocks + j], r, lane)

    in_specs = [pl.BlockSpec(memory_space=pltpu.SMEM)]
    in_specs += [pl.BlockSpec((1, sub, w), own_map) for w in widths] * 2
    operands = [scale, *weights, *fishers]
    for array, entry in received:
        if entry is None:
            in_specs.append(pl.BlockSpec((2, 1, sub, total), lambda j, r, s: (0, 0, r, 0)))
        else:
            in_specs.append(
                pl.BlockSpec((2, 1, sub, total), lambda j, r, s, e=entry: (0, s[e], r, 0))
            )
        operands.append(array)

    def kernel(idx_ref, scale_ref, *refs):
        out_ref = refs[-1]
        task_scale = scale_ref[0]
        at = 0
        for k in range(n):
            scaled = refs[n + k][0].astype(F32) * task_scale
            term = scaled * refs[k][0].astype(F32)
            part = [term.astype(BF16), scaled.astype(BF16)]
            cols = slice(at, at + widths[k])
            at += widths[k]
            if received:
                part = [
                    p.astype(F32) + sum(g[i, 0, :, cols].astype(F32) for g in refs[2 * n : -1])
                    for i, p in enumerate(part)
                ]
            if finish:
                out_ref[:, cols] = (part[0] / part[1]).astype(BF16)
            else:
                out_ref[0, 0, :, cols] = part[0].astype(BF16)
                out_ref[1, 0, :, cols] = part[1].astype(BF16)

    if finish:
        out_shape = jax.ShapeDtypeStruct((rows, total), BF16)
        out_spec = pl.BlockSpec((sub, total), lambda j, r, s: (r, 0))
    else:
        out_shape = jax.ShapeDtypeStruct((2, count, rows, total), BF16)
        out_spec = pl.BlockSpec((2, 1, sub, total), lambda j, r, s: (0, j, r, 0))
    return pl.pallas_call(
        kernel,
        out_shape=out_shape,
        grid_spec=pltpu.PrefetchScalarGridSpec(
            num_scalar_prefetch=1,
            grid=(count, rows // sub),
            in_specs=in_specs,
            out_specs=out_spec,
        ),
        compiler_params=params(),
    )(idx, *operands)


def normed_copies(states, gain, copies):
    rows, width = states.shape

    def kernel(states_ref, gain_ref, out_ref):
        x = states_ref[...].astype(F32)
        scale = lax.rsqrt(jnp.mean(x * x, axis=-1, keepdims=True) + 1e-06)
        y = (x * scale * gain_ref[...]).astype(BF16)
        for k in range(copies):
            out_ref[k] = y

    return pl.pallas_call(
        kernel,
        out_shape=jax.ShapeDtypeStruct((copies, rows, width), BF16),
        compiler_params=params(),
    )(states, gain)


def project(idx, normed, own, peer, cosine, sine):
    copies, rows, width = normed.shape
    tokens = copies * rows
    quarter = width // 4
    half = own[2].shape[0]
    pieces = len(own)

    def kernel(idx_ref, x_ref, cos_ref, sin_ref, *refs):
        q_own_ref, q_peer_ref, kv_ref = refs[-3:]
        x_index = idx_ref[0]
        core = idx_ref[1]

        def one(ws):
            acc = None
            for d, lo, w in ws:
                at = pl.multiple_of((x_index ^ d) * quarter + lo, 128)
                part = x_ref[:, :, pl.ds(at, w.shape[0])].reshape(tokens, w.shape[0])
                prod = jnp.dot(part, w[...], preferred_element_type=F32)
                acc = prod if acc is None else acc + prod
            return acc

        def listed(ws):
            p0, p1, p2a, p2b, p3 = ws
            return [(0, 0, p0), (1, 0, p1), (2, 0, p2a), (2, half, p2b), (3, 0, p3)]

        mine = one(listed(refs[:pieces]))
        theirs = one(listed(refs[pieces : 2 * pieces]))
        cos = cos_ref[...]
        sin = sin_ref[...]

        def rotated(q):
            a = q[:, :128]
            b = q[:, 128:]
            return (a * cos - b * sin).astype(BF16), (b * cos + a * sin).astype(BF16)

        for ref, acc in ((q_own_ref, mine), (q_peer_ref, theirs)):
            lo, hi = rotated(acc[:, :256])
            ref[:, :128] = lo
            ref[:, 128:] = hi
        first = core == 0
        k_mine = mine[:, 256:384].astype(BF16).astype(F32)
        k_theirs = theirs[:, 256:384].astype(BF16).astype(F32)
        a = jnp.where(first, k_mine, k_theirs)
        b = jnp.where(first, k_theirs, k_mine)
        kv_ref[:, :128] = (a * cos - b * sin).astype(BF16)
        kv_ref[:, 128:256] = (b * cos + a * sin).astype(BF16)
        kv_ref[:, 256:384] = jnp.where(first, mine[:, 384:], theirs[:, 384:]).astype(BF16)
        kv_ref[:, 384:] = jnp.where(first, theirs[:, 384:], mine[:, 384:]).astype(BF16)

    vmem = pl.BlockSpec(memory_space=pltpu.VMEM)
    return pl.pallas_call(
        kernel,
        out_shape=(
            jax.ShapeDtypeStruct((tokens, 256), BF16),
            jax.ShapeDtypeStruct((tokens, 256), BF16),
            jax.ShapeDtypeStruct((tokens, 512), BF16),
        ),
        in_specs=[pl.BlockSpec(memory_space=pltpu.SMEM)] + [vmem] * (3 + 2 * pieces),
        out_specs=(vmem, vmem, vmem),
        compiler_params=params(),
    )(idx, normed, cosine, sine, *own, *peer)


def attend(idx, q_own, q_peer, kv_own, kv_peer, out_own, out_peer, copies):
    tokens = q_own.shape[0]
    rows = tokens // copies
    width = out_own.shape[1]

    def kernel(idx_ref, qo_ref, qp_ref, ko_ref, kp_ref, wo_ref, wp_ref, out_ref):
        core = idx_ref[1]
        length = idx_ref[2]

        def positions(shape, dim, which):
            i = lax.broadcasted_iota(jnp.int32, shape, dim)
            return (i // rows) * (2 * rows) + which * rows + i % rows

        shape = (tokens, tokens)
        q_pos = positions(shape, 0, core)
        masks = []
        for which in (core, 1 - core):
            k_pos = positions(shape, 1, which)
            masks.append((k_pos <= q_pos) & (k_pos < length))
        contexts = []
        for q_ref in (qo_ref, qp_ref):
            q = q_ref[...]
            numerators = []
            for kv_ref, allowed in ((ko_ref, masks[0]), (kp_ref, masks[1])):
                scores = lax.dot_general(
                    q,
                    kv_ref[:, :256],
                    (((1,), (1,)), ((), ())),
                    preferred_element_type=F32,
                ) * HEAD_DIM ** (-0.5)
                capped = 50.0 * jnp.tanh(scores / 50.0)
                numerators.append(jnp.where(allowed, jnp.exp(capped), 0.0))
            total = jnp.sum(numerators[0], axis=-1, keepdims=True) + jnp.sum(
                numerators[1], axis=-1, keepdims=True
            )
            ctx = None
            for num, kv_ref in zip(numerators, (ko_ref, kp_ref)):
                prod = jnp.dot(
                    (num / total).astype(BF16), kv_ref[:, 256:], preferred_element_type=F32
                )
                ctx = prod if ctx is None else ctx + prod
            contexts.append(ctx.astype(BF16))
        out = jnp.dot(contexts[0], wo_ref[...], preferred_element_type=F32) + jnp.dot(
            contexts[1], wp_ref[...], preferred_element_type=F32
        )
        out_ref[...] = out.astype(BF16).reshape(copies, rows, width)

    vmem = pl.BlockSpec(memory_space=pltpu.VMEM)
    return pl.pallas_call(
        kernel,
        out_shape=jax.ShapeDtypeStruct((copies, rows, width), BF16),
        in_specs=[pl.BlockSpec(memory_space=pltpu.SMEM)] + [vmem] * 6,
        out_specs=vmem,
        compiler_params=params(),
    )(idx, q_own, q_peer, kv_own, kv_peer, out_own, out_peer)


def assembled(idx, pieces):
    p0, p1, p2a, p2b, p3 = pieces
    rows, width = p0.shape
    half = p2a.shape[1]

    def kernel(idx_ref, r0, r1, r2a, r2b, r3, out_ref):
        x_index = idx_ref[0]
        out_ref[x_index] = r0[...]
        out_ref[x_index ^ 1] = r1[...]
        out_ref[x_index ^ 2, :, :half] = r2a[...]
        out_ref[x_index ^ 2, :, half:] = r2b[...]
        out_ref[x_index ^ 3] = r3[...]

    vmem = pl.BlockSpec(memory_space=pltpu.VMEM)
    return pl.pallas_call(
        kernel,
        out_shape=jax.ShapeDtypeStruct((4, rows, width), BF16),
        in_specs=[pl.BlockSpec(memory_space=pltpu.SMEM)] + [vmem] * 5,
        out_specs=vmem,
        compiler_params=params(),
    )(idx, p0, p1, p2a, p2b, p3).reshape(4 * rows, width)


def finished(pieces, states, gain):
    rows, width = states.shape

    def kernel(p_ref, states_ref, gain_ref, out_ref):
        total = jnp.sum(p_ref[...].astype(F32), axis=0)
        scale = lax.rsqrt(jnp.mean(total * total, axis=-1, keepdims=True) + 1e-06)
        out = states_ref[...].astype(F32) + total * scale * gain_ref[...]
        out_ref[...] = out.astype(BF16)

    return pl.pallas_call(
        kernel,
        out_shape=jax.ShapeDtypeStruct((rows, width), BF16),
        compiler_params=params(),
    )(pieces, states, gain)


def reduced_shares(plan, scale, sets):
    near, far = 1, 3
    halves = []
    for which, (weights, fishers, lane) in enumerate(sets):
        first, second = (near, far) if which == 0 else (far, near)
        base = 8 * which
        call = functools.partial(share_call, plan, scale, weights, fishers, lane)
        halves.append((call, base, first, second))
    got = [exchanged(call(base, 2, (), False), "task", first) for call, base, first, _ in halves]
    more = [
        exchanged(call(base + 2, 1, ((g, base + 3),), False), "task", second)
        for (call, base, _, second), g in zip(halves, got)
    ]
    return [
        call(base + 4, 1, ((g, base + 5), (m, None)), True)
        for (call, base, _, _), g, m in zip(halves, got, more)
    ]


def gathered_pieces(own, axis):
    dim, length = axis
    half = (length // 2 + 127) // 128 * 128
    from_near = exchanged(own, "task", 1)
    from_far = exchanged(own, "task", 3)
    low = lax.slice_in_dim(from_far, 0, half, axis=dim)
    high = lax.slice_in_dim(from_near, half, length, axis=dim)
    return (
        own,
        from_near,
        exchanged(low, "task", 1),
        exchanged(high, "task", 3),
        from_far,
    )


def per_device(
    hidden_in,
    lengths,
    layer_targets,
    task_weights,
    norm_gains,
    query_weight,
    key_weight,
    value_weight,
    output_weight,
    query_fisher,
    key_fisher,
    value_fisher,
    output_fisher,
):
    x_index = lax.axis_index("task")
    mp_index = lax.axis_index("mp")
    section_index = lax.axis_index("section")
    core = mp_index % 2
    chips = lax.axis_size("mp") // 2
    groups = [[2 * z + c for z in range(chips)] for c in range(2)]
    sections = lax.axis_size("section")
    states = hidden_in[0]
    rows, width = states.shape
    length = lengths[0]
    pre_gain = norm_gains[0, 0:1]
    post_gain = norm_gains[0, 1:2]
    scale = lax.dynamic_slice_in_dim(task_weights, x_index, 1)

    b = x_index // 2
    a = (x_index % 2) ^ b

    def block_a(h1, h2):
        return jnp.where(h1 == 0, 3 * h2, 1 + h2)

    def block_b(h1, h2):
        return jnp.where(h1 == 0, h2, 3 - h2)

    zero = jnp.zeros_like(a)
    plan = jnp.stack(
        [
            block_a(1 - a, 0),
            block_a(1 - a, 1),
            block_a(a, 1 - b),
            1 - b,
            x_index,
            b,
            zero,
            zero,
            block_b(1 - b, 0),
            block_b(1 - b, 1),
            block_b(b, 1 - a),
            1 - a,
            x_index,
            a,
            zero,
            zero,
        ]
    ).astype(jnp.int32)
    scalars = jnp.stack([x_index, core, length]).astype(jnp.int32)

    def quarters(array):
        array = array[0, 0]
        return array.reshape(4, array.shape[0] // 4, array.shape[1])

    qkv_sets = (
        ((quarters(query_weight),), (quarters(query_fisher),), None),
        (
            (quarters(key_weight), quarters(value_weight)),
            (quarters(key_fisher), quarters(value_fisher)),
            None,
        ),
    )
    out_sets = tuple(
        ((quarters(output_weight),), (quarters(output_fisher),), lane) for lane in (0, 1)
    )

    positions = (
        2 * rows * jnp.arange(chips, dtype=jnp.int32)[:, None]
        + core * rows
        + jnp.arange(rows, dtype=jnp.int32)[None, :]
    ).reshape(-1)
    frequency = 10000.0 ** (-2.0 * jnp.arange(HEAD_DIM // 2, dtype=F32) / HEAD_DIM)
    angles = positions.astype(F32)[:, None] * frequency[None, :]
    cosine = jnp.cos(angles)
    sine = jnp.sin(angles)

    def spread(array):
        return lax.all_to_all(array, "mp", 0, 0, tiled=True, axis_index_groups=groups)

    with jax.named_scope("merge_qkv"):
        q_share, kv_share = reduced_shares(plan, scale, qkv_sets)
        share = jnp.concatenate([q_share, kv_share], axis=1)
        qkv_own = gathered_pieces(share, (0, share.shape[0]))
        qkv_peer = tuple(exchanged(p, "mp", 1) for p in qkv_own)
    with jax.named_scope("merge_out"):
        low_share, high_share = reduced_shares(plan, scale, out_sets)
        share = jnp.concatenate([low_share, high_share], axis=1)
        out_own = assembled(scalars, gathered_pieces(share, (1, share.shape[1])))
        out_peer = exchanged(out_own, "mp", 1)

    chosen = None
    for step in range(sections):
        with jax.named_scope("layer"):
            if step > 0:
                states = lax.ppermute(
                    layer_out, "section", [(i, i + 1) for i in range(sections - 1)]
                )
            normed = spread(normed_copies(states, pre_gain, chips))
            q_own, q_peer, kv_own = project(scalars, normed, qkv_own, qkv_peer, cosine, sine)
            kv_peer = exchanged(kv_own, "mp", 1)
            partial = attend(scalars, q_own, q_peer, kv_own, kv_peer, out_own, out_peer, chips)
            layer_out = finished(spread(partial), states, post_gain)
            chosen = (
                layer_out
                if chosen is None
                else jnp.where(section_index == step, layer_out, chosen)
            )
    with jax.named_scope("loss"):
        own_positions = mp_index * rows + jnp.arange(rows, dtype=jnp.int32)
        mismatch = chosen.astype(F32) - layer_targets[0, 0].astype(F32)
        loss_part = jnp.sum(jnp.where((own_positions < length)[:, None], mismatch * mismatch, 0.0))
        copies = jnp.broadcast_to(loss_part, (2 * chips, 1))
        total = jnp.sum(lax.all_to_all(copies, "mp", 0, 0, tiled=True))
        loss = total / (length.astype(F32) * width)
    return (chosen[None, None], loss[None, None])


def solution(mesh):
    in_specs = (
        P("task", "mp", None),
        P("task"),
        P("section", "task", "mp", None),
        P(),
        P("section", None, None),
        P("task", "section", None, "mp"),
        P("task", "section", None, "mp"),
        P("task", "section", None, "mp"),
        P("task", "section", "mp", None),
        P("task", "section", None, "mp"),
        P("task", "section", None, "mp"),
        P("task", "section", None, "mp"),
        P("task", "section", "mp", None),
    )
    out_specs = (P("section", "task", "mp", None), P("section", "task"))
    return jax.shard_map(
        per_device, mesh=mesh, in_specs=in_specs, out_specs=out_specs, check_vma=False
    )
```

```python
import functools

import jax
import jax.numpy as jnp
from jax import lax
from jax.experimental import pallas as pl
from jax.experimental.pallas import tpu as pltpu
from jax.sharding import PartitionSpec as P

HEAD_DIM = 256
F32 = jnp.float32
BF16 = jnp.bfloat16
SMEM = pltpu.SMEM
VMEM = pltpu.VMEM
HBM = pltpu.HBM


def exchanged(array, axis, mask):
    return lax.ppermute(array, axis, [(i, i ^ mask) for i in range(lax.axis_size(axis))])


def placed(array, space):
    return pltpu.with_memory_space_constraint(array, space)


def result_on_chip(shape, dtype=BF16):
    return VMEM(shape, dtype)


def kernel_call(kernel, operands, spaces, shapes, scratch=(), mib=16):
    operands = [a if space == SMEM else placed(a, space) for a, space in zip(operands, spaces)]
    outs = pl.pallas_call(
        kernel,
        out_shape=tuple(result_on_chip(shape) for shape in shapes),
        in_specs=[pl.BlockSpec(memory_space=space) for space in spaces],
        out_specs=tuple(pl.BlockSpec(memory_space=VMEM) for _ in shapes),
        scratch_shapes=scratch,
        compiler_params=pltpu.CompilerParams(vmem_limit_bytes=mib * 1024 * 1024),
    )(*operands)
    return outs[0] if len(shapes) == 1 else outs


def share_call(plan, scale, source, base, count, received, finish):
    weights, fishers, rows, widths, cut = source
    n = len(weights)
    sub = rows // 2
    parts = count * 2
    strip = 64 if sub % 64 == 0 and sub > 64 else 16
    total = sum(widths)
    entries = [entry for _, entry in received]

    def kernel(plan_ref, scale_ref, *refs):
        arrays = refs[: 2 * n]
        gots = refs[2 * n : 2 * n + len(entries)]
        out_ref = refs[2 * n + len(entries)]
        buffers = refs[2 * n + len(entries) + 1 : -1]
        sems = refs[-1]

        def copy(k, part):
            return pltpu.make_async_copy(
                cut(arrays[k], plan_ref[base + part // 2], (part % 2) * sub, sub),
                buffers[k].at[part],
                sems.at[k, part],
            )

        for part in range(parts):
            for k in range(2 * n):
                copy(k, part).start()
        task_scale = scale_ref[0]
        got_blocks = [0 if entry is None else plan_ref[entry] for entry in entries]

        def strip_of(part, i):
            inside = pl.ds(pl.multiple_of(i * strip, strip), strip)
            lines = pl.ds(pl.multiple_of((part % 2) * sub + i * strip, strip), strip)
            at = 0
            for k in range(n):
                scaled = buffers[n + k][part, inside, :].astype(F32) * task_scale
                term = scaled * buffers[k][part, inside, :].astype(F32)
                sums = [term.astype(BF16), scaled.astype(BF16)]
                cols = slice(at, at + widths[k])
                at += widths[k]
                for got, block in zip(gots, got_blocks):
                    sums = [
                        v.astype(F32) + got[i, block, lines, cols].astype(F32)
                        for i, v in enumerate(sums)
                    ]
                if finish:
                    out_ref[lines, cols] = (sums[0] / sums[1]).astype(BF16)
                else:
                    out_ref[0, part // 2, lines, cols] = sums[0].astype(BF16)
                    out_ref[1, part // 2, lines, cols] = sums[1].astype(BF16)

        def one_part(part, carry):
            for k in range(2 * n):
                copy(k, part).wait()
            lax.fori_loop(0, sub // strip, lambda i, c: (strip_of(part, i), c)[1], 0)
            return carry

        lax.fori_loop(0, parts, one_part, 0)

    scratch = [VMEM((parts, sub, widths[k % n]), BF16) for k in range(2 * n)]
    scratch.append(pltpu.SemaphoreType.DMA((2 * n, parts)))
    return kernel_call(
        kernel,
        [plan, scale, *weights, *fishers, *(array for array, _ in received)],
        [SMEM, SMEM] + [HBM] * (2 * n) + [VMEM] * len(entries),
        [(rows, total) if finish else (2, count, rows, total)],
        scratch,
    )


def normed_copies(states, gain, copies):
    rows, width = states.shape

    def kernel(states_ref, gain_ref, out_ref):
        x = states_ref[...].astype(F32)
        scale = lax.rsqrt(jnp.mean(x * x, axis=-1, keepdims=True) + 1e-06)
        y = (x * scale * gain_ref[...]).astype(BF16)
        for k in range(copies):
            out_ref[k] = y

    return kernel_call(kernel, [states, gain], [VMEM] * 2, [(copies, rows, width)])


def project(idx, normed, own, peer, cosine, sine):
    copies, rows, width = normed.shape
    tokens = copies * rows
    quarter = width // 4

    def kernel(idx_ref, x_ref, cos_ref, sin_ref, *refs):
        q_own_ref, q_peer_ref, kv_ref = refs[-3:]
        x_index = idx_ref[0]
        core = idx_ref[1]
        sums = [None] * 4
        for d in range(4):
            at = pl.multiple_of((x_index ^ d) * quarter, 128)
            part = x_ref[:, :, pl.ds(at, quarter)].reshape(tokens, quarter)
            for k in range(4):
                prod = jnp.dot(part, refs[4 * k + d][...], preferred_element_type=F32)
                sums[k] = prod if d == 0 else sums[k] + prod
        q_mine, mine, q_theirs, theirs = sums
        cos = cos_ref[...]
        sin = sin_ref[...]
        for ref, q in ((q_own_ref, q_mine), (q_peer_ref, q_theirs)):
            a = q[:, :128]
            b = q[:, 128:]
            ref[:, :128] = (a * cos - b * sin).astype(BF16)
            ref[:, 128:] = (b * cos + a * sin).astype(BF16)
        first = core == 0
        k_mine = mine[:, :128].astype(BF16).astype(F32)
        k_theirs = theirs[:, :128].astype(BF16).astype(F32)
        a = jnp.where(first, k_mine, k_theirs)
        b = jnp.where(first, k_theirs, k_mine)
        kv_ref[:, :128] = (a * cos - b * sin).astype(BF16)
        kv_ref[:, 128:256] = (b * cos + a * sin).astype(BF16)
        kv_ref[:, 256:384] = jnp.where(first, mine[:, 128:], theirs[:, 128:]).astype(BF16)
        kv_ref[:, 384:] = jnp.where(first, theirs[:, 128:], mine[:, 128:]).astype(BF16)

    return kernel_call(
        kernel,
        [idx, normed, cosine, sine, *own[0], *own[1], *peer[0], *peer[1]],
        [SMEM] + [VMEM] * 19,
        [(tokens, 256), (tokens, 256), (tokens, 512)],
    )


def attend(idx, q_own, q_peer, kv_own, kv_peer, own, peer, copies):
    tokens = q_own.shape[0]
    rows = tokens // copies
    quarter = own[0][0].shape[1]

    def kernel(idx_ref, qo_ref, qp_ref, ko_ref, kp_ref, *refs):
        out_ref = refs[-1]
        x_index = idx_ref[0]
        core = idx_ref[1]
        length = idx_ref[2]

        def positions(shape, dim, which):
            i = lax.broadcasted_iota(jnp.int32, shape, dim)
            return (i // rows) * (2 * rows) + which * rows + i % rows

        shape = (tokens, tokens)
        q_pos = positions(shape, 0, core)
        masks = []
        for which in (core, 1 - core):
            k_pos = positions(shape, 1, which)
            masks.append((k_pos <= q_pos) & (k_pos < length))
        contexts = []
        for q_ref in (qo_ref, qp_ref):
            q = q_ref[...]
            numerators = []
            for kv_ref, allowed in ((ko_ref, masks[0]), (kp_ref, masks[1])):
                scores = lax.dot_general(
                    q,
                    kv_ref[:, :256],
                    (((1,), (1,)), ((), ())),
                    preferred_element_type=F32,
                ) * HEAD_DIM ** (-0.5)
                capped = 50.0 * jnp.tanh(scores / 50.0)
                numerators.append(jnp.where(allowed, jnp.exp(capped), 0.0))
            total = jnp.sum(numerators[0], axis=-1, keepdims=True) + jnp.sum(
                numerators[1], axis=-1, keepdims=True
            )
            ctx = None
            for num, kv_ref in zip(numerators, (ko_ref, kp_ref)):
                prod = jnp.dot(
                    (num / total).astype(BF16), kv_ref[:, 256:], preferred_element_type=F32
                )
                ctx = prod if ctx is None else ctx + prod
            contexts.append(ctx.astype(BF16))
        lefts = [c[:, h * 128 : (h + 1) * 128] for c in contexts for h in range(2)]
        for d in range(4):
            out = None
            for k in range(4):
                prod = jnp.dot(lefts[k], refs[4 * k + d][...], preferred_element_type=F32)
                out = prod if out is None else out + prod
            at = pl.multiple_of((x_index ^ d) * quarter, 128)
            out_ref[:, :, pl.ds(at, quarter)] = out.astype(BF16).reshape(copies, rows, quarter)

    return kernel_call(
        kernel,
        [idx, q_own, q_peer, kv_own, kv_peer, *own[0], *own[1], *peer[0], *peer[1]],
        [SMEM] + [VMEM] * 20,
        [(copies, rows, 4 * quarter)],
    )


def finished(pieces, states, gain):
    def kernel(p_ref, states_ref, gain_ref, out_ref):
        total = jnp.sum(p_ref[...].astype(F32), axis=0)
        scale = lax.rsqrt(jnp.mean(total * total, axis=-1, keepdims=True) + 1e-06)
        out = states_ref[...].astype(F32) + total * scale * gain_ref[...]
        out_ref[...] = out.astype(BF16)

    return kernel_call(kernel, [pieces, states, gain], [VMEM] * 3, [states.shape])


NEAR, FAR = 1, 3


def first_halves(plan, scale, sources):
    sent = [share_call(plan, scale, s, 8 * i, 2, (), False) for i, s in enumerate(sources)]
    return [exchanged(s, "task", (NEAR, FAR)[i]) for i, s in enumerate(sent)]


def second_halves(plan, scale, sources, got):
    sent = [
        share_call(plan, scale, s, 8 * i + 2, 1, ((got[i], 8 * i + 3),), False)
        for i, s in enumerate(sources)
    ]
    return sent, [exchanged(s, "task", (FAR, NEAR)[i]) for i, s in enumerate(sent)]


def shares(plan, scale, sources, got, more):
    return [
        share_call(plan, scale, s, 8 * i + 4, 1, ((got[i], 8 * i + 5), (more[i], None)), True)
        for i, s in enumerate(sources)
    ]


def neighbours(own):
    near = [exchanged(o, "task", NEAR) for o in own]
    far = [exchanged(o, "task", FAR) for o in own]
    return near, far


def completed(own, near, far):
    opposite = [exchanged(far[0], "task", NEAR), exchanged(near[1], "task", FAR)]
    return [(own[i], near[i], opposite[i], far[i]) for i in range(2)]


def gathered(own):
    return completed(own, *neighbours(own))


def of_partner(pieces):
    return [tuple(exchanged(p, "mp", 1) for p in group) for group in pieces]


def per_device(
    hidden_in,
    lengths,
    layer_targets,
    task_weights,
    norm_gains,
    query_weight,
    key_weight,
    value_weight,
    output_weight,
    query_fisher,
    key_fisher,
    value_fisher,
    output_fisher,
):
    x_index = lax.axis_index("task")
    mp_index = lax.axis_index("mp")
    section_index = lax.axis_index("section")
    core = mp_index % 2
    chips = lax.axis_size("mp") // 2
    groups = [[2 * z + c for z in range(chips)] for c in range(2)]
    sections = lax.axis_size("section")
    states = hidden_in[0]
    rows, width = states.shape
    length = lengths[0]
    pre_gain = norm_gains[0, 0:1]
    post_gain = norm_gains[0, 1:2]
    scale = lax.dynamic_slice_in_dim(task_weights, x_index, 1)

    b = x_index // 2
    a = (x_index % 2) ^ b

    def block_a(h1, h2):
        return jnp.where(h1 == 0, 3 * h2, 1 + h2)

    def block_b(h1, h2):
        return jnp.where(h1 == 0, h2, 3 - h2)

    zero = jnp.zeros_like(a)
    plan = jnp.stack(
        [
            block_a(1 - a, 0),
            block_a(1 - a, 1),
            block_a(a, 1 - b),
            1 - b,
            x_index,
            b,
            zero,
            zero,
            block_b(1 - b, 0),
            block_b(1 - b, 1),
            block_b(b, 1 - a),
            1 - a,
            x_index,
            a,
            zero,
            zero,
        ]
    ).astype(jnp.int32)
    scalars = jnp.stack([x_index, core, length]).astype(jnp.int32)

    def quarters(array):
        array = array[0, 0]
        return array.reshape(4, array.shape[0] // 4, array.shape[1])

    def cut_rows(ref, block, row, sub):
        return ref.at[block, pl.ds(row, sub), :]

    def cut_columns(start):
        def cut(ref, block, row, sub):
            at = pl.multiple_of(block * (width // 4), 128)
            return ref.at[pl.ds(start + row, sub), pl.ds(at, width // 4)]

        return cut

    qkv_sources = (
        ((quarters(query_weight),), (quarters(query_fisher),), width // 4, (256,), cut_rows),
        (
            (quarters(key_weight), quarters(value_weight)),
            (quarters(key_fisher), quarters(value_fisher)),
            width // 4,
            (128, 128),
            cut_rows,
        ),
    )
    out_sources = tuple(
        (
            (output_weight[0, 0],),
            (output_fisher[0, 0],),
            128,
            (width // 4,),
            cut_columns(start),
        )
        for start in (0, 128)
    )

    positions = (
        2 * rows * jnp.arange(chips, dtype=jnp.int32)[:, None]
        + core * rows
        + jnp.arange(rows, dtype=jnp.int32)[None, :]
    ).reshape(-1)
    frequency = 10000.0 ** (-2.0 * jnp.arange(HEAD_DIM // 2, dtype=F32) / HEAD_DIM)
    angles = positions.astype(F32)[:, None] * frequency[None, :]
    cosine = jnp.cos(angles)
    sine = jnp.sin(angles)

    def spread(array):
        return lax.all_to_all(array, "mp", 0, 0, tiled=True, axis_index_groups=groups)

    def projected(normed):
        q_own, q_peer, kv_own = project(scalars, normed, qkv_own, qkv_peer, cosine, sine)
        return q_own, q_peer, kv_own, exchanged(kv_own, "mp", 1)

    with jax.named_scope("merge"):
        qkv_got = first_halves(plan, scale, qkv_sources)
        first_normed = spread(normed_copies(states, pre_gain, chips))
        out_got = first_halves(plan, scale, out_sources)
        qkv_got, first_normed, cosine, sine = lax.optimization_barrier(
            (qkv_got, first_normed, cosine, sine)
        )
        qkv_sent, qkv_more = second_halves(plan, scale, qkv_sources, qkv_got)
        out_got, _ = lax.optimization_barrier((out_got, qkv_sent))
        out_sent, out_more = second_halves(plan, scale, out_sources, out_got)
        qkv_share = shares(plan, scale, qkv_sources, qkv_got, qkv_more)
        out_more, _ = lax.optimization_barrier((out_more, qkv_share))
        out_share = shares(plan, scale, out_sources, out_got, out_more)
        qkv_own = gathered(qkv_share)
        qkv_peer = of_partner(qkv_own)
        out_first = neighbours(out_share)
    with jax.named_scope("layer"):
        queries = projected(first_normed)
    with jax.named_scope("merge"):
        out_first, _ = lax.optimization_barrier((out_first, queries[0]))
        out_own = completed(out_share, *out_first)
        out_peer = of_partner(out_own)

    chosen = None
    for step in range(sections):
        with jax.named_scope("layer"):
            if step > 0:
                states = lax.ppermute(
                    layer_out, "section", [(i, i + 1) for i in range(sections - 1)]
                )
                queries = projected(spread(normed_copies(states, pre_gain, chips)))
            partial = attend(scalars, *queries, out_own, out_peer, chips)
            layer_out = finished(spread(partial), states, post_gain)
            chosen = (
                layer_out
                if chosen is None
                else jnp.where(section_index == step, layer_out, chosen)
            )
    with jax.named_scope("loss"):
        own_positions = mp_index * rows + jnp.arange(rows, dtype=jnp.int32)
        mismatch = chosen.astype(F32) - layer_targets[0, 0].astype(F32)
        loss_part = jnp.sum(jnp.where((own_positions < length)[:, None], mismatch * mismatch, 0.0))
        copies = jnp.broadcast_to(loss_part, (2 * chips, 1))
        total = jnp.sum(lax.all_to_all(copies, "mp", 0, 0, tiled=True))
        loss = total / (length.astype(F32) * width)
    return (chosen[None, None], loss[None, None])


def solution(mesh):
    in_specs = (
        P("task", "mp", None),
        P("task"),
        P("section", "task", "mp", None),
        P(),
        P("section", None, None),
        P("task", "section", None, "mp"),
        P("task", "section", None, "mp"),
        P("task", "section", None, "mp"),
        P("task", "section", "mp", None),
        P("task", "section", None, "mp"),
        P("task", "section", None, "mp"),
        P("task", "section", None, "mp"),
        P("task", "section", "mp", None),
    )
    out_specs = (P("section", "task", "mp", None), P("section", "task"))
    return jax.shard_map(
        per_device, mesh=mesh, in_specs=in_specs, out_specs=out_specs, check_vma=False
    )
```

```python
import functools

import jax
import jax.numpy as jnp
from jax import lax
from jax.experimental import pallas as pl
from jax.experimental.pallas import tpu as pltpu
from jax.sharding import PartitionSpec as P

HEAD_DIM = 256
F32 = jnp.float32
BF16 = jnp.bfloat16
SMEM = pltpu.SMEM
VMEM = pltpu.VMEM
HBM = pltpu.HBM


def exchanged(array, axis, mask):
    return lax.ppermute(array, axis, [(i, i ^ mask) for i in range(lax.axis_size(axis))])


def placed(array, space):
    return pltpu.with_memory_space_constraint(array, space)


def result_on_chip(shape, dtype=BF16):
    return VMEM(shape, dtype)


def kernel_call(kernel, operands, spaces, shapes, scratch=(), mib=16):
    operands = [a if space == SMEM else placed(a, space) for a, space in zip(operands, spaces)]
    outs = pl.pallas_call(
        kernel,
        out_shape=tuple(result_on_chip(shape) for shape in shapes),
        in_specs=[pl.BlockSpec(memory_space=space) for space in spaces],
        out_specs=tuple(pl.BlockSpec(memory_space=VMEM) for _ in shapes),
        scratch_shapes=scratch,
        compiler_params=pltpu.CompilerParams(vmem_limit_bytes=mib * 1024 * 1024),
    )(*operands)
    return outs[0] if len(shapes) == 1 else outs


def share_call(plan, scale, source, base, count, received, finish):
    weights, fishers, rows, widths, cut = source
    n = len(weights)
    sub = rows // 2
    parts = count * 2
    strip = 64 if sub % 64 == 0 and sub > 64 else 16
    total = sum(widths)
    entries = [entry for _, entry in received]

    def kernel(plan_ref, scale_ref, *refs):
        arrays = refs[: 2 * n]
        gots = refs[2 * n : 2 * n + len(entries)]
        out_ref = refs[2 * n + len(entries)]
        buffers = refs[2 * n + len(entries) + 1 : -1]
        sems = refs[-1]

        def copy(k, part):
            return pltpu.make_async_copy(
                cut(arrays[k], plan_ref[base + part // 2], (part % 2) * sub, sub),
                buffers[k].at[part],
                sems.at[k, part],
            )

        for part in range(parts):
            for k in range(2 * n):
                copy(k, part).start()
        task_scale = scale_ref[0]
        got_blocks = [0 if entry is None else plan_ref[entry] for entry in entries]

        def strip_of(part, i):
            inside = pl.ds(pl.multiple_of(i * strip, strip), strip)
            lines = pl.ds(pl.multiple_of((part % 2) * sub + i * strip, strip), strip)
            at = 0
            for k in range(n):
                scaled = buffers[n + k][part, inside, :].astype(F32) * task_scale
                term = scaled * buffers[k][part, inside, :].astype(F32)
                sums = [term.astype(BF16), scaled.astype(BF16)]
                cols = slice(at, at + widths[k])
                at += widths[k]
                for got, block in zip(gots, got_blocks):
                    sums = [
                        v.astype(F32) + got[i, block, lines, cols].astype(F32)
                        for i, v in enumerate(sums)
                    ]
                if finish:
                    out_ref[lines, cols] = (sums[0] / sums[1]).astype(BF16)
                else:
                    out_ref[0, part // 2, lines, cols] = sums[0].astype(BF16)
                    out_ref[1, part // 2, lines, cols] = sums[1].astype(BF16)

        def one_part(part, carry):
            for k in range(2 * n):
                copy(k, part).wait()
            lax.fori_loop(0, sub // strip, lambda i, c: (strip_of(part, i), c)[1], 0)
            return carry

        lax.fori_loop(0, parts, one_part, 0)

    scratch = [VMEM((parts, sub, widths[k % n]), BF16) for k in range(2 * n)]
    scratch.append(pltpu.SemaphoreType.DMA((2 * n, parts)))
    return kernel_call(
        kernel,
        [plan, scale, *weights, *fishers, *(array for array, _ in received)],
        [SMEM, SMEM] + [HBM] * (2 * n) + [VMEM] * len(entries),
        [(rows, total) if finish else (2, count, rows, total)],
        scratch,
    )


def normed_copies(states, gain, copies):
    rows, width = states.shape

    def kernel(states_ref, gain_ref, out_ref):
        x = states_ref[...].astype(F32)
        scale = lax.rsqrt(jnp.mean(x * x, axis=-1, keepdims=True) + 1e-06)
        y = (x * scale * gain_ref[...]).astype(BF16)
        for k in range(copies):
            out_ref[k * rows : (k + 1) * rows, :] = y

    return kernel_call(kernel, [states, gain], [VMEM] * 2, [(copies * rows, width)])


def project(idx, normed, own, peer, cosine, sine):
    tokens, width = normed.shape
    quarter = width // 4

    def kernel(idx_ref, x_ref, cos_ref, sin_ref, *refs):
        q_ref, kv_ref = refs[-2:]
        x_index = idx_ref[0]
        core = idx_ref[1]
        part_index = idx_ref[3]
        sums = [None] * 4
        for d in range(4):
            at = pl.multiple_of((x_index ^ d) * quarter, 128)
            part = x_ref[:, pl.ds(at, quarter)]
            for k in range(4):
                prod = jnp.dot(part, refs[4 * k + d][...], preferred_element_type=F32)
                sums[k] = prod if d == 0 else sums[k] + prod
        q_mine, mine, q_theirs, theirs = sums
        cos = cos_ref[part_index]
        sin = sin_ref[part_index]
        for at, q in ((0, q_mine), (tokens, q_theirs)):
            a = q[:, :128]
            b = q[:, 128:]
            q_ref[at : at + tokens, :128] = (a * cos - b * sin).astype(BF16)
            q_ref[at : at + tokens, 128:] = (b * cos + a * sin).astype(BF16)
        first = core == 0
        k_mine = mine[:, :128].astype(BF16).astype(F32)
        k_theirs = theirs[:, :128].astype(BF16).astype(F32)
        a = jnp.where(first, k_mine, k_theirs)
        b = jnp.where(first, k_theirs, k_mine)
        kv_ref[:, :128] = (a * cos - b * sin).astype(BF16)
        kv_ref[:, 128:256] = (b * cos + a * sin).astype(BF16)
        kv_ref[:, 256:384] = jnp.where(first, mine[:, 128:], theirs[:, 128:]).astype(BF16)
        kv_ref[:, 384:] = jnp.where(first, theirs[:, 128:], mine[:, 128:]).astype(BF16)

    return kernel_call(
        kernel,
        [idx, normed, cosine, sine, *own[0], *own[1], *peer[0], *peer[1]],
        [SMEM] + [VMEM] * 19,
        [(2 * tokens, 256), (tokens, 512)],
    )


def attend(idx, queries, blocks, own, peer, rows):
    tokens = queries.shape[0] // 2
    quarter = own[0][0].shape[1]
    part_rows = 2 * tokens

    def kernel(idx_ref, q_ref, *refs):
        out_ref = refs[-1]
        kv_refs = refs[:4]
        weights = refs[4:-1]
        x_index = idx_ref[0]
        core = idx_ref[1]
        length = idx_ref[2]
        part_index = idx_ref[3]

        def positions(dim, part, which):
            i = lax.broadcasted_iota(jnp.int32, (2 * tokens, tokens), dim) % tokens
            return part * part_rows + (i // rows) * (2 * rows) + which * rows + i % rows

        q_pos = positions(0, part_index, core)
        q = q_ref[...]
        numerators = []
        total = None
        for n, kv_ref in enumerate(kv_refs):
            k_pos = positions(1, part_index - 1 + n // 2, core if n % 2 == 0 else 1 - core)
            allowed = (k_pos <= q_pos) & (k_pos < length) & (k_pos >= 0)
            scores = lax.dot_general(
                q,
                kv_ref[:, :256],
                (((1,), (1,)), ((), ())),
                preferred_element_type=F32,
            ) * HEAD_DIM ** (-0.5)
            capped = 50.0 * jnp.tanh(scores / 50.0)
            numerators.append(jnp.where(allowed, jnp.exp(capped), 0.0))
            added = jnp.sum(numerators[-1], axis=-1, keepdims=True)
            total = added if total is None else total + added
        context = None
        for num, kv_ref in zip(numerators, kv_refs):
            prod = jnp.dot(
                (num / total).astype(BF16), kv_ref[:, 256:], preferred_element_type=F32
            )
            context = prod if context is None else context + prod
        context = context.astype(BF16)
        lefts = [
            context[c * tokens : (c + 1) * tokens, h * 128 : (h + 1) * 128]
            for c in range(2)
            for h in range(2)
        ]
        for d in range(4):
            out = None
            for k in range(4):
                prod = jnp.dot(lefts[k], weights[4 * k + d][...], preferred_element_type=F32)
                out = prod if out is None else out + prod
            at = pl.multiple_of((x_index ^ d) * quarter, 128)
            out_ref[:, pl.ds(at, quarter)] = out.astype(BF16)

    return kernel_call(
        kernel,
        [idx, queries, *blocks, *own[0], *own[1], *peer[0], *peer[1]],
        [SMEM] + [VMEM] * 21,
        [(tokens, 4 * quarter)],
    )


def finished(pieces, states, gain):
    rows, width = states.shape
    copies = pieces.shape[0] // rows

    def kernel(p_ref, states_ref, gain_ref, out_ref):
        total = p_ref[:rows, :].astype(F32)
        for k in range(1, copies):
            total = total + p_ref[k * rows : (k + 1) * rows, :].astype(F32)
        scale = lax.rsqrt(jnp.mean(total * total, axis=-1, keepdims=True) + 1e-06)
        out = states_ref[...].astype(F32) + total * scale * gain_ref[...]
        out_ref[...] = out.astype(BF16)

    return kernel_call(kernel, [pieces, states, gain], [VMEM] * 3, [states.shape])


NEAR, FAR = 1, 3


def first_halves(plan, scale, sources):
    sent = [share_call(plan, scale, s, 8 * i, 2, (), False) for i, s in enumerate(sources)]
    return [exchanged(s, "task", (NEAR, FAR)[i]) for i, s in enumerate(sent)]


def second_halves(plan, scale, sources, got):
    sent = [
        share_call(plan, scale, s, 8 * i + 2, 1, ((got[i], 8 * i + 3),), False)
        for i, s in enumerate(sources)
    ]
    return sent, [exchanged(s, "task", (FAR, NEAR)[i]) for i, s in enumerate(sent)]


def shares(plan, scale, sources, got, more):
    return [
        share_call(plan, scale, s, 8 * i + 4, 1, ((got[i], 8 * i + 5), (more[i], None)), True)
        for i, s in enumerate(sources)
    ]


def neighbours(own):
    near = [exchanged(o, "task", NEAR) for o in own]
    far = [exchanged(o, "task", FAR) for o in own]
    return near, far


def completed(own, near, far):
    opposite = [exchanged(far[0], "task", NEAR), exchanged(near[1], "task", FAR)]
    return [(own[i], near[i], opposite[i], far[i]) for i in range(2)]


def gathered(own):
    return completed(own, *neighbours(own))


def of_partner(pieces):
    return [tuple(exchanged(p, "mp", 1) for p in group) for group in pieces]


def per_device(
    hidden_in,
    lengths,
    layer_targets,
    task_weights,
    norm_gains,
    query_weight,
    key_weight,
    value_weight,
    output_weight,
    query_fisher,
    key_fisher,
    value_fisher,
    output_fisher,
):
    x_index = lax.axis_index("task")
    mp_index = lax.axis_index("mp")
    section_index = lax.axis_index("section")
    core = mp_index % 2
    chips = lax.axis_size("mp") // 2
    groups = [[2 * z + c for z in range(chips)] for c in range(2)]
    sections = lax.axis_size("section")
    width = hidden_in.shape[2]
    parts = 2
    rows = hidden_in.shape[1] // parts
    last_part = mp_index >= chips
    length = lengths[0]
    pre_gain = norm_gains[0, 0:1]
    post_gain = norm_gains[0, 1:2]
    scale = lax.dynamic_slice_in_dim(task_weights, x_index, 1)

    b = x_index // 2
    a = (x_index % 2) ^ b

    def block_a(h1, h2):
        return jnp.where(h1 == 0, 3 * h2, 1 + h2)

    def block_b(h1, h2):
        return jnp.where(h1 == 0, h2, 3 - h2)

    zero = jnp.zeros_like(a)
    plan = jnp.stack(
        [
            block_a(1 - a, 0),
            block_a(1 - a, 1),
            block_a(a, 1 - b),
            1 - b,
            x_index,
            b,
            zero,
            zero,
            block_b(1 - b, 0),
            block_b(1 - b, 1),
            block_b(b, 1 - a),
            1 - a,
            x_index,
            a,
            zero,
            zero,
        ]
    ).astype(jnp.int32)
    part_at = [jnp.clip(t - section_index, 0, parts - 1) for t in range(sections + parts - 1)]
    scalars = [jnp.stack([x_index, core, length, h]).astype(jnp.int32) for h in part_at]

    def quarters(array):
        array = array[0, 0]
        return array.reshape(4, array.shape[0] // 4, array.shape[1])

    def cut_rows(ref, block, row, sub):
        return ref.at[block, pl.ds(row, sub), :]

    def cut_columns(start):
        def cut(ref, block, row, sub):
            at = pl.multiple_of(block * (width // 4), 128)
            return ref.at[pl.ds(start + row, sub), pl.ds(at, width // 4)]

        return cut

    qkv_sources = (
        ((quarters(query_weight),), (quarters(query_fisher),), width // 4, (256,), cut_rows),
        (
            (quarters(key_weight), quarters(value_weight)),
            (quarters(key_fisher), quarters(value_fisher)),
            width // 4,
            (128, 128),
            cut_rows,
        ),
    )
    out_sources = tuple(
        (
            (output_weight[0, 0],),
            (output_fisher[0, 0],),
            128,
            (width // 4,),
            cut_columns(start),
        )
        for start in (0, 128)
    )

    part_rows = 2 * rows * chips
    positions = (
        part_rows * jnp.arange(parts, dtype=jnp.int32)[:, None, None]
        + 2 * rows * jnp.arange(chips, dtype=jnp.int32)[None, :, None]
        + core * rows
        + jnp.arange(rows, dtype=jnp.int32)[None, None, :]
    ).reshape(parts, -1)
    frequency = 10000.0 ** (-2.0 * jnp.arange(HEAD_DIM // 2, dtype=F32) / HEAD_DIM)
    angles = positions.astype(F32)[:, :, None] * frequency[None, None, :]
    cosine = jnp.cos(angles)
    sine = jnp.sin(angles)

    def spread(array):
        pieces = array.reshape(chips, rows, width)
        moved = lax.all_to_all(pieces, "mp", 0, 0, tiled=True, axis_index_groups=groups)
        return moved.reshape(chips * rows, width)

    straight = [(m, 2 * m) for m in range(chips)]
    straight += [(m, 2 * (m - chips) + 1) for m in range(chips, 2 * chips)]
    crossed = [(m, 2 * m + 1) for m in range(chips)]
    crossed += [(m, 2 * (m - chips)) for m in range(chips, 2 * chips)]

    def dealt(array):
        low, high = array[:rows], array[rows:]
        one = lax.ppermute(jnp.where(last_part, high, low), "mp", straight)
        other = lax.ppermute(jnp.where(last_part, low, high), "mp", crossed)
        return jnp.where(core == 0, one, other), jnp.where(core == 0, other, one)

    def collected(first, second):
        one = lax.ppermute(
            jnp.where(core == 0, first, second), "mp", [(j, i) for i, j in straight]
        )
        other = lax.ppermute(
            jnp.where(core == 0, second, first), "mp", [(j, i) for i, j in crossed]
        )
        low = jnp.where(last_part, other, one)
        high = jnp.where(last_part, one, other)
        return jnp.concatenate([low, high], axis=0)

    def projected(t, normed):
        queries, kv = project(scalars[t], normed, qkv_own, qkv_peer, cosine, sine)
        return queries, (kv, exchanged(kv, "mp", 1))

    with jax.named_scope("merge"):
        qkv_got = first_halves(plan, scale, qkv_sources)
        inputs = dealt(hidden_in[0])
        first_normed = spread(normed_copies(inputs[0], pre_gain, chips))
        targets = dealt(layer_targets[0, 0])
        out_got = first_halves(plan, scale, out_sources)
        qkv_got, inputs, first_normed, targets, cosine, sine = lax.optimization_barrier(
            (qkv_got, inputs, first_normed, targets, cosine, sine)
        )
        qkv_sent, qkv_more = second_halves(plan, scale, qkv_sources, qkv_got)
        out_got, _ = lax.optimization_barrier((out_got, qkv_sent))
        out_sent, out_more = second_halves(plan, scale, out_sources, out_got)
        qkv_share = shares(plan, scale, qkv_sources, qkv_got, qkv_more)
        out_more, _ = lax.optimization_barrier((out_more, qkv_share))
        out_share = shares(plan, scale, out_sources, out_got, out_more)
        qkv_first = neighbours(qkv_share)
        qkv_first, _ = lax.optimization_barrier((qkv_first, out_share))
        qkv_own = completed(qkv_share, *qkv_first)
        qkv_peer = of_partner(qkv_own)
        out_first = neighbours(out_share)
    with jax.named_scope("layer"):
        queries, kv = projected(0, first_normed)
    with jax.named_scope("merge"):
        out_first, _ = lax.optimization_barrier((out_first, queries))
        out_own = completed(out_share, *out_first)
        out_peer = of_partner(out_own)

    chosen = [None] * parts
    states = inputs[0]
    before = kv
    for t in range(sections + parts - 1):
        with jax.named_scope("layer"):
            if t > 0:
                states = lax.ppermute(
                    layer_out, "section", [(i, i + 1) for i in range(sections - 1)]
                )
                if t < parts:
                    states = jnp.where(section_index == 0, inputs[t], states)
                before = kv
                queries, kv = projected(t, spread(normed_copies(states, pre_gain, chips)))
            partial = attend(scalars[t], queries, (*before, *kv), out_own, out_peer, rows)
            layer_out = finished(spread(partial), states, post_gain)
            for h in range(parts):
                if 0 <= t - h < sections:
                    chosen[h] = (
                        layer_out
                        if chosen[h] is None
                        else jnp.where(section_index == t - h, layer_out, chosen[h])
                    )
    with jax.named_scope("loss"):
        loss_part = 0.0
        own_rows = jnp.arange(rows, dtype=jnp.int32) + mp_index * rows
        for h in range(parts):
            mismatch = chosen[h].astype(F32) - targets[h].astype(F32)
            live = (part_rows * h + own_rows < length)[:, None]
            loss_part = loss_part + jnp.sum(jnp.where(live, mismatch * mismatch, 0.0))
        copies = jnp.broadcast_to(loss_part, (2 * chips, 1))
        total = jnp.sum(lax.all_to_all(copies, "mp", 0, 0, tiled=True))
        loss = total / (length.astype(F32) * width)
        outputs = collected(*chosen)
    return (outputs[None, None], loss[None, None])


def solution(mesh):
    in_specs = (
        P("task", "mp", None),
        P("task"),
        P("section", "task", "mp", None),
        P(),
        P("section", None, None),
        P("task", "section", None, "mp"),
        P("task", "section", None, "mp"),
        P("task", "section", None, "mp"),
        P("task", "section", "mp", None),
        P("task", "section", None, "mp"),
        P("task", "section", None, "mp"),
        P("task", "section", None, "mp"),
        P("task", "section", "mp", None),
    )
    out_specs = (P("section", "task", "mp", None), P("section", "task"))
    return jax.shard_map(
        per_device, mesh=mesh, in_specs=in_specs, out_specs=out_specs, check_vma=False
    )
```

```python
import functools

import jax
import jax.numpy as jnp
from jax import lax
from jax.experimental import pallas as pl
from jax.experimental.pallas import tpu as pltpu
from jax.sharding import PartitionSpec as P

HEAD_DIM = 256
F32 = jnp.float32
BF16 = jnp.bfloat16
SMEM = pltpu.SMEM
VMEM = pltpu.VMEM
HBM = pltpu.HBM


def exchanged(array, axis, mask):
    return lax.ppermute(array, axis, [(i, i ^ mask) for i in range(lax.axis_size(axis))])


def placed(array, space):
    return pltpu.with_memory_space_constraint(array, space)


def result_on_chip(shape, dtype=BF16):
    return VMEM(shape, dtype)


def kernel_call(kernel, operands, spaces, shapes, scratch=(), mib=16):
    operands = [a if space == SMEM else placed(a, space) for a, space in zip(operands, spaces)]
    outs = pl.pallas_call(
        kernel,
        out_shape=tuple(
            result_on_chip(shape[:-1], F32) if shape[-1] is F32 else result_on_chip(shape)
            for shape in shapes
        ),
        in_specs=[pl.BlockSpec(memory_space=space) for space in spaces],
        out_specs=tuple(pl.BlockSpec(memory_space=VMEM) for _ in shapes),
        scratch_shapes=scratch,
        compiler_params=pltpu.CompilerParams(vmem_limit_bytes=mib * 1024 * 1024),
    )(*operands)
    return outs[0] if len(shapes) == 1 else outs


def share_call(plan, scale, jobs, count, finish):
    rows = jobs[0][0][2]
    total = sum(jobs[0][0][3])
    sub = rows // 2
    parts = count * 2
    strip = 64 if sub % 64 == 0 and sub > 64 else 16
    operands = [plan, scale]
    spaces = [SMEM, SMEM]
    scratch = []
    for (weights, fishers, _, widths, _), _, received in jobs:
        n = len(weights)
        operands += [*weights, *fishers, *(array for array, _ in received)]
        spaces += [HBM] * (2 * n) + [VMEM] * len(received)
        scratch += [VMEM((parts, sub, widths[k % n]), BF16) for k in range(2 * n)]
        scratch.append(pltpu.SemaphoreType.DMA((2 * n, parts)))
    shape = (len(jobs), rows, total) if finish else (2, count, rows, total)

    def kernel(plan_ref, scale_ref, *refs):
        ins = list(refs[: len(operands) - 2])
        out_ref = refs[len(operands) - 2]
        held = list(refs[len(operands) - 1 :])
        task_scale = scale_ref[0]
        work = []
        for job, ((weights, _, _, widths, cut), base, received) in enumerate(jobs):
            n = len(weights)
            arrays = [ins.pop(0) for _ in range(2 * n)]
            gots = [ins.pop(0) for _ in received]
            buffers = [held.pop(0) for _ in range(2 * n)]
            sems = held.pop(0)
            blocks = [0 if entry is None else plan_ref[entry] for _, entry in received]

            def copy(k, part, arrays=arrays, buffers=buffers, sems=sems, base=base, cut=cut):
                return pltpu.make_async_copy(
                    cut(arrays[k], plan_ref[base + part // 2], (part % 2) * sub, sub),
                    buffers[k].at[part],
                    sems.at[k, part],
                )

            for part in range(parts):
                for k in range(2 * n):
                    copy(k, part).start()
            work.append((job, n, widths, copy, buffers, gots, blocks))

        for job, n, widths, copy, buffers, gots, blocks in work:

            def one_strip(part, i):
                inside = pl.ds(pl.multiple_of(i * strip, strip), strip)
                lines = pl.ds(pl.multiple_of((part % 2) * sub + i * strip, strip), strip)
                at = 0
                for k in range(n):
                    scaled = buffers[n + k][part, inside, :].astype(F32) * task_scale
                    term = scaled * buffers[k][part, inside, :].astype(F32)
                    sums = [term.astype(BF16), scaled.astype(BF16)]
                    cols = slice(at, at + widths[k])
                    at += widths[k]
                    for got, block in zip(gots, blocks):
                        sums = [
                            v.astype(F32) + got[i, block, lines, cols].astype(F32)
                            for i, v in enumerate(sums)
                        ]
                    if finish:
                        out_ref[job, lines, cols] = (sums[0] / sums[1]).astype(BF16)
                    else:
                        out_ref[0, part // 2, lines, cols] = sums[0].astype(BF16)
                        out_ref[1, part // 2, lines, cols] = sums[1].astype(BF16)

            def one_part(part, carry):
                for k in range(2 * n):
                    copy(k, part).wait()
                lax.fori_loop(0, sub // strip, lambda i, c: (one_strip(part, i), c)[1], 0)
                return carry

            lax.fori_loop(0, parts, one_part, 0)

    return kernel_call(kernel, operands, spaces, [shape], scratch)


def dealing(idx, hidden, target):
    rows, width = hidden.shape
    half = rows // 2

    def kernel(idx_ref, h_ref, t_ref, straight_ref, crossed_ref):
        last = idx_ref[4] == 1
        for at, ref in ((0, h_ref), (half, t_ref)):
            low = ref[:half, :].astype(F32)
            high = ref[half:, :].astype(F32)
            straight_ref[at : at + half, :] = jnp.where(last, high, low).astype(BF16)
            crossed_ref[at : at + half, :] = jnp.where(last, low, high).astype(BF16)

    return kernel_call(
        kernel, [idx, hidden, target], [SMEM, VMEM, VMEM], [(rows, width), (rows, width)]
    )


def entered(idx, gain, straight, crossed, incoming, part, copies):
    rows, width = straight.shape[0] // 2, straight.shape[1]
    arrays = [straight, crossed] + ([] if incoming is None else [incoming])

    def kernel(idx_ref, gain_ref, s_ref, c_ref, *refs):
        out_ref, states_ref = refs[-2:]
        x = jnp.where(
            idx_ref[1] == part, s_ref[:rows, :].astype(F32), c_ref[:rows, :].astype(F32)
        )
        if incoming is not None:
            x = jnp.where(idx_ref[3] == 0, x, refs[0][...].astype(F32))
        scale = lax.rsqrt(jnp.mean(x * x, axis=-1, keepdims=True) + 1e-06)
        y = (x * scale * gain_ref[...]).astype(BF16)
        for k in range(copies):
            out_ref[k * rows : (k + 1) * rows, :] = y
        states_ref[...] = x.astype(BF16)

    return kernel_call(
        kernel,
        [idx, gain, *arrays],
        [SMEM, VMEM] + [VMEM] * len(arrays),
        [(copies * rows, width), (rows, width)],
    )


def left(idx, outs, straight, crossed):
    rows, width = outs[0][0].shape
    flat = [o for group in outs for o in group]

    def kernel(idx_ref, s_ref, c_ref, *refs):
        keep_ref, cross_ref, loss_ref = refs[-3:]
        core = idx_ref[1]
        length = idx_ref[2]
        section = idx_ref[3]
        mp = idx_ref[5]
        total = None
        chosen = []
        for h, group in enumerate(outs):
            ins = refs[h * len(group) : (h + 1) * len(group)]
            out = ins[0][...].astype(F32)
            for layer in range(1, len(group)):
                out = jnp.where(section == layer, ins[layer][...].astype(F32), out)
            chosen.append(out)
            target = jnp.where(
                core == h, s_ref[rows:, :].astype(F32), c_ref[rows:, :].astype(F32)
            )
            row = lax.broadcasted_iota(jnp.int32, (rows, width), 0)
            live = h * (rows * idx_ref[6]) + mp * rows + row < length
            error = jnp.where(live, (out - target) * (out - target), 0.0)
            error = jnp.sum(jnp.sum(error, axis=1, keepdims=True), axis=0, keepdims=True)
            total = error if total is None else total + error
        keep_ref[...] = jnp.where(core == 0, chosen[0], chosen[1]).astype(BF16)
        cross_ref[...] = jnp.where(core == 0, chosen[1], chosen[0]).astype(BF16)
        loss_ref[...] = jnp.broadcast_to(total[:, :, None], loss_ref.shape)

    return kernel_call(
        kernel,
        [idx, straight, crossed, *flat],
        [SMEM] + [VMEM] * (2 + len(flat)),
        [(rows, width), (rows, width), (16, 1, 128, F32)],
    )


def rejoined(idx, kept, crossed):
    rows, width = kept.shape

    def kernel(idx_ref, k_ref, c_ref, out_ref):
        last = idx_ref[4] == 1
        a = k_ref[...].astype(F32)
        b = c_ref[...].astype(F32)
        out_ref[:rows, :] = jnp.where(last, b, a).astype(BF16)
        out_ref[rows:, :] = jnp.where(last, a, b).astype(BF16)

    return kernel_call(kernel, [idx, kept, crossed], [SMEM, VMEM, VMEM], [(2 * rows, width)])


def weight(refs, d, k):
    own, near, low, high, far = refs
    if d == 2:
        return (low, high)[k][...]
    return (own, near, None, far)[d][k]


def part_of(idx_ref, step):
    return jnp.clip(step - idx_ref[3], 0, 1)


def project(idx, step, normed, own, peer, cosine, sine):
    tokens, width = normed.shape
    quarter = width // 4

    def kernel(idx_ref, x_ref, cos_ref, sin_ref, *refs):
        q_ref, kv_ref = refs[-2:]
        x_index = idx_ref[0]
        core = idx_ref[1]
        part_index = part_of(idx_ref, step)
        sums = [None] * 4
        for d in range(4):
            at = pl.multiple_of((x_index ^ d) * quarter, 128)
            part = x_ref[:, pl.ds(at, quarter)]
            for k in range(4):
                w = weight(refs[5 * (k // 2) : 5 * (k // 2) + 5], d, k % 2)
                prod = jnp.dot(part, w, preferred_element_type=F32)
                sums[k] = prod if d == 0 else sums[k] + prod
        q_mine, mine, q_theirs, theirs = sums
        cos = cos_ref[part_index]
        sin = sin_ref[part_index]
        for at, q in ((0, q_mine), (tokens, q_theirs)):
            a = q[:, :128]
            b = q[:, 128:]
            q_ref[at : at + tokens, :128] = (a * cos - b * sin).astype(BF16)
            q_ref[at : at + tokens, 128:] = (b * cos + a * sin).astype(BF16)
        first = core == 0
        k_mine = mine[:, :128].astype(BF16).astype(F32)
        k_theirs = theirs[:, :128].astype(BF16).astype(F32)
        a = jnp.where(first, k_mine, k_theirs)
        b = jnp.where(first, k_theirs, k_mine)
        kv_ref[:, :128] = (a * cos - b * sin).astype(BF16)
        kv_ref[:, 128:256] = (b * cos + a * sin).astype(BF16)
        kv_ref[:, 256:384] = jnp.where(first, mine[:, 128:], theirs[:, 128:]).astype(BF16)
        kv_ref[:, 384:] = jnp.where(first, theirs[:, 128:], mine[:, 128:]).astype(BF16)

    return kernel_call(
        kernel,
        [idx, normed, cosine, sine, *own, *peer],
        [SMEM] + [VMEM] * 13,
        [(2 * tokens, 256), (tokens, 512)],
    )


def attend(idx, step, queries, blocks, own, peer, rows):
    tokens = queries.shape[0] // 2
    quarter = own[0].shape[2]
    part_rows = 2 * tokens

    def kernel(idx_ref, q_ref, *refs):
        out_ref = refs[-1]
        kv_refs = refs[:4]
        weights = refs[4:-1]
        x_index = idx_ref[0]
        core = idx_ref[1]
        length = idx_ref[2]
        part_index = part_of(idx_ref, step)

        def positions(dim, part, which):
            i = lax.broadcasted_iota(jnp.int32, (2 * tokens, tokens), dim) % tokens
            return part * part_rows + (i // rows) * (2 * rows) + which * rows + i % rows

        q_pos = positions(0, part_index, core)
        q = q_ref[...]
        numerators = []
        total = None
        for n, kv_ref in enumerate(kv_refs):
            k_pos = positions(1, part_index - 1 + n // 2, core if n % 2 == 0 else 1 - core)
            allowed = (k_pos <= q_pos) & (k_pos < length) & (k_pos >= 0)
            scores = lax.dot_general(
                q,
                kv_ref[:, :256],
                (((1,), (1,)), ((), ())),
                preferred_element_type=F32,
            ) * HEAD_DIM ** (-0.5)
            capped = 50.0 * jnp.tanh(scores / 50.0)
            numerators.append(jnp.where(allowed, jnp.exp(capped), 0.0))
            added = jnp.sum(numerators[-1], axis=-1, keepdims=True)
            total = added if total is None else total + added
        context = None
        for num, kv_ref in zip(numerators, kv_refs):
            prod = jnp.dot(
                (num / total).astype(BF16), kv_ref[:, 256:], preferred_element_type=F32
            )
            context = prod if context is None else context + prod
        context = context.astype(BF16)
        lefts = [
            context[c * tokens : (c + 1) * tokens, h * 128 : (h + 1) * 128]
            for c in range(2)
            for h in range(2)
        ]
        for d in range(4):
            out = None
            for k in range(4):
                w = weight(weights[5 * (k // 2) : 5 * (k // 2) + 5], d, k % 2)
                prod = jnp.dot(lefts[k], w, preferred_element_type=F32)
                out = prod if out is None else out + prod
            at = pl.multiple_of((x_index ^ d) * quarter, 128)
            out_ref[:, pl.ds(at, quarter)] = out.astype(BF16)

    return kernel_call(
        kernel,
        [idx, queries, *blocks, *own, *peer],
        [SMEM] + [VMEM] * 15,
        [(tokens, 4 * quarter)],
    )


def normed_copies(states, gain, copies):
    rows, width = states.shape

    def kernel(states_ref, gain_ref, out_ref):
        x = states_ref[...].astype(F32)
        scale = lax.rsqrt(jnp.mean(x * x, axis=-1, keepdims=True) + 1e-06)
        y = (x * scale * gain_ref[...]).astype(BF16)
        for k in range(copies):
            out_ref[k * rows : (k + 1) * rows, :] = y

    return kernel_call(kernel, [states, gain], [VMEM] * 2, [(copies * rows, width)])


def finished(pieces, states, gain):
    rows, width = states.shape
    copies = pieces.shape[0] // rows

    def kernel(p_ref, states_ref, gain_ref, out_ref):
        total = p_ref[:rows, :].astype(F32)
        for k in range(1, copies):
            total = total + p_ref[k * rows : (k + 1) * rows, :].astype(F32)
        scale = lax.rsqrt(jnp.mean(total * total, axis=-1, keepdims=True) + 1e-06)
        out = states_ref[...].astype(F32) + total * scale * gain_ref[...]
        out_ref[...] = out.astype(BF16)

    return kernel_call(kernel, [pieces, states, gain], [VMEM] * 3, [states.shape])


NEAR, FAR = 1, 3


def first_halves(plan, scale, sources):
    sent = [share_call(plan, scale, [(s, 8 * i, ())], 2, False) for i, s in enumerate(sources)]
    return sent, [exchanged(s, "task", (NEAR, FAR)[i]) for i, s in enumerate(sent)]


def second_halves(plan, scale, sources, got):
    sent = [
        share_call(plan, scale, [(s, 8 * i + 2, ((got[i], 8 * i + 3),))], 1, False)
        for i, s in enumerate(sources)
    ]
    return sent, [exchanged(s, "task", (FAR, NEAR)[i]) for i, s in enumerate(sent)]


def shares(plan, scale, sources, got, more):
    jobs = [
        (s, 8 * i + 4, ((got[i], 8 * i + 5), (more[i], None))) for i, s in enumerate(sources)
    ]
    return share_call(plan, scale, jobs, 1, True)


def neighbours(own):
    return exchanged(own, "task", NEAR), exchanged(own, "task", FAR)


def completed(own, near, far):
    return own, near, exchanged(far[0], "task", NEAR), exchanged(near[1], "task", FAR), far


def of_partner(pieces):
    return tuple(exchanged(p, "mp", 1) for p in pieces)


def per_device(
    hidden_in,
    lengths,
    layer_targets,
    task_weights,
    norm_gains,
    query_weight,
    key_weight,
    value_weight,
    output_weight,
    query_fisher,
    key_fisher,
    value_fisher,
    output_fisher,
):
    x_index = lax.axis_index("task")
    mp_index = lax.axis_index("mp")
    section_index = lax.axis_index("section")
    core = mp_index % 2
    chips = lax.axis_size("mp") // 2
    groups = [[2 * z + c for z in range(chips)] for c in range(2)]
    sections = lax.axis_size("section")
    width = hidden_in.shape[2]
    parts = 2
    rows = hidden_in.shape[1] // parts
    length = lengths[0]
    pre_gain = norm_gains[0, 0:1]
    post_gain = norm_gains[0, 1:2]
    scale = lax.dynamic_slice_in_dim(task_weights, x_index, 1)

    b = x_index // 2
    a = (x_index % 2) ^ b

    def block_a(h1, h2):
        return jnp.where(h1 == 0, 3 * h2, 1 + h2)

    def block_b(h1, h2):
        return jnp.where(h1 == 0, h2, 3 - h2)

    zero = jnp.zeros_like(a)
    plan = jnp.stack(
        [
            block_a(1 - a, 0),
            block_a(1 - a, 1),
            block_a(a, 1 - b),
            1 - b,
            x_index,
            b,
            zero,
            zero,
            block_b(1 - b, 0),
            block_b(1 - b, 1),
            block_b(b, 1 - a),
            1 - a,
            x_index,
            a,
            zero,
            zero,
        ]
    ).astype(jnp.int32)
    scalars = jnp.stack(
        [x_index, core, length, section_index, mp_index // chips, mp_index, 2 * chips]
    ).astype(jnp.int32)

    def quarters(array):
        array = array[0, 0]
        return array.reshape(4, array.shape[0] // 4, array.shape[1])

    def cut_rows(ref, block, row, sub):
        return ref.at[block, pl.ds(row, sub), :]

    def cut_columns(start):
        def cut(ref, block, row, sub):
            at = pl.multiple_of(block * (width // 4), 128)
            return ref.at[pl.ds(start + row, sub), pl.ds(at, width // 4)]

        return cut

    qkv_sources = (
        ((quarters(query_weight),), (quarters(query_fisher),), width // 4, (256,), cut_rows),
        (
            (quarters(key_weight), quarters(value_weight)),
            (quarters(key_fisher), quarters(value_fisher)),
            width // 4,
            (128, 128),
            cut_rows,
        ),
    )
    out_sources = tuple(
        (
            (output_weight[0, 0],),
            (output_fisher[0, 0],),
            128,
            (width // 4,),
            cut_columns(start),
        )
        for start in (0, 128)
    )

    part_rows = 2 * rows * chips
    positions = (
        part_rows * jnp.arange(parts, dtype=jnp.int32)[:, None, None]
        + 2 * rows * jnp.arange(chips, dtype=jnp.int32)[None, :, None]
        + core * rows
        + jnp.arange(rows, dtype=jnp.int32)[None, None, :]
    ).reshape(parts, -1)
    frequency = 10000.0 ** (-2.0 * jnp.arange(HEAD_DIM // 2, dtype=F32) / HEAD_DIM)
    angles = positions.astype(F32)[:, :, None] * frequency[None, None, :]
    cosine = jnp.cos(angles)
    sine = jnp.sin(angles)

    def spread(array):
        pieces = array.reshape(chips, rows, width)
        moved = lax.all_to_all(pieces, "mp", 0, 0, tiled=True, axis_index_groups=groups)
        return moved.reshape(chips * rows, width)

    straight = [(m, 2 * m) for m in range(chips)]
    straight += [(m, 2 * (m - chips) + 1) for m in range(chips, 2 * chips)]
    crossed = [(m, 2 * m + 1) for m in range(chips)]
    crossed += [(m, 2 * (m - chips)) for m in range(chips, 2 * chips)]

    def over_mp(array, pairs):
        return lax.ppermute(array, "mp", pairs)

    def projected(t, normed):
        queries, kv = project(scalars, t, normed, qkv_own, qkv_peer, cosine, sine)
        return queries, (kv, exchanged(kv, "mp", 1))

    with jax.named_scope("merge"):
        _, qkv_got = first_halves(plan, scale, qkv_sources)
        one, other = dealing(scalars, hidden_in[0], layer_targets[0, 0])
        one, other = over_mp(one, straight), over_mp(other, crossed)
        out_sent, out_got = first_halves(plan, scale, out_sources)
        first, states = entered(scalars, pre_gain, one, other, None, 0, chips)
        first, cosine, sine, _ = lax.optimization_barrier((first, cosine, sine, out_sent))
        first = spread(first)
        qkv_got, first = lax.optimization_barrier((qkv_got, first))
        qkv_sent, qkv_more = second_halves(plan, scale, qkv_sources, qkv_got)
        out_got, _ = lax.optimization_barrier((out_got, qkv_sent))
        out_sent, out_more = second_halves(plan, scale, out_sources, out_got)
        qkv_share = shares(plan, scale, qkv_sources, qkv_got, qkv_more)
        out_more, _ = lax.optimization_barrier((out_more, qkv_share))
        out_share = shares(plan, scale, out_sources, out_got, out_more)
        qkv_first = neighbours(qkv_share)
        qkv_first, _ = lax.optimization_barrier((qkv_first, out_share))
        qkv_own = completed(qkv_share, *qkv_first)
        qkv_peer = of_partner(qkv_own)
        out_first = neighbours(out_share)
    with jax.named_scope("layer"):
        queries, kv = projected(0, first)
    with jax.named_scope("merge"):
        out_own = completed(out_share, *out_first)
        out_peer = of_partner(out_own)

    outs = []
    before = kv
    for t in range(sections + parts - 1):
        with jax.named_scope("layer"):
            if t > 0:
                incoming = lax.ppermute(
                    outs[-1], "section", [(i, i + 1) for i in range(sections - 1)]
                )
                if t < parts:
                    normed, states = entered(scalars, pre_gain, one, other, incoming, t, chips)
                else:
                    normed, states = normed_copies(incoming, pre_gain, chips), incoming
                before = kv
                queries, kv = projected(t, spread(normed))
            partial = attend(scalars, t, queries, (*before, *kv), out_own, out_peer, rows)
            outs.append(finished(spread(partial), states, post_gain))
    with jax.named_scope("loss"):
        kept, moved, error = left(
            scalars, [outs[h : h + sections] for h in range(parts)], one, other
        )
        error = lax.all_to_all(error, "mp", 0, 0, tiled=True)
        kept = over_mp(kept, [(j, i) for i, j in straight])
        moved = over_mp(moved, [(j, i) for i, j in crossed])
        outputs = rejoined(scalars, kept, moved)
        loss = jnp.sum(error[:, 0, 0]) / (length.astype(F32) * width)
    return (outputs[None, None], loss[None, None])


def solution(mesh):
    in_specs = (
        P("task", "mp", None),
        P("task"),
        P("section", "task", "mp", None),
        P(),
        P("section", None, None),
        P("task", "section", None, "mp"),
        P("task", "section", None, "mp"),
        P("task", "section", None, "mp"),
        P("task", "section", "mp", None),
        P("task", "section", None, "mp"),
        P("task", "section", None, "mp"),
        P("task", "section", None, "mp"),
        P("task", "section", "mp", None),
    )
    out_specs = (P("section", "task", "mp", None), P("section", "task"))
    return jax.shard_map(
        per_device, mesh=mesh, in_specs=in_specs, out_specs=out_specs, check_vma=False
    )
```

```python
import functools

import jax
import jax.numpy as jnp
from jax import lax
from jax.experimental import pallas as pl
from jax.experimental.pallas import tpu as pltpu
from jax.sharding import PartitionSpec as P

HEAD_DIM = 256
F32 = jnp.float32
BF16 = jnp.bfloat16
SMEM = pltpu.SMEM
VMEM = pltpu.VMEM
HBM = pltpu.HBM


def exchanged(array, axis, mask):
    return lax.ppermute(array, axis, [(i, i ^ mask) for i in range(lax.axis_size(axis))])


def placed(array, space):
    return pltpu.with_memory_space_constraint(array, space)


def result_on_chip(shape, dtype=BF16):
    return VMEM(shape, dtype)


def kernel_call(kernel, operands, spaces, shapes, scratch=(), mib=16):
    operands = [a if space == SMEM else placed(a, space) for a, space in zip(operands, spaces)]
    outs = pl.pallas_call(
        kernel,
        out_shape=tuple(
            result_on_chip(shape[:-1], F32) if shape[-1] is F32 else result_on_chip(shape)
            for shape in shapes
        ),
        in_specs=[pl.BlockSpec(memory_space=space) for space in spaces],
        out_specs=tuple(pl.BlockSpec(memory_space=VMEM) for _ in shapes),
        scratch_shapes=scratch,
        compiler_params=pltpu.CompilerParams(vmem_limit_bytes=mib * 1024 * 1024),
    )(*operands)
    return outs[0] if len(shapes) == 1 else outs


def share_call(plan, scale, jobs, count, finish):
    rows = jobs[0][0][2]
    total = sum(jobs[0][0][3])
    sub = rows // 2
    parts = count * 2
    strip = 64 if sub % 64 == 0 and sub > 64 else 16
    operands = [plan, scale]
    spaces = [SMEM, SMEM]
    scratch = []
    for (weights, fishers, _, widths, _), _, received in jobs:
        n = len(weights)
        operands += [*weights, *fishers, *(array for array, _ in received)]
        spaces += [HBM] * (2 * n) + [VMEM] * len(received)
        scratch += [VMEM((parts, sub, widths[k % n]), BF16) for k in range(2 * n)]
        scratch.append(pltpu.SemaphoreType.DMA((2 * n, parts)))
    shape = (len(jobs), rows, total) if finish else (2, count, rows, total)

    def kernel(plan_ref, scale_ref, *refs):
        ins = list(refs[: len(operands) - 2])
        out_ref = refs[len(operands) - 2]
        held = list(refs[len(operands) - 1 :])
        task_scale = scale_ref[0]
        work = []
        for job, ((weights, _, _, widths, cut), base, received) in enumerate(jobs):
            n = len(weights)
            arrays = [ins.pop(0) for _ in range(2 * n)]
            gots = [ins.pop(0) for _ in received]
            buffers = [held.pop(0) for _ in range(2 * n)]
            sems = held.pop(0)
            blocks = [0 if entry is None else plan_ref[entry] for _, entry in received]

            def copy(k, part, arrays=arrays, buffers=buffers, sems=sems, base=base, cut=cut):
                return pltpu.make_async_copy(
                    cut(arrays[k], plan_ref[base + part // 2], (part % 2) * sub, sub),
                    buffers[k].at[part],
                    sems.at[k, part],
                )

            for part in range(parts):
                for k in range(2 * n):
                    copy(k, part).start()
            work.append((job, n, widths, copy, buffers, gots, blocks))

        for job, n, widths, copy, buffers, gots, blocks in work:

            def one_strip(part, i):
                inside = pl.ds(pl.multiple_of(i * strip, strip), strip)
                lines = pl.ds(pl.multiple_of((part % 2) * sub + i * strip, strip), strip)
                at = 0
                for k in range(n):
                    scaled = buffers[n + k][part, inside, :].astype(F32) * task_scale
                    term = scaled * buffers[k][part, inside, :].astype(F32)
                    sums = [term.astype(BF16), scaled.astype(BF16)]
                    cols = slice(at, at + widths[k])
                    at += widths[k]
                    for got, block in zip(gots, blocks):
                        sums = [
                            v.astype(F32) + got[i, block, lines, cols].astype(F32)
                            for i, v in enumerate(sums)
                        ]
                    if finish:
                        out_ref[job, lines, cols] = (sums[0] / sums[1]).astype(BF16)
                    else:
                        out_ref[0, part // 2, lines, cols] = sums[0].astype(BF16)
                        out_ref[1, part // 2, lines, cols] = sums[1].astype(BF16)

            def one_part(part, carry):
                for k in range(2 * n):
                    copy(k, part).wait()
                lax.fori_loop(0, sub // strip, lambda i, c: (one_strip(part, i), c)[1], 0)
                return carry

            lax.fori_loop(0, parts, one_part, 0)

    return kernel_call(kernel, operands, spaces, [shape], scratch)


def dealing(idx, hidden, target):
    rows, width = hidden.shape
    half = rows // 2

    def kernel(idx_ref, h_ref, t_ref, straight_ref, crossed_ref):
        last = idx_ref[4] == 1
        for at, ref in ((0, h_ref), (half, t_ref)):
            low = ref[:half, :].astype(F32)
            high = ref[half:, :].astype(F32)
            straight_ref[at : at + half, :] = jnp.where(last, high, low).astype(BF16)
            crossed_ref[at : at + half, :] = jnp.where(last, low, high).astype(BF16)

    return kernel_call(
        kernel, [idx, hidden, target], [SMEM, VMEM, VMEM], [(rows, width), (rows, width)]
    )


def entered(idx, gain, straight, crossed, incoming, part, copies):
    rows, width = straight.shape[0] // 2, straight.shape[1]
    arrays = [straight, crossed] + ([] if incoming is None else [incoming])

    def kernel(idx_ref, gain_ref, s_ref, c_ref, *refs):
        out_ref, states_ref = refs[-2:]
        x = jnp.where(
            idx_ref[1] == part, s_ref[:rows, :].astype(F32), c_ref[:rows, :].astype(F32)
        )
        if incoming is not None:
            x = jnp.where(idx_ref[3] == 0, x, refs[0][...].astype(F32))
        scale = lax.rsqrt(jnp.mean(x * x, axis=-1, keepdims=True) + 1e-06)
        y = (x * scale * gain_ref[...]).astype(BF16)
        for k in range(copies):
            out_ref[k * rows : (k + 1) * rows, :] = y
        states_ref[...] = x.astype(BF16)

    return kernel_call(
        kernel,
        [idx, gain, *arrays],
        [SMEM, VMEM] + [VMEM] * len(arrays),
        [(copies * rows, width), (rows, width)],
    )


def left(idx, outs, straight, crossed):
    rows, width = outs[0][0].shape
    flat = [o for group in outs for o in group]

    def kernel(idx_ref, s_ref, c_ref, *refs):
        keep_ref, cross_ref, loss_ref = refs[-3:]
        core = idx_ref[1]
        length = idx_ref[2]
        section = idx_ref[3]
        mp = idx_ref[5]
        total = None
        chosen = []
        for h, group in enumerate(outs):
            ins = refs[h * len(group) : (h + 1) * len(group)]
            out = ins[0][...].astype(F32)
            for layer in range(1, len(group)):
                out = jnp.where(section == layer, ins[layer][...].astype(F32), out)
            chosen.append(out)
            target = jnp.where(
                core == h, s_ref[rows:, :].astype(F32), c_ref[rows:, :].astype(F32)
            )
            row = lax.broadcasted_iota(jnp.int32, (rows, width), 0)
            live = h * (rows * idx_ref[6]) + mp * rows + row < length
            error = jnp.where(live, (out - target) * (out - target), 0.0)
            error = jnp.sum(jnp.sum(error, axis=1, keepdims=True), axis=0, keepdims=True)
            total = error if total is None else total + error
        keep_ref[...] = jnp.where(core == 0, chosen[0], chosen[1]).astype(BF16)
        cross_ref[...] = jnp.where(core == 0, chosen[1], chosen[0]).astype(BF16)
        loss_ref[...] = jnp.broadcast_to(total[:, :, None], loss_ref.shape)

    return kernel_call(
        kernel,
        [idx, straight, crossed, *flat],
        [SMEM] + [VMEM] * (2 + len(flat)),
        [(rows, width), (rows, width), (16, 1, 128, F32)],
    )


def rejoined(idx, kept, crossed):
    rows, width = kept.shape

    def kernel(idx_ref, k_ref, c_ref, out_ref):
        last = idx_ref[4] == 1
        a = k_ref[...].astype(F32)
        b = c_ref[...].astype(F32)
        out_ref[:rows, :] = jnp.where(last, b, a).astype(BF16)
        out_ref[rows:, :] = jnp.where(last, a, b).astype(BF16)

    return kernel_call(kernel, [idx, kept, crossed], [SMEM, VMEM, VMEM], [(2 * rows, width)])


def weight(refs, d, k):
    own, near, low, high, far = refs
    if d == 2:
        return (low, high)[k][...]
    return (own, near, None, far)[d][k]


def part_of(idx_ref, step):
    return jnp.clip(step - idx_ref[3], 0, 1)


def project(idx, step, normed, own, peer, cosine, sine):
    tokens, width = normed.shape
    quarter = width // 4

    def kernel(idx_ref, x_ref, cos_ref, sin_ref, *refs):
        q_ref, kv_ref = refs[-2:]
        x_index = idx_ref[0]
        core = idx_ref[1]
        part_index = part_of(idx_ref, step)
        sums = [None] * 4
        for d in range(4):
            at = pl.multiple_of((x_index ^ d) * quarter, 128)
            part = x_ref[:, pl.ds(at, quarter)]
            for k in range(4):
                w = weight(refs[5 * (k // 2) : 5 * (k // 2) + 5], d, k % 2)
                prod = jnp.dot(part, w, preferred_element_type=F32)
                sums[k] = prod if d == 0 else sums[k] + prod
        q_mine, mine, q_theirs, theirs = sums
        cos = cos_ref[part_index]
        sin = sin_ref[part_index]
        for at, q in ((0, q_mine), (tokens, q_theirs)):
            a = q[:, :128]
            b = q[:, 128:]
            q_ref[at : at + tokens, :128] = (a * cos - b * sin).astype(BF16)
            q_ref[at : at + tokens, 128:] = (b * cos + a * sin).astype(BF16)
        first = core == 0
        k_mine = mine[:, :128].astype(BF16).astype(F32)
        k_theirs = theirs[:, :128].astype(BF16).astype(F32)
        a = jnp.where(first, k_mine, k_theirs)
        b = jnp.where(first, k_theirs, k_mine)
        kv_ref[:, :128] = (a * cos - b * sin).astype(BF16)
        kv_ref[:, 128:256] = (b * cos + a * sin).astype(BF16)
        kv_ref[:, 256:384] = jnp.where(first, mine[:, 128:], theirs[:, 128:]).astype(BF16)
        kv_ref[:, 384:] = jnp.where(first, theirs[:, 128:], mine[:, 128:]).astype(BF16)

    return kernel_call(
        kernel,
        [idx, normed, cosine, sine, *own, *peer],
        [SMEM] + [VMEM] * 13,
        [(2 * tokens, 256), (tokens, 512)],
    )


def attend(idx, step, queries, blocks, own, peer, rows):
    tokens = queries.shape[0] // 2
    quarter = own[0].shape[2]
    part_rows = 2 * tokens

    def kernel(idx_ref, q_ref, *refs):
        out_ref = refs[-1]
        kv_refs = refs[:4]
        weights = refs[4:-1]
        x_index = idx_ref[0]
        core = idx_ref[1]
        length = idx_ref[2]
        part_index = part_of(idx_ref, step)

        def positions(dim, part, which):
            i = lax.broadcasted_iota(jnp.int32, (2 * tokens, tokens), dim) % tokens
            return part * part_rows + (i // rows) * (2 * rows) + which * rows + i % rows

        q_pos = positions(0, part_index, core)
        q = q_ref[...]
        numerators = []
        total = None
        for n, kv_ref in enumerate(kv_refs):
            k_pos = positions(1, part_index - 1 + n // 2, core if n % 2 == 0 else 1 - core)
            allowed = (k_pos <= q_pos) & (k_pos < length) & (k_pos >= 0)
            scores = lax.dot_general(
                q,
                kv_ref[:, :256],
                (((1,), (1,)), ((), ())),
                preferred_element_type=F32,
            ) * HEAD_DIM ** (-0.5)
            capped = 50.0 * jnp.tanh(scores / 50.0)
            numerators.append(jnp.where(allowed, jnp.exp(capped), 0.0))
            added = jnp.sum(numerators[-1], axis=-1, keepdims=True)
            total = added if total is None else total + added
        context = None
        for num, kv_ref in zip(numerators, kv_refs):
            prod = jnp.dot(
                (num / total).astype(BF16), kv_ref[:, 256:], preferred_element_type=F32
            )
            context = prod if context is None else context + prod
        context = context.astype(BF16)
        lefts = [
            context[c * tokens : (c + 1) * tokens, h * 128 : (h + 1) * 128]
            for c in range(2)
            for h in range(2)
        ]
        for d in range(4):
            out = None
            for k in range(4):
                w = weight(weights[5 * (k // 2) : 5 * (k // 2) + 5], d, k % 2)
                prod = jnp.dot(lefts[k], w, preferred_element_type=F32)
                out = prod if out is None else out + prod
            at = pl.multiple_of((x_index ^ d) * quarter, 128)
            out_ref[:, pl.ds(at, quarter)] = out.astype(BF16)

    return kernel_call(
        kernel,
        [idx, queries, *blocks, *own, *peer],
        [SMEM] + [VMEM] * 15,
        [(tokens, 4 * quarter)],
    )


def normed_copies(states, gain, copies):
    rows, width = states.shape

    def kernel(states_ref, gain_ref, out_ref):
        x = states_ref[...].astype(F32)
        scale = lax.rsqrt(jnp.mean(x * x, axis=-1, keepdims=True) + 1e-06)
        y = (x * scale * gain_ref[...]).astype(BF16)
        for k in range(copies):
            out_ref[k * rows : (k + 1) * rows, :] = y

    return kernel_call(kernel, [states, gain], [VMEM] * 2, [(copies * rows, width)])


def finished(pieces, states, gain):
    rows, width = states.shape
    copies = pieces.shape[0] // rows

    def kernel(p_ref, states_ref, gain_ref, out_ref):
        total = p_ref[:rows, :].astype(F32)
        for k in range(1, copies):
            total = total + p_ref[k * rows : (k + 1) * rows, :].astype(F32)
        scale = lax.rsqrt(jnp.mean(total * total, axis=-1, keepdims=True) + 1e-06)
        out = states_ref[...].astype(F32) + total * scale * gain_ref[...]
        out_ref[...] = out.astype(BF16)

    return kernel_call(kernel, [pieces, states, gain], [VMEM] * 3, [states.shape])


NEAR, FAR = 1, 3


def first_halves(plan, scale, sources):
    sent = [share_call(plan, scale, [(s, 8 * i, ())], 2, False) for i, s in enumerate(sources)]
    return sent, [exchanged(s, "task", (NEAR, FAR)[i]) for i, s in enumerate(sent)]


def second_halves(plan, scale, sources, got):
    sent = [
        share_call(plan, scale, [(s, 8 * i + 2, ((got[i], 8 * i + 3),))], 1, False)
        for i, s in enumerate(sources)
    ]
    return sent, [exchanged(s, "task", (FAR, NEAR)[i]) for i, s in enumerate(sent)]


def shares(plan, scale, sources, got, more):
    jobs = [
        (s, 8 * i + 4, ((got[i], 8 * i + 5), (more[i], None))) for i, s in enumerate(sources)
    ]
    return share_call(plan, scale, jobs, 1, True)


def neighbours(own):
    return exchanged(own, "task", NEAR), exchanged(own, "task", FAR)


def completed(own, near, far):
    return own, near, exchanged(far[0], "task", NEAR), exchanged(near[1], "task", FAR), far


def of_partner(pieces):
    return tuple(exchanged(p, "mp", 1) for p in pieces)


def per_device(
    hidden_in,
    lengths,
    layer_targets,
    task_weights,
    norm_gains,
    query_weight,
    key_weight,
    value_weight,
    output_weight,
    query_fisher,
    key_fisher,
    value_fisher,
    output_fisher,
):
    x_index = lax.axis_index("task")
    mp_index = lax.axis_index("mp")
    section_index = lax.axis_index("section")
    core = mp_index % 2
    chips = lax.axis_size("mp") // 2
    groups = [[2 * z + c for z in range(chips)] for c in range(2)]
    sections = lax.axis_size("section")
    width = hidden_in.shape[2]
    parts = 2
    rows = hidden_in.shape[1] // parts
    length = lengths[0]
    pre_gain = norm_gains[0, 0:1]
    post_gain = norm_gains[0, 1:2]
    scale = lax.dynamic_slice_in_dim(task_weights, x_index, 1)

    b = x_index // 2
    a = (x_index % 2) ^ b

    def block_a(h1, h2):
        return jnp.where(h1 == 0, 3 * h2, 1 + h2)

    def block_b(h1, h2):
        return jnp.where(h1 == 0, h2, 3 - h2)

    zero = jnp.zeros_like(a)
    plan = jnp.stack(
        [
            block_a(1 - a, 0),
            block_a(1 - a, 1),
            block_a(a, 1 - b),
            1 - b,
            x_index,
            b,
            zero,
            zero,
            block_b(1 - b, 0),
            block_b(1 - b, 1),
            block_b(b, 1 - a),
            1 - a,
            x_index,
            a,
            zero,
            zero,
        ]
    ).astype(jnp.int32)
    scalars = jnp.stack(
        [x_index, core, length, section_index, mp_index // chips, mp_index, 2 * chips]
    ).astype(jnp.int32)

    def quarters(array):
        array = array[0, 0]
        return array.reshape(4, array.shape[0] // 4, array.shape[1])

    def cut_rows(ref, block, row, sub):
        return ref.at[block, pl.ds(row, sub), :]

    def cut_columns(start):
        def cut(ref, block, row, sub):
            at = pl.multiple_of(block * (width // 4), 128)
            return ref.at[pl.ds(start + row, sub), pl.ds(at, width // 4)]

        return cut

    qkv_sources = (
        ((quarters(query_weight),), (quarters(query_fisher),), width // 4, (256,), cut_rows),
        (
            (quarters(key_weight), quarters(value_weight)),
            (quarters(key_fisher), quarters(value_fisher)),
            width // 4,
            (128, 128),
            cut_rows,
        ),
    )
    out_sources = tuple(
        (
            (output_weight[0, 0],),
            (output_fisher[0, 0],),
            128,
            (width // 4,),
            cut_columns(start),
        )
        for start in (0, 128)
    )

    part_rows = 2 * rows * chips
    positions = (
        part_rows * jnp.arange(parts, dtype=jnp.int32)[:, None, None]
        + 2 * rows * jnp.arange(chips, dtype=jnp.int32)[None, :, None]
        + core * rows
        + jnp.arange(rows, dtype=jnp.int32)[None, None, :]
    ).reshape(parts, -1)
    frequency = 10000.0 ** (-2.0 * jnp.arange(HEAD_DIM // 2, dtype=F32) / HEAD_DIM)
    angles = positions.astype(F32)[:, :, None] * frequency[None, None, :]
    cosine = jnp.cos(angles)
    sine = jnp.sin(angles)

    def spread(array):
        pieces = array.reshape(chips, rows, width)
        moved = lax.all_to_all(pieces, "mp", 0, 0, tiled=True, axis_index_groups=groups)
        return moved.reshape(chips * rows, width)

    straight = [(m, 2 * m) for m in range(chips)]
    straight += [(m, 2 * (m - chips) + 1) for m in range(chips, 2 * chips)]
    crossed = [(m, 2 * m + 1) for m in range(chips)]
    crossed += [(m, 2 * (m - chips)) for m in range(chips, 2 * chips)]

    def over_mp(array, pairs):
        return lax.ppermute(array, "mp", pairs)

    def projected(t, normed):
        queries, kv = project(scalars, t, normed, qkv_own, qkv_peer, cosine, sine)
        return queries, (kv, exchanged(kv, "mp", 1))

    with jax.named_scope("merge"):
        out_sent, out_got = first_halves(plan, scale, out_sources)
        plan, _ = lax.optimization_barrier((plan, out_sent))
        qkv_sent, qkv_got = first_halves(plan, scale, qkv_sources)
        rows_in, rows_target, _ = lax.optimization_barrier(
            (hidden_in[0], layer_targets[0, 0], qkv_sent)
        )
        one, other = dealing(scalars, rows_in, rows_target)
        one, other = over_mp(one, straight), over_mp(other, crossed)
        first, states = entered(scalars, pre_gain, one, other, None, 0, chips)
        first, cosine, sine = lax.optimization_barrier((first, cosine, sine))
        first = spread(first)
        out_got, first = lax.optimization_barrier((out_got, first))
        out_sent, out_more = second_halves(plan, scale, out_sources, out_got)
        qkv_got, _ = lax.optimization_barrier((qkv_got, out_sent))
        qkv_sent, qkv_more = second_halves(plan, scale, qkv_sources, qkv_got)
        qkv_share = shares(plan, scale, qkv_sources, qkv_got, qkv_more)
        qkv_first = neighbours(qkv_share)
        out_more, _ = lax.optimization_barrier((out_more, qkv_share))
        out_share = shares(plan, scale, out_sources, out_got, out_more)
        out_first = neighbours(out_share)
        qkv_own = completed(qkv_share, *qkv_first)
        qkv_peer = of_partner(qkv_own)
    with jax.named_scope("layer"):
        queries, kv = projected(0, first)
    with jax.named_scope("merge"):
        out_first, _ = lax.optimization_barrier((out_first, queries))
        out_own = completed(out_share, *out_first)
        out_peer = of_partner(out_own)

    outs = []
    before = kv
    for t in range(sections + parts - 1):
        with jax.named_scope("layer"):
            if t > 0:
                incoming = lax.ppermute(
                    outs[-1], "section", [(i, i + 1) for i in range(sections - 1)]
                )
                if t < parts:
                    normed, states = entered(scalars, pre_gain, one, other, incoming, t, chips)
                else:
                    normed, states = normed_copies(incoming, pre_gain, chips), incoming
                before = kv
                queries, kv = projected(t, spread(normed))
            partial = attend(scalars, t, queries, (*before, *kv), out_own, out_peer, rows)
            outs.append(finished(spread(partial), states, post_gain))
    with jax.named_scope("loss"):
        kept, moved, error = left(
            scalars, [outs[h : h + sections] for h in range(parts)], one, other
        )
        error = lax.all_to_all(error, "mp", 0, 0, tiled=True)
        kept = over_mp(kept, [(j, i) for i, j in straight])
        moved = over_mp(moved, [(j, i) for i, j in crossed])
        outputs = rejoined(scalars, kept, moved)
        loss = jnp.sum(error[:, 0, 0]) / (length.astype(F32) * width)
    return (outputs[None, None], loss[None, None])


def solution(mesh):
    in_specs = (
        P("task", "mp", None),
        P("task"),
        P("section", "task", "mp", None),
        P(),
        P("section", None, None),
        P("task", "section", None, "mp"),
        P("task", "section", None, "mp"),
        P("task", "section", None, "mp"),
        P("task", "section", "mp", None),
        P("task", "section", None, "mp"),
        P("task", "section", None, "mp"),
        P("task", "section", None, "mp"),
        P("task", "section", "mp", None),
    )
    out_specs = (P("section", "task", "mp", None), P("section", "task"))
    return jax.shard_map(
        per_device, mesh=mesh, in_specs=in_specs, out_specs=out_specs, check_vma=False
    )
```

```python
import functools

import jax
import jax.numpy as jnp
from jax import lax
from jax.experimental import pallas as pl
from jax.experimental.pallas import tpu as pltpu
from jax.sharding import PartitionSpec as P

HEAD_DIM = 256
F32 = jnp.float32
BF16 = jnp.bfloat16
SMEM = pltpu.SMEM
VMEM = pltpu.VMEM
HBM = pltpu.HBM


def exchanged(array, axis, mask):
    return lax.ppermute(array, axis, [(i, i ^ mask) for i in range(lax.axis_size(axis))])


def placed(array, space):
    return pltpu.with_memory_space_constraint(array, space)


def result_on_chip(shape, dtype=BF16):
    return VMEM(shape, dtype)


def kernel_call(kernel, operands, spaces, shapes, scratch=(), mib=16):
    operands = [a if space == SMEM else placed(a, space) for a, space in zip(operands, spaces)]
    outs = pl.pallas_call(
        kernel,
        out_shape=tuple(
            result_on_chip(shape[:-1], F32) if shape[-1] is F32 else result_on_chip(shape)
            for shape in shapes
        ),
        in_specs=[pl.BlockSpec(memory_space=space) for space in spaces],
        out_specs=tuple(pl.BlockSpec(memory_space=VMEM) for _ in shapes),
        scratch_shapes=scratch,
        compiler_params=pltpu.CompilerParams(vmem_limit_bytes=mib * 1024 * 1024),
        cost_estimate=pl.CostEstimate(flops=1, transcendentals=0, bytes_accessed=1),
    )(*operands)
    return outs[0] if len(shapes) == 1 else outs


def share_call(plan, scale, jobs, count, finish):
    rows = jobs[0][0][2]
    total = sum(jobs[0][0][3])
    sub = rows // 2
    parts = count * 2
    strip = 64 if sub % 64 == 0 and sub > 64 else 16
    operands = [plan, scale]
    spaces = [SMEM, SMEM]
    scratch = []
    for (weights, fishers, _, widths, _), _, received in jobs:
        n = len(weights)
        operands += [*weights, *fishers, *(array for array, _ in received)]
        spaces += [HBM] * (2 * n) + [VMEM] * len(received)
        scratch += [VMEM((parts, sub, widths[k % n]), BF16) for k in range(2 * n)]
        scratch.append(pltpu.SemaphoreType.DMA((2 * n, parts)))
    shape = (len(jobs), rows, total) if finish else (2, count, rows, total)

    def kernel(plan_ref, scale_ref, *refs):
        ins = list(refs[: len(operands) - 2])
        out_ref = refs[len(operands) - 2]
        held = list(refs[len(operands) - 1 :])
        task_scale = scale_ref[0]
        work = []
        for job, ((weights, _, _, widths, cut), base, received) in enumerate(jobs):
            n = len(weights)
            arrays = [ins.pop(0) for _ in range(2 * n)]
            gots = [ins.pop(0) for _ in received]
            buffers = [held.pop(0) for _ in range(2 * n)]
            sems = held.pop(0)
            blocks = [0 if entry is None else plan_ref[entry] for _, entry in received]

            def copy(k, part, arrays=arrays, buffers=buffers, sems=sems, base=base, cut=cut):
                return pltpu.make_async_copy(
                    cut(arrays[k], plan_ref[base + part // 2], (part % 2) * sub, sub),
                    buffers[k].at[part],
                    sems.at[k, part],
                )

            for part in range(parts):
                for k in range(2 * n):
                    copy(k, part).start()
            work.append((job, n, widths, copy, buffers, gots, blocks))

        for job, n, widths, copy, buffers, gots, blocks in work:

            def one_strip(part, i):
                inside = pl.ds(pl.multiple_of(i * strip, strip), strip)
                lines = pl.ds(pl.multiple_of((part % 2) * sub + i * strip, strip), strip)
                at = 0
                for k in range(n):
                    scaled = buffers[n + k][part, inside, :].astype(F32) * task_scale
                    term = scaled * buffers[k][part, inside, :].astype(F32)
                    sums = [term.astype(BF16), scaled.astype(BF16)]
                    cols = slice(at, at + widths[k])
                    at += widths[k]
                    for got, block in zip(gots, blocks):
                        sums = [
                            v.astype(F32) + got[i, block, lines, cols].astype(F32)
                            for i, v in enumerate(sums)
                        ]
                    if finish:
                        out_ref[job, lines, cols] = (sums[0] / sums[1]).astype(BF16)
                    else:
                        out_ref[0, part // 2, lines, cols] = sums[0].astype(BF16)
                        out_ref[1, part // 2, lines, cols] = sums[1].astype(BF16)

            def one_part(part, carry):
                for k in range(2 * n):
                    copy(k, part).wait()
                lax.fori_loop(0, sub // strip, lambda i, c: (one_strip(part, i), c)[1], 0)
                return carry

            lax.fori_loop(0, parts, one_part, 0)

    return kernel_call(kernel, operands, spaces, [shape], scratch)


def dealing(idx, hidden, target):
    rows, width = hidden.shape
    half = rows // 2

    def kernel(idx_ref, h_ref, t_ref, straight_ref, crossed_ref):
        last = idx_ref[4] == 1
        for at, ref in ((0, h_ref), (half, t_ref)):
            low = ref[:half, :].astype(F32)
            high = ref[half:, :].astype(F32)
            straight_ref[at : at + half, :] = jnp.where(last, high, low).astype(BF16)
            crossed_ref[at : at + half, :] = jnp.where(last, low, high).astype(BF16)

    return kernel_call(
        kernel, [idx, hidden, target], [SMEM, VMEM, VMEM], [(rows, width), (rows, width)]
    )


def entered(idx, gain, straight, crossed, incoming, part, copies):
    rows, width = straight.shape[0] // 2, straight.shape[1]
    arrays = [straight, crossed] + ([] if incoming is None else [incoming])

    def kernel(idx_ref, gain_ref, s_ref, c_ref, *refs):
        out_ref, states_ref = refs[-2:]
        x = jnp.where(
            idx_ref[1] == part, s_ref[:rows, :].astype(F32), c_ref[:rows, :].astype(F32)
        )
        if incoming is not None:
            x = jnp.where(idx_ref[3] == 0, x, refs[0][...].astype(F32))
        scale = lax.rsqrt(jnp.mean(x * x, axis=-1, keepdims=True) + 1e-06)
        y = (x * scale * gain_ref[...]).astype(BF16)
        for k in range(copies):
            out_ref[k * rows : (k + 1) * rows, :] = y
        states_ref[...] = x.astype(BF16)

    return kernel_call(
        kernel,
        [idx, gain, *arrays],
        [SMEM, VMEM] + [VMEM] * len(arrays),
        [(copies * rows, width), (rows, width)],
    )


def left(idx, outs, straight, crossed):
    rows, width = outs[0][0].shape
    flat = [o for group in outs for o in group]

    def kernel(idx_ref, s_ref, c_ref, *refs):
        keep_ref, cross_ref, loss_ref = refs[-3:]
        core = idx_ref[1]
        length = idx_ref[2]
        section = idx_ref[3]
        mp = idx_ref[5]
        total = None
        chosen = []
        for h, group in enumerate(outs):
            ins = refs[h * len(group) : (h + 1) * len(group)]
            out = ins[0][...].astype(F32)
            for layer in range(1, len(group)):
                out = jnp.where(section == layer, ins[layer][...].astype(F32), out)
            chosen.append(out)
            target = jnp.where(
                core == h, s_ref[rows:, :].astype(F32), c_ref[rows:, :].astype(F32)
            )
            row = lax.broadcasted_iota(jnp.int32, (rows, width), 0)
            live = h * (rows * idx_ref[6]) + mp * rows + row < length
            error = jnp.where(live, (out - target) * (out - target), 0.0)
            error = jnp.sum(jnp.sum(error, axis=1, keepdims=True), axis=0, keepdims=True)
            total = error if total is None else total + error
        keep_ref[...] = jnp.where(core == 0, chosen[0], chosen[1]).astype(BF16)
        cross_ref[...] = jnp.where(core == 0, chosen[1], chosen[0]).astype(BF16)
        loss_ref[...] = jnp.broadcast_to(total[:, :, None], loss_ref.shape)

    return kernel_call(
        kernel,
        [idx, straight, crossed, *flat],
        [SMEM] + [VMEM] * (2 + len(flat)),
        [(rows, width), (rows, width), (16, 1, 128, F32)],
    )


def rejoined(idx, kept, crossed):
    rows, width = kept.shape

    def kernel(idx_ref, k_ref, c_ref, out_ref):
        last = idx_ref[4] == 1
        a = k_ref[...].astype(F32)
        b = c_ref[...].astype(F32)
        out_ref[:rows, :] = jnp.where(last, b, a).astype(BF16)
        out_ref[rows:, :] = jnp.where(last, a, b).astype(BF16)

    return kernel_call(kernel, [idx, kept, crossed], [SMEM, VMEM, VMEM], [(2 * rows, width)])


def weight(refs, d, k):
    own, near, low, high, far = refs
    if d == 2:
        return (low, high)[k][...]
    return (own, near, None, far)[d][k]


def part_of(idx_ref, step):
    return jnp.clip(step - idx_ref[3], 0, 1)


def project(idx, step, normed, own, peer, cosine, sine):
    tokens, width = normed.shape
    quarter = width // 4

    def kernel(idx_ref, x_ref, cos_ref, sin_ref, *refs):
        q_ref, kv_ref = refs[-2:]
        x_index = idx_ref[0]
        core = idx_ref[1]
        part_index = part_of(idx_ref, step)
        sums = [None] * 4
        for d in range(4):
            at = pl.multiple_of((x_index ^ d) * quarter, 128)
            part = x_ref[:, pl.ds(at, quarter)]
            for k in range(4):
                w = weight(refs[5 * (k // 2) : 5 * (k // 2) + 5], d, k % 2)
                prod = jnp.dot(part, w, preferred_element_type=F32)
                sums[k] = prod if d == 0 else sums[k] + prod
        q_mine, mine, q_theirs, theirs = sums
        cos = cos_ref[part_index]
        sin = sin_ref[part_index]
        for at, q in ((0, q_mine), (tokens, q_theirs)):
            a = q[:, :128]
            b = q[:, 128:]
            q_ref[at : at + tokens, :128] = (a * cos - b * sin).astype(BF16)
            q_ref[at : at + tokens, 128:] = (b * cos + a * sin).astype(BF16)
        first = core == 0
        k_mine = mine[:, :128].astype(BF16).astype(F32)
        k_theirs = theirs[:, :128].astype(BF16).astype(F32)
        a = jnp.where(first, k_mine, k_theirs)
        b = jnp.where(first, k_theirs, k_mine)
        kv_ref[:, :128] = (a * cos - b * sin).astype(BF16)
        kv_ref[:, 128:256] = (b * cos + a * sin).astype(BF16)
        kv_ref[:, 256:384] = jnp.where(first, mine[:, 128:], theirs[:, 128:]).astype(BF16)
        kv_ref[:, 384:] = jnp.where(first, theirs[:, 128:], mine[:, 128:]).astype(BF16)

    return kernel_call(
        kernel,
        [idx, normed, cosine, sine, *own, *peer],
        [SMEM] + [VMEM] * 13,
        [(2 * tokens, 256), (tokens, 512)],
    )


def attend(idx, step, queries, blocks, own, peer, rows):
    tokens = queries.shape[0] // 2
    quarter = own[0].shape[2]
    part_rows = 2 * tokens

    def kernel(idx_ref, q_ref, *refs):
        out_ref = refs[-1]
        kv_refs = refs[:4]
        weights = refs[4:-1]
        x_index = idx_ref[0]
        core = idx_ref[1]
        length = idx_ref[2]
        part_index = part_of(idx_ref, step)

        def positions(dim, part, which):
            i = lax.broadcasted_iota(jnp.int32, (2 * tokens, tokens), dim) % tokens
            return part * part_rows + (i // rows) * (2 * rows) + which * rows + i % rows

        q_pos = positions(0, part_index, core)
        q = q_ref[...]
        numerators = []
        total = None
        for n, kv_ref in enumerate(kv_refs):
            k_pos = positions(1, part_index - 1 + n // 2, core if n % 2 == 0 else 1 - core)
            allowed = (k_pos <= q_pos) & (k_pos < length) & (k_pos >= 0)
            scores = lax.dot_general(
                q,
                kv_ref[:, :256],
                (((1,), (1,)), ((), ())),
                preferred_element_type=F32,
            ) * HEAD_DIM ** (-0.5)
            capped = 50.0 * jnp.tanh(scores / 50.0)
            numerators.append(jnp.where(allowed, jnp.exp(capped), 0.0))
            added = jnp.sum(numerators[-1], axis=-1, keepdims=True)
            total = added if total is None else total + added
        context = None
        for num, kv_ref in zip(numerators, kv_refs):
            prod = jnp.dot(
                (num / total).astype(BF16), kv_ref[:, 256:], preferred_element_type=F32
            )
            context = prod if context is None else context + prod
        context = context.astype(BF16)
        lefts = [
            context[c * tokens : (c + 1) * tokens, h * 128 : (h + 1) * 128]
            for c in range(2)
            for h in range(2)
        ]
        for d in range(4):
            out = None
            for k in range(4):
                w = weight(weights[5 * (k // 2) : 5 * (k // 2) + 5], d, k % 2)
                prod = jnp.dot(lefts[k], w, preferred_element_type=F32)
                out = prod if out is None else out + prod
            at = pl.multiple_of((x_index ^ d) * quarter, 128)
            out_ref[:, pl.ds(at, quarter)] = out.astype(BF16)

    return kernel_call(
        kernel,
        [idx, queries, *blocks, *own, *peer],
        [SMEM] + [VMEM] * 15,
        [(tokens, 4 * quarter)],
    )


def normed_copies(states, gain, copies):
    rows, width = states.shape

    def kernel(states_ref, gain_ref, out_ref):
        x = states_ref[...].astype(F32)
        scale = lax.rsqrt(jnp.mean(x * x, axis=-1, keepdims=True) + 1e-06)
        y = (x * scale * gain_ref[...]).astype(BF16)
        for k in range(copies):
            out_ref[k * rows : (k + 1) * rows, :] = y

    return kernel_call(kernel, [states, gain], [VMEM] * 2, [(copies * rows, width)])


def finished(pieces, states, gain):
    rows, width = states.shape
    copies = pieces.shape[0] // rows

    def kernel(p_ref, states_ref, gain_ref, out_ref):
        total = p_ref[:rows, :].astype(F32)
        for k in range(1, copies):
            total = total + p_ref[k * rows : (k + 1) * rows, :].astype(F32)
        scale = lax.rsqrt(jnp.mean(total * total, axis=-1, keepdims=True) + 1e-06)
        out = states_ref[...].astype(F32) + total * scale * gain_ref[...]
        out_ref[...] = out.astype(BF16)

    return kernel_call(kernel, [pieces, states, gain], [VMEM] * 3, [states.shape])


NEAR, FAR = 1, 3


def first_halves(plan, scale, sources):
    sent = [share_call(plan, scale, [(s, 8 * i, ())], 2, False) for i, s in enumerate(sources)]
    return sent, [exchanged(s, "task", (NEAR, FAR)[i]) for i, s in enumerate(sent)]


def second_halves(plan, scale, sources, got):
    sent = [
        share_call(plan, scale, [(s, 8 * i + 2, ((got[i], 8 * i + 3),))], 1, False)
        for i, s in enumerate(sources)
    ]
    return sent, [exchanged(s, "task", (FAR, NEAR)[i]) for i, s in enumerate(sent)]


def shares(plan, scale, sources, got, more):
    jobs = [
        (s, 8 * i + 4, ((got[i], 8 * i + 5), (more[i], None))) for i, s in enumerate(sources)
    ]
    return share_call(plan, scale, jobs, 1, True)


def neighbours(own):
    return exchanged(own, "task", NEAR), exchanged(own, "task", FAR)


def completed(own, near, far):
    return own, near, exchanged(far[0], "task", NEAR), exchanged(near[1], "task", FAR), far


def of_partner(pieces):
    return tuple(exchanged(p, "mp", 1) for p in pieces)


def per_device(
    hidden_in,
    lengths,
    layer_targets,
    task_weights,
    norm_gains,
    query_weight,
    key_weight,
    value_weight,
    output_weight,
    query_fisher,
    key_fisher,
    value_fisher,
    output_fisher,
):
    x_index = lax.axis_index("task")
    mp_index = lax.axis_index("mp")
    section_index = lax.axis_index("section")
    core = mp_index % 2
    chips = lax.axis_size("mp") // 2
    groups = [[2 * z + c for z in range(chips)] for c in range(2)]
    sections = lax.axis_size("section")
    width = hidden_in.shape[2]
    parts = 2
    rows = hidden_in.shape[1] // parts
    length = lengths[0]
    pre_gain = norm_gains[0, 0:1]
    post_gain = norm_gains[0, 1:2]
    scale = lax.dynamic_slice_in_dim(task_weights, x_index, 1)

    b = x_index // 2
    a = (x_index % 2) ^ b

    def block_a(h1, h2):
        return jnp.where(h1 == 0, 3 * h2, 1 + h2)

    def block_b(h1, h2):
        return jnp.where(h1 == 0, h2, 3 - h2)

    zero = jnp.zeros_like(a)
    plan = jnp.stack(
        [
            block_a(1 - a, 0),
            block_a(1 - a, 1),
            block_a(a, 1 - b),
            1 - b,
            x_index,
            b,
            zero,
            zero,
            block_b(1 - b, 0),
            block_b(1 - b, 1),
            block_b(b, 1 - a),
            1 - a,
            x_index,
            a,
            zero,
            zero,
        ]
    ).astype(jnp.int32)
    scalars = jnp.stack(
        [x_index, core, length, section_index, mp_index // chips, mp_index, 2 * chips]
    ).astype(jnp.int32)

    def quarters(array):
        array = array[0, 0]
        return array.reshape(4, array.shape[0] // 4, array.shape[1])

    def cut_rows(ref, block, row, sub):
        return ref.at[block, pl.ds(row, sub), :]

    def cut_columns(start):
        def cut(ref, block, row, sub):
            at = pl.multiple_of(block * (width // 4), 128)
            return ref.at[pl.ds(start + row, sub), pl.ds(at, width // 4)]

        return cut

    qkv_sources = (
        ((quarters(query_weight),), (quarters(query_fisher),), width // 4, (256,), cut_rows),
        (
            (quarters(key_weight), quarters(value_weight)),
            (quarters(key_fisher), quarters(value_fisher)),
            width // 4,
            (128, 128),
            cut_rows,
        ),
    )
    out_sources = tuple(
        (
            (output_weight[0, 0],),
            (output_fisher[0, 0],),
            128,
            (width // 4,),
            cut_columns(start),
        )
        for start in (0, 128)
    )

    part_rows = 2 * rows * chips
    positions = (
        part_rows * jnp.arange(parts, dtype=jnp.int32)[:, None, None]
        + 2 * rows * jnp.arange(chips, dtype=jnp.int32)[None, :, None]
        + core * rows
        + jnp.arange(rows, dtype=jnp.int32)[None, None, :]
    ).reshape(parts, -1)
    frequency = 10000.0 ** (-2.0 * jnp.arange(HEAD_DIM // 2, dtype=F32) / HEAD_DIM)
    angles = positions.astype(F32)[:, :, None] * frequency[None, None, :]
    cosine = jnp.cos(angles)
    sine = jnp.sin(angles)

    def spread(array):
        pieces = array.reshape(chips, rows, width)
        moved = lax.all_to_all(pieces, "mp", 0, 0, tiled=True, axis_index_groups=groups)
        return moved.reshape(chips * rows, width)

    straight = [(m, 2 * m) for m in range(chips)]
    straight += [(m, 2 * (m - chips) + 1) for m in range(chips, 2 * chips)]
    crossed = [(m, 2 * m + 1) for m in range(chips)]
    crossed += [(m, 2 * (m - chips)) for m in range(chips, 2 * chips)]

    def over_mp(array, pairs):
        return lax.ppermute(array, "mp", pairs)

    def projected(t, normed):
        queries, kv = project(scalars, t, normed, qkv_own, qkv_peer, cosine, sine)
        return queries, (kv, exchanged(kv, "mp", 1))

    with jax.named_scope("merge"):
        out_sent, out_got = first_halves(plan, scale, out_sources)
        plan, _ = lax.optimization_barrier((plan, out_sent))
        qkv_sent, qkv_got = first_halves(plan, scale, qkv_sources)
        rows_in, rows_target, _ = lax.optimization_barrier(
            (hidden_in[0], layer_targets[0, 0], qkv_sent)
        )
        one, other = dealing(scalars, rows_in, rows_target)
        one, other = over_mp(one, straight), over_mp(other, crossed)
        first, states = entered(scalars, pre_gain, one, other, None, 0, chips)
        first, cosine, sine = lax.optimization_barrier((first, cosine, sine))
        first = spread(first)
        out_got, first = lax.optimization_barrier((out_got, first))
        out_sent, out_more = second_halves(plan, scale, out_sources, out_got)
        qkv_got, _ = lax.optimization_barrier((qkv_got, out_sent))
        qkv_sent, qkv_more = second_halves(plan, scale, qkv_sources, qkv_got)
        out_more, _ = lax.optimization_barrier((out_more, qkv_sent))
        out_share = shares(plan, scale, out_sources, out_got, out_more)
        out_first = neighbours(out_share)
        qkv_more, _ = lax.optimization_barrier((qkv_more, out_share))
        qkv_share = shares(plan, scale, qkv_sources, qkv_got, qkv_more)
        qkv_first = neighbours(qkv_share)
        out_first, _ = lax.optimization_barrier((out_first, qkv_share))
        out_own = completed(out_share, *out_first)
        out_peer = of_partner(out_own)
        share, near, low, high, far = completed(qkv_share, *qkv_first)
        low, high, _ = lax.optimization_barrier((low, high, out_peer))
        qkv_own = (share, near, low, high, far)
        qkv_peer = of_partner(qkv_own)
    with jax.named_scope("layer"):
        queries, kv = projected(0, first)
    outs = []
    before = kv
    for t in range(sections + parts - 1):
        with jax.named_scope("layer"):
            if t > 0:
                incoming = lax.ppermute(
                    outs[-1], "section", [(i, i + 1) for i in range(sections - 1)]
                )
                if t < parts:
                    normed, states = entered(scalars, pre_gain, one, other, incoming, t, chips)
                else:
                    normed, states = normed_copies(incoming, pre_gain, chips), incoming
                before = kv
                queries, kv = projected(t, spread(normed))
            partial = attend(scalars, t, queries, (*before, *kv), out_own, out_peer, rows)
            outs.append(finished(spread(partial), states, post_gain))
    with jax.named_scope("loss"):
        kept, moved, error = left(
            scalars, [outs[h : h + sections] for h in range(parts)], one, other
        )
        error = lax.all_to_all(error, "mp", 0, 0, tiled=True)
        kept = over_mp(kept, [(j, i) for i, j in straight])
        moved = over_mp(moved, [(j, i) for i, j in crossed])
        outputs = rejoined(scalars, kept, moved)
        loss = jnp.sum(error[:, 0, 0]) / (length.astype(F32) * width)
    return (outputs[None, None], loss[None, None])


def solution(mesh):
    in_specs = (
        P("task", "mp", None),
        P("task"),
        P("section", "task", "mp", None),
        P(),
        P("section", None, None),
        P("task", "section", None, "mp"),
        P("task", "section", None, "mp"),
        P("task", "section", None, "mp"),
        P("task", "section", "mp", None),
        P("task", "section", None, "mp"),
        P("task", "section", None, "mp"),
        P("task", "section", None, "mp"),
        P("task", "section", "mp", None),
    )
    out_specs = (P("section", "task", "mp", None), P("section", "task"))
    return jax.shard_map(
        per_device, mesh=mesh, in_specs=in_specs, out_specs=out_specs, check_vma=False
    )
```

```python
import functools

import jax
import jax.numpy as jnp
from jax import lax
from jax.experimental import pallas as pl
from jax.experimental.pallas import tpu as pltpu
from jax.sharding import PartitionSpec as P

HEAD_DIM = 256
F32 = jnp.float32
BF16 = jnp.bfloat16
SMEM = pltpu.SMEM
VMEM = pltpu.VMEM
HBM = pltpu.HBM


def exchanged(array, axis, mask):
    return lax.ppermute(array, axis, [(i, i ^ mask) for i in range(lax.axis_size(axis))])


def placed(array, space):
    return pltpu.with_memory_space_constraint(array, space)


def result_on_chip(shape, dtype=BF16):
    return VMEM(shape, dtype)


def kernel_call(kernel, operands, spaces, shapes, scratch=(), mib=16):
    operands = [a if space == SMEM else placed(a, space) for a, space in zip(operands, spaces)]
    outs = pl.pallas_call(
        kernel,
        out_shape=tuple(
            result_on_chip(shape[:-1], F32) if shape[-1] is F32 else result_on_chip(shape)
            for shape in shapes
        ),
        in_specs=[pl.BlockSpec(memory_space=space) for space in spaces],
        out_specs=tuple(pl.BlockSpec(memory_space=VMEM) for _ in shapes),
        scratch_shapes=scratch,
        compiler_params=pltpu.CompilerParams(vmem_limit_bytes=mib * 1024 * 1024),
        cost_estimate=pl.CostEstimate(flops=1, transcendentals=0, bytes_accessed=1),
    )(*operands)
    return outs[0] if len(shapes) == 1 else outs


def share_call(plan, scale, jobs, count, finish):
    rows = jobs[0][0][2]
    total = sum(jobs[0][0][3])
    sub = rows // 2
    parts = count * 2
    strip = 64 if sub % 64 == 0 and sub > 64 else 16
    operands = [plan, scale]
    spaces = [SMEM, SMEM]
    scratch = []
    for (weights, fishers, _, widths, _), _, received in jobs:
        n = len(weights)
        operands += [*weights, *fishers, *(array for array, _ in received)]
        spaces += [HBM] * (2 * n) + [VMEM] * len(received)
        scratch += [VMEM((parts, sub, widths[k % n]), BF16) for k in range(2 * n)]
        scratch.append(pltpu.SemaphoreType.DMA((2 * n, parts)))
    shape = (len(jobs), rows, total) if finish else (2, count, rows, total)

    def kernel(plan_ref, scale_ref, *refs):
        ins = list(refs[: len(operands) - 2])
        out_ref = refs[len(operands) - 2]
        held = list(refs[len(operands) - 1 :])
        task_scale = scale_ref[0]
        work = []
        for job, ((weights, _, _, widths, cut), base, received) in enumerate(jobs):
            n = len(weights)
            arrays = [ins.pop(0) for _ in range(2 * n)]
            gots = [ins.pop(0) for _ in received]
            buffers = [held.pop(0) for _ in range(2 * n)]
            sems = held.pop(0)
            blocks = [0 if entry is None else plan_ref[entry] for _, entry in received]

            def copy(k, part, arrays=arrays, buffers=buffers, sems=sems, base=base, cut=cut):
                return pltpu.make_async_copy(
                    cut(arrays[k], plan_ref[base + part // 2], (part % 2) * sub, sub),
                    buffers[k].at[part],
                    sems.at[k, part],
                )

            for part in range(parts):
                for k in range(2 * n):
                    copy(k, part).start()
            work.append((job, n, widths, copy, buffers, gots, blocks))

        for job, n, widths, copy, buffers, gots, blocks in work:

            def one_strip(part, i):
                inside = pl.ds(pl.multiple_of(i * strip, strip), strip)
                lines = pl.ds(pl.multiple_of((part % 2) * sub + i * strip, strip), strip)
                at = 0
                for k in range(n):
                    scaled = buffers[n + k][part, inside, :].astype(F32) * task_scale
                    term = scaled * buffers[k][part, inside, :].astype(F32)
                    sums = [term.astype(BF16), scaled.astype(BF16)]
                    cols = slice(at, at + widths[k])
                    at += widths[k]
                    for got, block in zip(gots, blocks):
                        sums = [
                            v.astype(F32) + got[i, block, lines, cols].astype(F32)
                            for i, v in enumerate(sums)
                        ]
                    if finish:
                        out_ref[job, lines, cols] = (sums[0] / sums[1]).astype(BF16)
                    else:
                        out_ref[0, part // 2, lines, cols] = sums[0].astype(BF16)
                        out_ref[1, part // 2, lines, cols] = sums[1].astype(BF16)

            def one_part(part, carry):
                for k in range(2 * n):
                    copy(k, part).wait()
                lax.fori_loop(0, sub // strip, lambda i, c: (one_strip(part, i), c)[1], 0)
                return carry

            lax.fori_loop(0, parts, one_part, 0)

    return kernel_call(kernel, operands, spaces, [shape], scratch)


def dealing(idx, hidden, target):
    rows, width = hidden.shape
    half = rows // 2

    def kernel(idx_ref, h_ref, t_ref, straight_ref, crossed_ref):
        last = idx_ref[4] == 1
        for at, ref in ((0, h_ref), (half, t_ref)):
            low = ref[:half, :].astype(F32)
            high = ref[half:, :].astype(F32)
            straight_ref[at : at + half, :] = jnp.where(last, high, low).astype(BF16)
            crossed_ref[at : at + half, :] = jnp.where(last, low, high).astype(BF16)

    return kernel_call(
        kernel, [idx, hidden, target], [SMEM, VMEM, VMEM], [(rows, width), (rows, width)]
    )


def entered(idx, gain, straight, crossed, incoming, part, copies):
    rows, width = straight.shape[0] // 2, straight.shape[1]
    arrays = [straight, crossed] + ([] if incoming is None else [incoming])

    def kernel(idx_ref, gain_ref, s_ref, c_ref, *refs):
        out_ref, states_ref = refs[-2:]
        x = jnp.where(
            idx_ref[1] == part, s_ref[:rows, :].astype(F32), c_ref[:rows, :].astype(F32)
        )
        if incoming is not None:
            x = jnp.where(idx_ref[3] == 0, x, refs[0][...].astype(F32))
        scale = lax.rsqrt(jnp.mean(x * x, axis=-1, keepdims=True) + 1e-06)
        y = (x * scale * gain_ref[...]).astype(BF16)
        for k in range(copies):
            out_ref[k * rows : (k + 1) * rows, :] = y
        states_ref[...] = x.astype(BF16)

    return kernel_call(
        kernel,
        [idx, gain, *arrays],
        [SMEM, VMEM] + [VMEM] * len(arrays),
        [(copies * rows, width), (rows, width)],
    )


def left(idx, outs, straight, crossed):
    rows, width = outs[0][0].shape
    flat = [o for group in outs for o in group]

    def kernel(idx_ref, s_ref, c_ref, *refs):
        keep_ref, cross_ref, loss_ref = refs[-3:]
        core = idx_ref[1]
        length = idx_ref[2]
        section = idx_ref[3]
        mp = idx_ref[5]
        total = None
        chosen = []
        for h, group in enumerate(outs):
            ins = refs[h * len(group) : (h + 1) * len(group)]
            out = ins[0][...].astype(F32)
            for layer in range(1, len(group)):
                out = jnp.where(section == layer, ins[layer][...].astype(F32), out)
            chosen.append(out)
            target = jnp.where(
                core == h, s_ref[rows:, :].astype(F32), c_ref[rows:, :].astype(F32)
            )
            row = lax.broadcasted_iota(jnp.int32, (rows, width), 0)
            live = h * (rows * idx_ref[6]) + mp * rows + row < length
            error = jnp.where(live, (out - target) * (out - target), 0.0)
            error = jnp.sum(jnp.sum(error, axis=1, keepdims=True), axis=0, keepdims=True)
            total = error if total is None else total + error
        keep_ref[...] = jnp.where(core == 0, chosen[0], chosen[1]).astype(BF16)
        cross_ref[...] = jnp.where(core == 0, chosen[1], chosen[0]).astype(BF16)
        loss_ref[...] = jnp.broadcast_to(total[:, :, None], loss_ref.shape)

    return kernel_call(
        kernel,
        [idx, straight, crossed, *flat],
        [SMEM] + [VMEM] * (2 + len(flat)),
        [(rows, width), (rows, width), (16, 1, 128, F32)],
    )


def rejoined(idx, kept, crossed):
    rows, width = kept.shape

    def kernel(idx_ref, k_ref, c_ref, out_ref):
        last = idx_ref[4] == 1
        a = k_ref[...].astype(F32)
        b = c_ref[...].astype(F32)
        out_ref[:rows, :] = jnp.where(last, b, a).astype(BF16)
        out_ref[rows:, :] = jnp.where(last, a, b).astype(BF16)

    return kernel_call(kernel, [idx, kept, crossed], [SMEM, VMEM, VMEM], [(2 * rows, width)])


def weight(refs, d, k):
    own, near, low, high, far = refs
    if d == 2:
        return (low, high)[k][...]
    return (own, near, None, far)[d][k]


def part_of(idx_ref, step):
    return jnp.clip(step - idx_ref[3], 0, 1)


def project(idx, step, normed, own, peer, cosine, sine):
    tokens, width = normed.shape
    quarter = width // 4

    def kernel(idx_ref, x_ref, cos_ref, sin_ref, *refs):
        q_ref, kv_ref = refs[-2:]
        x_index = idx_ref[0]
        core = idx_ref[1]
        part_index = part_of(idx_ref, step)
        sums = [None] * 4
        for d in range(4):
            at = pl.multiple_of((x_index ^ d) * quarter, 128)
            part = x_ref[:, pl.ds(at, quarter)]
            for k in range(4):
                w = weight(refs[5 * (k // 2) : 5 * (k // 2) + 5], d, k % 2)
                prod = jnp.dot(part, w, preferred_element_type=F32)
                sums[k] = prod if d == 0 else sums[k] + prod
        q_mine, mine, q_theirs, theirs = sums
        cos = cos_ref[part_index]
        sin = sin_ref[part_index]
        for at, q in ((0, q_mine), (tokens, q_theirs)):
            a = q[:, :128]
            b = q[:, 128:]
            q_ref[at : at + tokens, :128] = (a * cos - b * sin).astype(BF16)
            q_ref[at : at + tokens, 128:] = (b * cos + a * sin).astype(BF16)
        first = core == 0
        k_mine = mine[:, :128].astype(BF16).astype(F32)
        k_theirs = theirs[:, :128].astype(BF16).astype(F32)
        a = jnp.where(first, k_mine, k_theirs)
        b = jnp.where(first, k_theirs, k_mine)
        kv_ref[:, :128] = (a * cos - b * sin).astype(BF16)
        kv_ref[:, 128:256] = (b * cos + a * sin).astype(BF16)
        kv_ref[:, 256:384] = jnp.where(first, mine[:, 128:], theirs[:, 128:]).astype(BF16)
        kv_ref[:, 384:] = jnp.where(first, theirs[:, 128:], mine[:, 128:]).astype(BF16)

    return kernel_call(
        kernel,
        [idx, normed, cosine, sine, *own, *peer],
        [SMEM] + [VMEM] * 13,
        [(2 * tokens, 256), (tokens, 512)],
    )


def attend(idx, step, queries, blocks, own, peer, rows):
    tokens = queries.shape[0] // 2
    quarter = own[0].shape[2]
    part_rows = 2 * tokens

    def kernel(idx_ref, q_ref, *refs):
        out_ref = refs[-1]
        kv_refs = refs[:4]
        weights = refs[4:-1]
        x_index = idx_ref[0]
        core = idx_ref[1]
        length = idx_ref[2]
        part_index = part_of(idx_ref, step)

        def positions(dim, part, which):
            i = lax.broadcasted_iota(jnp.int32, (2 * tokens, tokens), dim) % tokens
            return part * part_rows + (i // rows) * (2 * rows) + which * rows + i % rows

        q_pos = positions(0, part_index, core)
        q = q_ref[...]
        numerators = []
        total = None
        for n, kv_ref in enumerate(kv_refs):
            k_pos = positions(1, part_index - 1 + n // 2, core if n % 2 == 0 else 1 - core)
            allowed = (k_pos <= q_pos) & (k_pos < length) & (k_pos >= 0)
            scores = lax.dot_general(
                q,
                kv_ref[:, :256],
                (((1,), (1,)), ((), ())),
                preferred_element_type=F32,
            ) * HEAD_DIM ** (-0.5)
            capped = 50.0 * jnp.tanh(scores / 50.0)
            numerators.append(jnp.where(allowed, jnp.exp(capped), 0.0))
            added = jnp.sum(numerators[-1], axis=-1, keepdims=True)
            total = added if total is None else total + added
        context = None
        for num, kv_ref in zip(numerators, kv_refs):
            prod = jnp.dot(
                (num / total).astype(BF16), kv_ref[:, 256:], preferred_element_type=F32
            )
            context = prod if context is None else context + prod
        context = context.astype(BF16)
        lefts = [
            context[c * tokens : (c + 1) * tokens, h * 128 : (h + 1) * 128]
            for c in range(2)
            for h in range(2)
        ]
        for d in range(4):
            out = None
            for k in range(4):
                w = weight(weights[5 * (k // 2) : 5 * (k // 2) + 5], d, k % 2)
                prod = jnp.dot(lefts[k], w, preferred_element_type=F32)
                out = prod if out is None else out + prod
            at = pl.multiple_of((x_index ^ d) * quarter, 128)
            out_ref[:, pl.ds(at, quarter)] = out.astype(BF16)

    return kernel_call(
        kernel,
        [idx, queries, *blocks, *own, *peer],
        [SMEM] + [VMEM] * 15,
        [(tokens, 4 * quarter)],
    )


def normed_copies(states, gain, copies):
    rows, width = states.shape

    def kernel(states_ref, gain_ref, out_ref):
        x = states_ref[...].astype(F32)
        scale = lax.rsqrt(jnp.mean(x * x, axis=-1, keepdims=True) + 1e-06)
        y = (x * scale * gain_ref[...]).astype(BF16)
        for k in range(copies):
            out_ref[k * rows : (k + 1) * rows, :] = y

    return kernel_call(kernel, [states, gain], [VMEM] * 2, [(copies * rows, width)])


def finished(pieces, states, gain):
    rows, width = states.shape
    copies = pieces.shape[0] // rows

    def kernel(p_ref, states_ref, gain_ref, out_ref):
        total = p_ref[:rows, :].astype(F32)
        for k in range(1, copies):
            total = total + p_ref[k * rows : (k + 1) * rows, :].astype(F32)
        scale = lax.rsqrt(jnp.mean(total * total, axis=-1, keepdims=True) + 1e-06)
        out = states_ref[...].astype(F32) + total * scale * gain_ref[...]
        out_ref[...] = out.astype(BF16)

    return kernel_call(kernel, [pieces, states, gain], [VMEM] * 3, [states.shape])


NEAR, FAR = 1, 3


def first_halves(plan, scale, sources):
    sent = [share_call(plan, scale, [(s, 8 * i, ())], 2, False) for i, s in enumerate(sources)]
    return sent, [exchanged(s, "task", (NEAR, FAR)[i]) for i, s in enumerate(sent)]


def second_halves(plan, scale, sources, got):
    sent = []
    for i, s in enumerate(sources):
        mine = got[i]
        if sent:
            mine, _ = lax.optimization_barrier((mine, sent[0]))
        sent.append(share_call(plan, scale, [(s, 8 * i + 2, ((mine, 8 * i + 3),))], 1, False))
    return sent, [exchanged(s, "task", (FAR, NEAR)[i]) for i, s in enumerate(sent)]


def shares(plan, scale, sources, got, more):
    jobs = [
        (s, 8 * i + 4, ((got[i], 8 * i + 5), (more[i], None))) for i, s in enumerate(sources)
    ]
    return share_call(plan, scale, jobs, 1, True)


def neighbours(own):
    return exchanged(own, "task", NEAR), exchanged(own, "task", FAR)


def completed(own, near, far):
    return own, near, exchanged(far[0], "task", NEAR), exchanged(near[1], "task", FAR), far


def of_partner(pieces):
    return tuple(exchanged(p, "mp", 1) for p in pieces)


def per_device(
    hidden_in,
    lengths,
    layer_targets,
    task_weights,
    norm_gains,
    query_weight,
    key_weight,
    value_weight,
    output_weight,
    query_fisher,
    key_fisher,
    value_fisher,
    output_fisher,
):
    x_index = lax.axis_index("task")
    mp_index = lax.axis_index("mp")
    section_index = lax.axis_index("section")
    core = mp_index % 2
    chips = lax.axis_size("mp") // 2
    groups = [[2 * z + c for z in range(chips)] for c in range(2)]
    sections = lax.axis_size("section")
    width = hidden_in.shape[2]
    parts = 2
    rows = hidden_in.shape[1] // parts
    length = lengths[0]
    pre_gain = norm_gains[0, 0:1]
    post_gain = norm_gains[0, 1:2]
    scale = lax.dynamic_slice_in_dim(task_weights, x_index, 1)

    b = x_index // 2
    a = (x_index % 2) ^ b

    def block_a(h1, h2):
        return jnp.where(h1 == 0, 3 * h2, 1 + h2)

    def block_b(h1, h2):
        return jnp.where(h1 == 0, h2, 3 - h2)

    zero = jnp.zeros_like(a)
    plan = jnp.stack(
        [
            block_a(1 - a, 0),
            block_a(1 - a, 1),
            block_a(a, 1 - b),
            1 - b,
            x_index,
            b,
            zero,
            zero,
            block_b(1 - b, 0),
            block_b(1 - b, 1),
            block_b(b, 1 - a),
            1 - a,
            x_index,
            a,
            zero,
            zero,
        ]
    ).astype(jnp.int32)
    scalars = jnp.stack(
        [x_index, core, length, section_index, mp_index // chips, mp_index, 2 * chips]
    ).astype(jnp.int32)

    def quarters(array):
        array = array[0, 0]
        return array.reshape(4, array.shape[0] // 4, array.shape[1])

    def cut_rows(ref, block, row, sub):
        return ref.at[block, pl.ds(row, sub), :]

    def cut_columns(start):
        def cut(ref, block, row, sub):
            at = pl.multiple_of(block * (width // 4), 128)
            return ref.at[pl.ds(start + row, sub), pl.ds(at, width // 4)]

        return cut

    qkv_sources = (
        ((quarters(query_weight),), (quarters(query_fisher),), width // 4, (256,), cut_rows),
        (
            (quarters(key_weight), quarters(value_weight)),
            (quarters(key_fisher), quarters(value_fisher)),
            width // 4,
            (128, 128),
            cut_rows,
        ),
    )
    out_sources = tuple(
        (
            (output_weight[0, 0],),
            (output_fisher[0, 0],),
            128,
            (width // 4,),
            cut_columns(start),
        )
        for start in (0, 128)
    )

    part_rows = 2 * rows * chips
    positions = (
        part_rows * jnp.arange(parts, dtype=jnp.int32)[:, None, None]
        + 2 * rows * jnp.arange(chips, dtype=jnp.int32)[None, :, None]
        + core * rows
        + jnp.arange(rows, dtype=jnp.int32)[None, None, :]
    ).reshape(parts, -1)
    frequency = 10000.0 ** (-2.0 * jnp.arange(HEAD_DIM // 2, dtype=F32) / HEAD_DIM)
    angles = positions.astype(F32)[:, :, None] * frequency[None, None, :]
    cosine = jnp.cos(angles)
    sine = jnp.sin(angles)

    def spread(array):
        pieces = array.reshape(chips, rows, width)
        moved = lax.all_to_all(pieces, "mp", 0, 0, tiled=True, axis_index_groups=groups)
        return moved.reshape(chips * rows, width)

    straight = [(m, 2 * m) for m in range(chips)]
    straight += [(m, 2 * (m - chips) + 1) for m in range(chips, 2 * chips)]
    crossed = [(m, 2 * m + 1) for m in range(chips)]
    crossed += [(m, 2 * (m - chips)) for m in range(chips, 2 * chips)]

    def over_mp(array, pairs):
        return lax.ppermute(array, "mp", pairs)

    def projected(t, normed):
        queries, kv = project(scalars, t, normed, qkv_own, qkv_peer, cosine, sine)
        return queries, (kv, exchanged(kv, "mp", 1))

    with jax.named_scope("merge"):
        out_sent, out_got = first_halves(plan, scale, out_sources)
        plan, _ = lax.optimization_barrier((plan, out_sent))
        qkv_sent, qkv_got = first_halves(plan, scale, qkv_sources)
        rows_in, rows_target, _ = lax.optimization_barrier(
            (hidden_in[0], layer_targets[0, 0], qkv_sent)
        )
        one, other = dealing(scalars, rows_in, rows_target)
        one, other = over_mp(one, straight), over_mp(other, crossed)
        first, states = entered(scalars, pre_gain, one, other, None, 0, chips)
        first, cosine, sine = lax.optimization_barrier((first, cosine, sine))
        first = spread(first)
        out_got, first = lax.optimization_barrier((out_got, first))
        out_sent, out_more = second_halves(plan, scale, out_sources, out_got)
        qkv_got, _ = lax.optimization_barrier((qkv_got, out_sent))
        qkv_sent, qkv_more = second_halves(plan, scale, qkv_sources, qkv_got)
        qkv_more, out_more = lax.optimization_barrier((qkv_more, out_more))
        qkv_share = shares(plan, scale, qkv_sources, qkv_got, qkv_more)
        qkv_first = neighbours(qkv_share)
        out_more, _ = lax.optimization_barrier((out_more, qkv_share))
        out_share = shares(plan, scale, out_sources, out_got, out_more)
        out_first = neighbours(out_share)
        share, near, low, high, far = completed(qkv_share, *qkv_first)
        out_first, low, high = lax.optimization_barrier((out_first, low, high))
        qkv_own = (share, near, low, high, far)
        qkv_peer = of_partner(qkv_own)
        out_own = completed(out_share, *out_first)
        out_peer = of_partner(out_own)
    with jax.named_scope("layer"):
        queries, kv = projected(0, first)
    outs = []
    before = kv
    for t in range(sections + parts - 1):
        with jax.named_scope("layer"):
            if t > 0:
                incoming = lax.ppermute(
                    outs[-1], "section", [(i, i + 1) for i in range(sections - 1)]
                )
                if t < parts:
                    normed, states = entered(scalars, pre_gain, one, other, incoming, t, chips)
                else:
                    normed, states = normed_copies(incoming, pre_gain, chips), incoming
                before = kv
                queries, kv = projected(t, spread(normed))
            partial = attend(scalars, t, queries, (*before, *kv), out_own, out_peer, rows)
            outs.append(finished(spread(partial), states, post_gain))
    with jax.named_scope("loss"):
        kept, moved, error = left(
            scalars, [outs[h : h + sections] for h in range(parts)], one, other
        )
        error = lax.all_to_all(error, "mp", 0, 0, tiled=True)
        kept = over_mp(kept, [(j, i) for i, j in straight])
        moved = over_mp(moved, [(j, i) for i, j in crossed])
        outputs = rejoined(scalars, kept, moved)
        loss = jnp.sum(error[:, 0, 0]) / (length.astype(F32) * width)
    return (outputs[None, None], loss[None, None])


def solution(mesh):
    in_specs = (
        P("task", "mp", None),
        P("task"),
        P("section", "task", "mp", None),
        P(),
        P("section", None, None),
        P("task", "section", None, "mp"),
        P("task", "section", None, "mp"),
        P("task", "section", None, "mp"),
        P("task", "section", "mp", None),
        P("task", "section", None, "mp"),
        P("task", "section", None, "mp"),
        P("task", "section", None, "mp"),
        P("task", "section", "mp", None),
    )
    out_specs = (P("section", "task", "mp", None), P("section", "task"))
    return jax.shard_map(
        per_device, mesh=mesh, in_specs=in_specs, out_specs=out_specs, check_vma=False
    )
```

```python
import functools

import jax
import jax.numpy as jnp
from jax import lax
from jax.experimental import pallas as pl
from jax.experimental.pallas import tpu as pltpu
from jax.sharding import PartitionSpec as P

HEAD_DIM = 256
F32 = jnp.float32
BF16 = jnp.bfloat16
SMEM = pltpu.SMEM
VMEM = pltpu.VMEM
HBM = pltpu.HBM


def exchanged(array, axis, mask):
    return lax.ppermute(array, axis, [(i, i ^ mask) for i in range(lax.axis_size(axis))])


def placed(array, space):
    return pltpu.with_memory_space_constraint(array, space)


def result_on_chip(shape, dtype=BF16):
    return VMEM(shape, dtype)


def kernel_call(kernel, operands, spaces, shapes, scratch=(), mib=16):
    operands = [a if space == SMEM else placed(a, space) for a, space in zip(operands, spaces)]
    outs = pl.pallas_call(
        kernel,
        out_shape=tuple(
            result_on_chip(shape[:-1], F32) if shape[-1] is F32 else result_on_chip(shape)
            for shape in shapes
        ),
        in_specs=[pl.BlockSpec(memory_space=space) for space in spaces],
        out_specs=tuple(pl.BlockSpec(memory_space=VMEM) for _ in shapes),
        scratch_shapes=scratch,
        compiler_params=pltpu.CompilerParams(vmem_limit_bytes=mib * 1024 * 1024),
        cost_estimate=pl.CostEstimate(flops=1, transcendentals=0, bytes_accessed=1),
    )(*operands)
    return outs[0] if len(shapes) == 1 else outs


def share_call(plan, scale, jobs, count, finish):
    rows = jobs[0][0][2]
    total = sum(jobs[0][0][3])
    sub = rows // 2
    parts = count * 2
    strip = 64 if sub % 64 == 0 and sub > 64 else 16
    operands = [plan, scale]
    spaces = [SMEM, SMEM]
    scratch = []
    for (weights, fishers, _, widths, _), _, received in jobs:
        n = len(weights)
        operands += [*weights, *fishers, *(array for array, _ in received)]
        spaces += [HBM] * (2 * n) + [VMEM] * len(received)
        scratch += [VMEM((parts, sub, widths[k % n]), BF16) for k in range(2 * n)]
        scratch.append(pltpu.SemaphoreType.DMA((2 * n, parts)))
    shape = (len(jobs), rows, total) if finish else (2, count, rows, total)

    def kernel(plan_ref, scale_ref, *refs):
        ins = list(refs[: len(operands) - 2])
        out_ref = refs[len(operands) - 2]
        held = list(refs[len(operands) - 1 :])
        task_scale = scale_ref[0]
        work = []
        for job, ((weights, _, _, widths, cut), base, received) in enumerate(jobs):
            n = len(weights)
            arrays = [ins.pop(0) for _ in range(2 * n)]
            gots = [ins.pop(0) for _ in received]
            buffers = [held.pop(0) for _ in range(2 * n)]
            sems = held.pop(0)
            blocks = [0 if entry is None else plan_ref[entry] for _, entry in received]

            def copy(k, part, arrays=arrays, buffers=buffers, sems=sems, base=base, cut=cut):
                return pltpu.make_async_copy(
                    cut(arrays[k], plan_ref[base + part // 2], (part % 2) * sub, sub),
                    buffers[k].at[part],
                    sems.at[k, part],
                )

            for part in range(parts):
                for k in range(2 * n):
                    copy(k, part).start()
            work.append((job, n, widths, copy, buffers, gots, blocks))

        for job, n, widths, copy, buffers, gots, blocks in work:

            def one_strip(part, i):
                inside = pl.ds(pl.multiple_of(i * strip, strip), strip)
                lines = pl.ds(pl.multiple_of((part % 2) * sub + i * strip, strip), strip)
                at = 0
                for k in range(n):
                    scaled = buffers[n + k][part, inside, :].astype(F32) * task_scale
                    term = scaled * buffers[k][part, inside, :].astype(F32)
                    sums = [term.astype(BF16), scaled.astype(BF16)]
                    cols = slice(at, at + widths[k])
                    at += widths[k]
                    for got, block in zip(gots, blocks):
                        sums = [
                            v.astype(F32) + got[i, block, lines, cols].astype(F32)
                            for i, v in enumerate(sums)
                        ]
                    if finish:
                        out_ref[job, lines, cols] = (sums[0] / sums[1]).astype(BF16)
                    else:
                        out_ref[0, part // 2, lines, cols] = sums[0].astype(BF16)
                        out_ref[1, part // 2, lines, cols] = sums[1].astype(BF16)

            def one_part(part, carry):
                for k in range(2 * n):
                    copy(k, part).wait()
                lax.fori_loop(0, sub // strip, lambda i, c: (one_strip(part, i), c)[1], 0)
                return carry

            lax.fori_loop(0, parts, one_part, 0)

    return kernel_call(kernel, operands, spaces, [shape], scratch)


def dealing(idx, hidden, target):
    rows, width = hidden.shape
    half = rows // 2

    def kernel(idx_ref, h_ref, t_ref, straight_ref, crossed_ref):
        last = idx_ref[4] == 1
        for at, ref in ((0, h_ref), (half, t_ref)):
            low = ref[:half, :].astype(F32)
            high = ref[half:, :].astype(F32)
            straight_ref[at : at + half, :] = jnp.where(last, high, low).astype(BF16)
            crossed_ref[at : at + half, :] = jnp.where(last, low, high).astype(BF16)

    return kernel_call(
        kernel, [idx, hidden, target], [SMEM, VMEM, VMEM], [(rows, width), (rows, width)]
    )


def entered(idx, gain, straight, crossed, incoming, part, copies):
    rows, width = straight.shape[0] // 2, straight.shape[1]
    arrays = [straight, crossed] + ([] if incoming is None else [incoming])

    def kernel(idx_ref, gain_ref, s_ref, c_ref, *refs):
        out_ref, states_ref = refs[-2:]
        x = jnp.where(
            idx_ref[1] == part, s_ref[:rows, :].astype(F32), c_ref[:rows, :].astype(F32)
        )
        if incoming is not None:
            x = jnp.where(idx_ref[3] == 0, x, refs[0][...].astype(F32))
        scale = lax.rsqrt(jnp.mean(x * x, axis=-1, keepdims=True) + 1e-06)
        y = (x * scale * gain_ref[...]).astype(BF16)
        for k in range(copies):
            out_ref[k * rows : (k + 1) * rows, :] = y
        states_ref[...] = x.astype(BF16)

    return kernel_call(
        kernel,
        [idx, gain, *arrays],
        [SMEM, VMEM] + [VMEM] * len(arrays),
        [(copies * rows, width), (rows, width)],
    )


def left(idx, outs, straight, crossed):
    rows, width = outs[0][0].shape
    flat = [o for group in outs for o in group]

    def kernel(idx_ref, s_ref, c_ref, *refs):
        keep_ref, cross_ref, loss_ref = refs[-3:]
        core = idx_ref[1]
        length = idx_ref[2]
        section = idx_ref[3]
        mp = idx_ref[5]
        total = None
        chosen = []
        for h, group in enumerate(outs):
            ins = refs[h * len(group) : (h + 1) * len(group)]
            out = ins[0][...].astype(F32)
            for layer in range(1, len(group)):
                out = jnp.where(section == layer, ins[layer][...].astype(F32), out)
            chosen.append(out)
            target = jnp.where(
                core == h, s_ref[rows:, :].astype(F32), c_ref[rows:, :].astype(F32)
            )
            row = lax.broadcasted_iota(jnp.int32, (rows, width), 0)
            live = h * (rows * idx_ref[6]) + mp * rows + row < length
            error = jnp.where(live, (out - target) * (out - target), 0.0)
            error = jnp.sum(jnp.sum(error, axis=1, keepdims=True), axis=0, keepdims=True)
            total = error if total is None else total + error
        keep_ref[...] = jnp.where(core == 0, chosen[0], chosen[1]).astype(BF16)
        cross_ref[...] = jnp.where(core == 0, chosen[1], chosen[0]).astype(BF16)
        loss_ref[...] = jnp.broadcast_to(total[:, :, None], loss_ref.shape)

    return kernel_call(
        kernel,
        [idx, straight, crossed, *flat],
        [SMEM] + [VMEM] * (2 + len(flat)),
        [(rows, width), (rows, width), (16, 1, 128, F32)],
    )


def rejoined(idx, kept, crossed):
    rows, width = kept.shape

    def kernel(idx_ref, k_ref, c_ref, out_ref):
        last = idx_ref[4] == 1
        a = k_ref[...].astype(F32)
        b = c_ref[...].astype(F32)
        out_ref[:rows, :] = jnp.where(last, b, a).astype(BF16)
        out_ref[rows:, :] = jnp.where(last, a, b).astype(BF16)

    return kernel_call(kernel, [idx, kept, crossed], [SMEM, VMEM, VMEM], [(2 * rows, width)])


def weight(refs, d, k):
    own, near, low, high, far = refs
    if d == 2:
        return (low, high)[k][...]
    return (own, near, None, far)[d][k]


def part_of(idx_ref, step):
    return jnp.clip(step - idx_ref[3], 0, 1)


def project(idx, step, normed, own, peer, cosine, sine):
    tokens, width = normed.shape
    quarter = width // 4

    def kernel(idx_ref, x_ref, cos_ref, sin_ref, *refs):
        q_ref, kv_ref = refs[-2:]
        x_index = idx_ref[0]
        core = idx_ref[1]
        part_index = part_of(idx_ref, step)
        sums = [None] * 4
        for d in range(4):
            at = pl.multiple_of((x_index ^ d) * quarter, 128)
            part = x_ref[:, pl.ds(at, quarter)]
            for k in range(4):
                w = weight(refs[5 * (k // 2) : 5 * (k // 2) + 5], d, k % 2)
                prod = jnp.dot(part, w, preferred_element_type=F32)
                sums[k] = prod if d == 0 else sums[k] + prod
        q_mine, mine, q_theirs, theirs = sums
        cos = cos_ref[part_index]
        sin = sin_ref[part_index]
        for at, q in ((0, q_mine), (tokens, q_theirs)):
            a = q[:, :128]
            b = q[:, 128:]
            q_ref[at : at + tokens, :128] = (a * cos - b * sin).astype(BF16)
            q_ref[at : at + tokens, 128:] = (b * cos + a * sin).astype(BF16)
        first = core == 0
        k_mine = mine[:, :128].astype(BF16).astype(F32)
        k_theirs = theirs[:, :128].astype(BF16).astype(F32)
        a = jnp.where(first, k_mine, k_theirs)
        b = jnp.where(first, k_theirs, k_mine)
        kv_ref[:, :128] = (a * cos - b * sin).astype(BF16)
        kv_ref[:, 128:256] = (b * cos + a * sin).astype(BF16)
        kv_ref[:, 256:384] = jnp.where(first, mine[:, 128:], theirs[:, 128:]).astype(BF16)
        kv_ref[:, 384:] = jnp.where(first, theirs[:, 128:], mine[:, 128:]).astype(BF16)

    return kernel_call(
        kernel,
        [idx, normed, cosine, sine, *own, *peer],
        [SMEM] + [VMEM] * 13,
        [(2 * tokens, 256), (tokens, 512)],
    )


def attend(idx, step, queries, blocks, own, peer, rows):
    tokens = queries.shape[0] // 2
    quarter = own[0].shape[2]
    part_rows = 2 * tokens

    def kernel(idx_ref, q_ref, *refs):
        out_ref = refs[-1]
        kv_refs = refs[:4]
        weights = refs[4:-1]
        x_index = idx_ref[0]
        core = idx_ref[1]
        length = idx_ref[2]
        part_index = part_of(idx_ref, step)

        def positions(dim, part, which):
            i = lax.broadcasted_iota(jnp.int32, (2 * tokens, tokens), dim) % tokens
            return part * part_rows + (i // rows) * (2 * rows) + which * rows + i % rows

        q_pos = positions(0, part_index, core)
        q = q_ref[...]
        numerators = []
        total = None
        for n, kv_ref in enumerate(kv_refs):
            k_pos = positions(1, part_index - 1 + n // 2, core if n % 2 == 0 else 1 - core)
            allowed = (k_pos <= q_pos) & (k_pos < length) & (k_pos >= 0)
            scores = lax.dot_general(
                q,
                kv_ref[:, :256],
                (((1,), (1,)), ((), ())),
                preferred_element_type=F32,
            ) * HEAD_DIM ** (-0.5)
            capped = 50.0 * jnp.tanh(scores / 50.0)
            numerators.append(jnp.where(allowed, jnp.exp(capped), 0.0))
            added = jnp.sum(numerators[-1], axis=-1, keepdims=True)
            total = added if total is None else total + added
        context = None
        for num, kv_ref in zip(numerators, kv_refs):
            prod = jnp.dot(
                (num / total).astype(BF16), kv_ref[:, 256:], preferred_element_type=F32
            )
            context = prod if context is None else context + prod
        context = context.astype(BF16)
        lefts = [
            context[c * tokens : (c + 1) * tokens, h * 128 : (h + 1) * 128]
            for c in range(2)
            for h in range(2)
        ]
        for d in range(4):
            out = None
            for k in range(4):
                w = weight(weights[5 * (k // 2) : 5 * (k // 2) + 5], d, k % 2)
                prod = jnp.dot(lefts[k], w, preferred_element_type=F32)
                out = prod if out is None else out + prod
            at = pl.multiple_of((x_index ^ d) * quarter, 128)
            out_ref[:, pl.ds(at, quarter)] = out.astype(BF16)

    return kernel_call(
        kernel,
        [idx, queries, *blocks, *own, *peer],
        [SMEM] + [VMEM] * 15,
        [(tokens, 4 * quarter)],
    )


def normed_copies(states, gain, copies):
    rows, width = states.shape

    def kernel(states_ref, gain_ref, out_ref):
        x = states_ref[...].astype(F32)
        scale = lax.rsqrt(jnp.mean(x * x, axis=-1, keepdims=True) + 1e-06)
        y = (x * scale * gain_ref[...]).astype(BF16)
        for k in range(copies):
            out_ref[k * rows : (k + 1) * rows, :] = y

    return kernel_call(kernel, [states, gain], [VMEM] * 2, [(copies * rows, width)])


def finished(pieces, states, gain):
    rows, width = states.shape
    copies = pieces.shape[0] // rows

    def kernel(p_ref, states_ref, gain_ref, out_ref):
        total = p_ref[:rows, :].astype(F32)
        for k in range(1, copies):
            total = total + p_ref[k * rows : (k + 1) * rows, :].astype(F32)
        scale = lax.rsqrt(jnp.mean(total * total, axis=-1, keepdims=True) + 1e-06)
        out = states_ref[...].astype(F32) + total * scale * gain_ref[...]
        out_ref[...] = out.astype(BF16)

    return kernel_call(kernel, [pieces, states, gain], [VMEM] * 3, [states.shape])


NEAR, FAR = 1, 3


def first_halves(plan, scale, sources):
    sent = [share_call(plan, scale, [(s, 8 * i, ())], 2, False) for i, s in enumerate(sources)]
    return sent, [exchanged(s, "task", (NEAR, FAR)[i]) for i, s in enumerate(sent)]


def second_halves(plan, scale, sources, got):
    sent = []
    for i, s in enumerate(sources):
        mine = got[i]
        if sent:
            mine, _ = lax.optimization_barrier((mine, sent[0]))
        sent.append(share_call(plan, scale, [(s, 8 * i + 2, ((mine, 8 * i + 3),))], 1, False))
    return sent, [exchanged(s, "task", (FAR, NEAR)[i]) for i, s in enumerate(sent)]


def shares(plan, scale, sources, got, more):
    jobs = [
        (s, 8 * i + 4, ((got[i], 8 * i + 5), (more[i], None))) for i, s in enumerate(sources)
    ]
    return share_call(plan, scale, jobs, 1, True)


def neighbours(own):
    return exchanged(own, "task", NEAR), exchanged(own, "task", FAR)


def completed(own, near, far):
    return own, near, exchanged(far[0], "task", NEAR), exchanged(near[1], "task", FAR), far


def of_partner(pieces):
    return tuple(exchanged(p, "mp", 1) for p in pieces)


def per_device(
    hidden_in,
    lengths,
    layer_targets,
    task_weights,
    norm_gains,
    query_weight,
    key_weight,
    value_weight,
    output_weight,
    query_fisher,
    key_fisher,
    value_fisher,
    output_fisher,
):
    x_index = lax.axis_index("task")
    mp_index = lax.axis_index("mp")
    section_index = lax.axis_index("section")
    core = mp_index % 2
    chips = lax.axis_size("mp") // 2
    groups = [[2 * z + c for z in range(chips)] for c in range(2)]
    sections = lax.axis_size("section")
    width = hidden_in.shape[2]
    parts = 2
    rows = hidden_in.shape[1] // parts
    length = lengths[0]
    pre_gain = norm_gains[0, 0:1]
    post_gain = norm_gains[0, 1:2]
    scale = lax.dynamic_slice_in_dim(task_weights, x_index, 1)

    b = x_index // 2
    a = (x_index % 2) ^ b

    def block_a(h1, h2):
        return jnp.where(h1 == 0, 3 * h2, 1 + h2)

    def block_b(h1, h2):
        return jnp.where(h1 == 0, h2, 3 - h2)

    zero = jnp.zeros_like(a)
    plan = jnp.stack(
        [
            block_a(1 - a, 0),
            block_a(1 - a, 1),
            block_a(a, 1 - b),
            1 - b,
            x_index,
            b,
            zero,
            zero,
            block_b(1 - b, 0),
            block_b(1 - b, 1),
            block_b(b, 1 - a),
            1 - a,
            x_index,
            a,
            zero,
            zero,
        ]
    ).astype(jnp.int32)
    scalars = jnp.stack(
        [x_index, core, length, section_index, mp_index // chips, mp_index, 2 * chips]
    ).astype(jnp.int32)

    def quarters(array):
        array = array[0, 0]
        return array.reshape(4, array.shape[0] // 4, array.shape[1])

    def cut_rows(ref, block, row, sub):
        return ref.at[block, pl.ds(row, sub), :]

    def cut_columns(start):
        def cut(ref, block, row, sub):
            at = pl.multiple_of(block * (width // 4), 128)
            return ref.at[pl.ds(start + row, sub), pl.ds(at, width // 4)]

        return cut

    qkv_sources = (
        ((quarters(query_weight),), (quarters(query_fisher),), width // 4, (256,), cut_rows),
        (
            (quarters(key_weight), quarters(value_weight)),
            (quarters(key_fisher), quarters(value_fisher)),
            width // 4,
            (128, 128),
            cut_rows,
        ),
    )
    out_sources = tuple(
        (
            (output_weight[0, 0],),
            (output_fisher[0, 0],),
            128,
            (width // 4,),
            cut_columns(start),
        )
        for start in (0, 128)
    )

    part_rows = 2 * rows * chips
    positions = (
        part_rows * jnp.arange(parts, dtype=jnp.int32)[:, None, None]
        + 2 * rows * jnp.arange(chips, dtype=jnp.int32)[None, :, None]
        + core * rows
        + jnp.arange(rows, dtype=jnp.int32)[None, None, :]
    ).reshape(parts, -1)
    frequency = 10000.0 ** (-2.0 * jnp.arange(HEAD_DIM // 2, dtype=F32) / HEAD_DIM)
    angles = positions.astype(F32)[:, :, None] * frequency[None, None, :]
    cosine = jnp.cos(angles)
    sine = jnp.sin(angles)

    def spread(array):
        pieces = array.reshape(chips, rows, width)
        moved = lax.all_to_all(pieces, "mp", 0, 0, tiled=True, axis_index_groups=groups)
        return moved.reshape(chips * rows, width)

    straight = [(m, 2 * m) for m in range(chips)]
    straight += [(m, 2 * (m - chips) + 1) for m in range(chips, 2 * chips)]
    crossed = [(m, 2 * m + 1) for m in range(chips)]
    crossed += [(m, 2 * (m - chips)) for m in range(chips, 2 * chips)]

    def over_mp(array, pairs):
        return lax.ppermute(array, "mp", pairs)

    def projected(t, normed):
        queries, kv = project(scalars, t, normed, qkv_own, qkv_peer, cosine, sine)
        return queries, (kv, exchanged(kv, "mp", 1))

    with jax.named_scope("merge"):
        out_sent, out_got = first_halves(plan, scale, out_sources)
        plan, _ = lax.optimization_barrier((plan, out_sent))
        qkv_sent, qkv_got = first_halves(plan, scale, qkv_sources)
        rows_in, rows_target, _ = lax.optimization_barrier(
            (hidden_in[0], layer_targets[0, 0], qkv_sent)
        )
        one, other = dealing(scalars, rows_in, rows_target)
        one, other = over_mp(one, straight), over_mp(other, crossed)
        first, states = entered(scalars, pre_gain, one, other, None, 0, chips)
        first, cosine, sine = lax.optimization_barrier((first, cosine, sine))
        first = spread(first)
        out_got, first = lax.optimization_barrier((out_got, first))
        out_sent, out_more = second_halves(plan, scale, out_sources, out_got)
        qkv_got = [lax.optimization_barrier((got, out_sent))[0] for got in qkv_got]
        qkv_sent, qkv_more = second_halves(plan, scale, qkv_sources, qkv_got)
        qkv_more, out_more = lax.optimization_barrier((qkv_more, out_more))
        qkv_share = shares(plan, scale, qkv_sources, qkv_got, qkv_more)
        qkv_first = neighbours(qkv_share)
        out_more, _ = lax.optimization_barrier((out_more, qkv_share))
        out_share = shares(plan, scale, out_sources, out_got, out_more)
        out_first = neighbours(out_share)
        share, near, low, high, far = completed(qkv_share, *qkv_first)
        out_first, low, high = lax.optimization_barrier((out_first, low, high))
        qkv_own = (share, near, low, high, far)
        qkv_peer = of_partner(qkv_own)
        out_own = completed(out_share, *out_first)
        out_peer = of_partner(out_own)
    with jax.named_scope("layer"):
        queries, kv = projected(0, first)
    outs = []
    before = kv
    for t in range(sections + parts - 1):
        with jax.named_scope("layer"):
            if t > 0:
                incoming = lax.ppermute(
                    outs[-1], "section", [(i, i + 1) for i in range(sections - 1)]
                )
                if t < parts:
                    normed, states = entered(scalars, pre_gain, one, other, incoming, t, chips)
                else:
                    normed, states = normed_copies(incoming, pre_gain, chips), incoming
                before = kv
                queries, kv = projected(t, spread(normed))
            partial = attend(scalars, t, queries, (*before, *kv), out_own, out_peer, rows)
            outs.append(finished(spread(partial), states, post_gain))
    with jax.named_scope("loss"):
        kept, moved, error = left(
            scalars, [outs[h : h + sections] for h in range(parts)], one, other
        )
        error = lax.all_to_all(error, "mp", 0, 0, tiled=True)
        kept = over_mp(kept, [(j, i) for i, j in straight])
        moved = over_mp(moved, [(j, i) for i, j in crossed])
        outputs = rejoined(scalars, kept, moved)
        loss = jnp.sum(error[:, 0, 0]) / (length.astype(F32) * width)
    return (outputs[None, None], loss[None, None])


def solution(mesh):
    in_specs = (
        P("task", "mp", None),
        P("task"),
        P("section", "task", "mp", None),
        P(),
        P("section", None, None),
        P("task", "section", None, "mp"),
        P("task", "section", None, "mp"),
        P("task", "section", None, "mp"),
        P("task", "section", "mp", None),
        P("task", "section", None, "mp"),
        P("task", "section", None, "mp"),
        P("task", "section", None, "mp"),
        P("task", "section", "mp", None),
    )
    out_specs = (P("section", "task", "mp", None), P("section", "task"))
    return jax.shard_map(
        per_device, mesh=mesh, in_specs=in_specs, out_specs=out_specs, check_vma=False
    )
```

```python
import functools

import jax
import jax.numpy as jnp
from jax import lax
from jax.experimental import pallas as pl
from jax.experimental.pallas import tpu as pltpu
from jax.sharding import PartitionSpec as P

HEAD_DIM = 256
F32 = jnp.float32
BF16 = jnp.bfloat16
SMEM = pltpu.SMEM
VMEM = pltpu.VMEM
HBM = pltpu.HBM


def exchanged(array, axis, mask):
    return lax.ppermute(array, axis, [(i, i ^ mask) for i in range(lax.axis_size(axis))])


def placed(array, space):
    return pltpu.with_memory_space_constraint(array, space)


def result_on_chip(shape, dtype=BF16):
    return VMEM(shape, dtype)


def kernel_call(kernel, operands, spaces, shapes, scratch=(), mib=16):
    operands = [a if space == SMEM else placed(a, space) for a, space in zip(operands, spaces)]
    outs = pl.pallas_call(
        kernel,
        out_shape=tuple(
            result_on_chip(shape[:-1], F32) if shape[-1] is F32 else result_on_chip(shape)
            for shape in shapes
        ),
        in_specs=[pl.BlockSpec(memory_space=space) for space in spaces],
        out_specs=tuple(pl.BlockSpec(memory_space=VMEM) for _ in shapes),
        scratch_shapes=scratch,
        compiler_params=pltpu.CompilerParams(vmem_limit_bytes=mib * 1024 * 1024),
        cost_estimate=pl.CostEstimate(flops=1, transcendentals=0, bytes_accessed=1),
    )(*operands)
    return outs[0] if len(shapes) == 1 else outs


def share_call(plan, scale, jobs, count, finish):
    rows = jobs[0][0][2]
    total = sum(jobs[0][0][3])
    sub = rows // 2
    parts = count * 2
    strip = 64 if sub % 64 == 0 and sub > 64 else 16
    operands = [plan, scale]
    spaces = [SMEM, SMEM]
    scratch = []
    for (weights, fishers, _, widths, _), _, received in jobs:
        n = len(weights)
        operands += [*weights, *fishers, *(array for array, _ in received)]
        spaces += [HBM] * (2 * n) + [VMEM] * len(received)
        scratch += [VMEM((parts, sub, widths[k % n]), BF16) for k in range(2 * n)]
        scratch.append(pltpu.SemaphoreType.DMA((2 * n, parts)))
    shape = (len(jobs), rows, total) if finish else (2, count, rows, total)

    def kernel(plan_ref, scale_ref, *refs):
        ins = list(refs[: len(operands) - 2])
        out_ref = refs[len(operands) - 2]
        held = list(refs[len(operands) - 1 :])
        task_scale = scale_ref[0]
        work = []
        for job, ((weights, _, _, widths, cut), base, received) in enumerate(jobs):
            n = len(weights)
            arrays = [ins.pop(0) for _ in range(2 * n)]
            gots = [ins.pop(0) for _ in received]
            buffers = [held.pop(0) for _ in range(2 * n)]
            sems = held.pop(0)
            blocks = [0 if entry is None else plan_ref[entry] for _, entry in received]

            def copy(k, part, arrays=arrays, buffers=buffers, sems=sems, base=base, cut=cut):
                return pltpu.make_async_copy(
                    cut(arrays[k], plan_ref[base + part // 2], (part % 2) * sub, sub),
                    buffers[k].at[part],
                    sems.at[k, part],
                )

            for part in range(parts):
                for k in range(2 * n):
                    copy(k, part).start()
            work.append((job, n, widths, copy, buffers, gots, blocks))

        for job, n, widths, copy, buffers, gots, blocks in work:

            def one_strip(part, i):
                inside = pl.ds(pl.multiple_of(i * strip, strip), strip)
                lines = pl.ds(pl.multiple_of((part % 2) * sub + i * strip, strip), strip)
                at = 0
                for k in range(n):
                    scaled = buffers[n + k][part, inside, :].astype(F32) * task_scale
                    term = scaled * buffers[k][part, inside, :].astype(F32)
                    sums = [term.astype(BF16), scaled.astype(BF16)]
                    cols = slice(at, at + widths[k])
                    at += widths[k]
                    for got, block in zip(gots, blocks):
                        sums = [
                            v.astype(F32) + got[i, block, lines, cols].astype(F32)
                            for i, v in enumerate(sums)
                        ]
                    if finish:
                        out_ref[job, lines, cols] = (sums[0] / sums[1]).astype(BF16)
                    else:
                        out_ref[0, part // 2, lines, cols] = sums[0].astype(BF16)
                        out_ref[1, part // 2, lines, cols] = sums[1].astype(BF16)

            def one_part(part, carry):
                for k in range(2 * n):
                    copy(k, part).wait()
                lax.fori_loop(0, sub // strip, lambda i, c: (one_strip(part, i), c)[1], 0)
                return carry

            lax.fori_loop(0, parts, one_part, 0)

    return kernel_call(kernel, operands, spaces, [shape], scratch)


def dealing(idx, hidden, target):
    rows, width = hidden.shape
    half = rows // 2

    def kernel(idx_ref, h_ref, t_ref, straight_ref, crossed_ref):
        last = idx_ref[4] == 1
        for at, ref in ((0, h_ref), (half, t_ref)):
            low = ref[:half, :].astype(F32)
            high = ref[half:, :].astype(F32)
            straight_ref[at : at + half, :] = jnp.where(last, high, low).astype(BF16)
            crossed_ref[at : at + half, :] = jnp.where(last, low, high).astype(BF16)

    return kernel_call(
        kernel, [idx, hidden, target], [SMEM, VMEM, VMEM], [(rows, width), (rows, width)]
    )


def entered(idx, gain, straight, crossed, incoming, part, copies):
    rows, width = straight.shape[0] // 2, straight.shape[1]
    arrays = [straight, crossed] + ([] if incoming is None else [incoming])

    def kernel(idx_ref, gain_ref, s_ref, c_ref, *refs):
        out_ref, states_ref = refs[-2:]
        x = jnp.where(
            idx_ref[1] == part, s_ref[:rows, :].astype(F32), c_ref[:rows, :].astype(F32)
        )
        if incoming is not None:
            x = jnp.where(idx_ref[3] == 0, x, refs[0][...].astype(F32))
        scale = lax.rsqrt(jnp.mean(x * x, axis=-1, keepdims=True) + 1e-06)
        y = (x * scale * gain_ref[...]).astype(BF16)
        for k in range(copies):
            out_ref[k * rows : (k + 1) * rows, :] = y
        states_ref[...] = x.astype(BF16)

    return kernel_call(
        kernel,
        [idx, gain, *arrays],
        [SMEM, VMEM] + [VMEM] * len(arrays),
        [(copies * rows, width), (rows, width)],
    )


def left(idx, outs, straight, crossed):
    rows, width = outs[0][0].shape
    flat = [o for group in outs for o in group]

    def kernel(idx_ref, s_ref, c_ref, *refs):
        keep_ref, cross_ref, loss_ref = refs[-3:]
        core = idx_ref[1]
        length = idx_ref[2]
        section = idx_ref[3]
        mp = idx_ref[5]
        total = None
        chosen = []
        for h, group in enumerate(outs):
            ins = refs[h * len(group) : (h + 1) * len(group)]
            out = ins[0][...].astype(F32)
            for layer in range(1, len(group)):
                out = jnp.where(section == layer, ins[layer][...].astype(F32), out)
            chosen.append(out)
            target = jnp.where(
                core == h, s_ref[rows:, :].astype(F32), c_ref[rows:, :].astype(F32)
            )
            row = lax.broadcasted_iota(jnp.int32, (rows, width), 0)
            live = h * (rows * idx_ref[6]) + mp * rows + row < length
            error = jnp.where(live, (out - target) * (out - target), 0.0)
            error = jnp.sum(jnp.sum(error, axis=1, keepdims=True), axis=0, keepdims=True)
            total = error if total is None else total + error
        keep_ref[...] = jnp.where(core == 0, chosen[0], chosen[1]).astype(BF16)
        cross_ref[...] = jnp.where(core == 0, chosen[1], chosen[0]).astype(BF16)
        loss_ref[...] = jnp.broadcast_to(total[:, :, None], loss_ref.shape)

    return kernel_call(
        kernel,
        [idx, straight, crossed, *flat],
        [SMEM] + [VMEM] * (2 + len(flat)),
        [(rows, width), (rows, width), (16, 1, 128, F32)],
    )


def rejoined(idx, kept, crossed):
    rows, width = kept.shape

    def kernel(idx_ref, k_ref, c_ref, out_ref):
        last = idx_ref[4] == 1
        a = k_ref[...].astype(F32)
        b = c_ref[...].astype(F32)
        out_ref[:rows, :] = jnp.where(last, b, a).astype(BF16)
        out_ref[rows:, :] = jnp.where(last, a, b).astype(BF16)

    return kernel_call(kernel, [idx, kept, crossed], [SMEM, VMEM, VMEM], [(2 * rows, width)])


def weight(refs, d, k):
    own, near, low, high, far = refs
    if d == 2:
        return (low, high)[k][...]
    return (own, near, None, far)[d][k]


def part_of(idx_ref, step):
    return jnp.clip(step - idx_ref[3], 0, 1)


def project(idx, step, normed, own, peer, cosine, sine):
    tokens, width = normed.shape
    quarter = width // 4

    def kernel(idx_ref, x_ref, cos_ref, sin_ref, *refs):
        q_ref, kv_ref = refs[-2:]
        x_index = idx_ref[0]
        core = idx_ref[1]
        part_index = part_of(idx_ref, step)
        sums = [None] * 4
        for d in range(4):
            at = pl.multiple_of((x_index ^ d) * quarter, 128)
            part = x_ref[:, pl.ds(at, quarter)]
            for k in range(4):
                w = weight(refs[5 * (k // 2) : 5 * (k // 2) + 5], d, k % 2)
                prod = jnp.dot(part, w, preferred_element_type=F32)
                sums[k] = prod if d == 0 else sums[k] + prod
        q_mine, mine, q_theirs, theirs = sums
        cos = cos_ref[part_index]
        sin = sin_ref[part_index]
        for at, q in ((0, q_mine), (tokens, q_theirs)):
            a = q[:, :128]
            b = q[:, 128:]
            q_ref[at : at + tokens, :128] = (a * cos - b * sin).astype(BF16)
            q_ref[at : at + tokens, 128:] = (b * cos + a * sin).astype(BF16)
        first = core == 0
        k_mine = mine[:, :128].astype(BF16).astype(F32)
        k_theirs = theirs[:, :128].astype(BF16).astype(F32)
        a = jnp.where(first, k_mine, k_theirs)
        b = jnp.where(first, k_theirs, k_mine)
        kv_ref[:, :128] = (a * cos - b * sin).astype(BF16)
        kv_ref[:, 128:256] = (b * cos + a * sin).astype(BF16)
        kv_ref[:, 256:384] = jnp.where(first, mine[:, 128:], theirs[:, 128:]).astype(BF16)
        kv_ref[:, 384:] = jnp.where(first, theirs[:, 128:], mine[:, 128:]).astype(BF16)

    return kernel_call(
        kernel,
        [idx, normed, cosine, sine, *own, *peer],
        [SMEM] + [VMEM] * 13,
        [(2 * tokens, 256), (tokens, 512)],
    )


def attend(idx, step, queries, blocks, own, peer, rows):
    tokens = queries.shape[0] // 2
    quarter = own[0].shape[2]
    part_rows = 2 * tokens

    def kernel(idx_ref, q_ref, *refs):
        out_ref = refs[-1]
        kv_refs = refs[:4]
        weights = refs[4:-1]
        x_index = idx_ref[0]
        core = idx_ref[1]
        length = idx_ref[2]
        part_index = part_of(idx_ref, step)

        def positions(dim, part, which):
            i = lax.broadcasted_iota(jnp.int32, (2 * tokens, tokens), dim) % tokens
            return part * part_rows + (i // rows) * (2 * rows) + which * rows + i % rows

        q_pos = positions(0, part_index, core)
        q = q_ref[...]
        numerators = []
        total = None
        for n, kv_ref in enumerate(kv_refs):
            k_pos = positions(1, part_index - 1 + n // 2, core if n % 2 == 0 else 1 - core)
            allowed = (k_pos <= q_pos) & (k_pos < length) & (k_pos >= 0)
            scores = lax.dot_general(
                q,
                kv_ref[:, :256],
                (((1,), (1,)), ((), ())),
                preferred_element_type=F32,
            ) * HEAD_DIM ** (-0.5)
            capped = 50.0 * jnp.tanh(scores / 50.0)
            numerators.append(jnp.where(allowed, jnp.exp(capped), 0.0))
            added = jnp.sum(numerators[-1], axis=-1, keepdims=True)
            total = added if total is None else total + added
        context = None
        for num, kv_ref in zip(numerators, kv_refs):
            prod = jnp.dot(
                (num / total).astype(BF16), kv_ref[:, 256:], preferred_element_type=F32
            )
            context = prod if context is None else context + prod
        context = context.astype(BF16)
        lefts = [
            context[c * tokens : (c + 1) * tokens, h * 128 : (h + 1) * 128]
            for c in range(2)
            for h in range(2)
        ]
        for d in range(4):
            out = None
            for k in range(4):
                w = weight(weights[5 * (k // 2) : 5 * (k // 2) + 5], d, k % 2)
                prod = jnp.dot(lefts[k], w, preferred_element_type=F32)
                out = prod if out is None else out + prod
            at = pl.multiple_of((x_index ^ d) * quarter, 128)
            out_ref[:, pl.ds(at, quarter)] = out.astype(BF16)

    return kernel_call(
        kernel,
        [idx, queries, *blocks, *own, *peer],
        [SMEM] + [VMEM] * 15,
        [(tokens, 4 * quarter)],
    )


def normed_copies(states, gain, copies):
    rows, width = states.shape

    def kernel(states_ref, gain_ref, out_ref):
        x = states_ref[...].astype(F32)
        scale = lax.rsqrt(jnp.mean(x * x, axis=-1, keepdims=True) + 1e-06)
        y = (x * scale * gain_ref[...]).astype(BF16)
        for k in range(copies):
            out_ref[k * rows : (k + 1) * rows, :] = y

    return kernel_call(kernel, [states, gain], [VMEM] * 2, [(copies * rows, width)])


def finished(pieces, states, gain):
    rows, width = states.shape
    copies = pieces.shape[0] // rows

    def kernel(p_ref, states_ref, gain_ref, out_ref):
        total = p_ref[:rows, :].astype(F32)
        for k in range(1, copies):
            total = total + p_ref[k * rows : (k + 1) * rows, :].astype(F32)
        scale = lax.rsqrt(jnp.mean(total * total, axis=-1, keepdims=True) + 1e-06)
        out = states_ref[...].astype(F32) + total * scale * gain_ref[...]
        out_ref[...] = out.astype(BF16)

    return kernel_call(kernel, [pieces, states, gain], [VMEM] * 3, [states.shape])


NEAR, FAR = 1, 3


def first_halves(plan, scale, sources):
    sent = [share_call(plan, scale, [(s, 8 * i, ())], 2, False) for i, s in enumerate(sources)]
    return sent, [exchanged(s, "task", (NEAR, FAR)[i]) for i, s in enumerate(sent)]


def second_halves(plan, scale, sources, got):
    sent = []
    for i, s in enumerate(sources):
        mine = got[i]
        if sent:
            mine, _ = lax.optimization_barrier((mine, sent[0]))
        sent.append(share_call(plan, scale, [(s, 8 * i + 2, ((mine, 8 * i + 3),))], 1, False))
    return sent, [exchanged(s, "task", (FAR, NEAR)[i]) for i, s in enumerate(sent)]


def shares(plan, scale, sources, got, more):
    jobs = [
        (s, 8 * i + 4, ((got[i], 8 * i + 5), (more[i], None))) for i, s in enumerate(sources)
    ]
    return share_call(plan, scale, jobs, 1, True)


def neighbours(own):
    return exchanged(own, "task", NEAR), exchanged(own, "task", FAR)


def completed(own, near, far):
    return own, near, exchanged(far[0], "task", NEAR), exchanged(near[1], "task", FAR), far


def of_partner(pieces):
    return tuple(exchanged(p, "mp", 1) for p in pieces)


def per_device(
    hidden_in,
    lengths,
    layer_targets,
    task_weights,
    norm_gains,
    query_weight,
    key_weight,
    value_weight,
    output_weight,
    query_fisher,
    key_fisher,
    value_fisher,
    output_fisher,
):
    x_index = lax.axis_index("task")
    mp_index = lax.axis_index("mp")
    section_index = lax.axis_index("section")
    core = mp_index % 2
    chips = lax.axis_size("mp") // 2
    groups = [[2 * z + c for z in range(chips)] for c in range(2)]
    sections = lax.axis_size("section")
    width = hidden_in.shape[2]
    parts = 2
    rows = hidden_in.shape[1] // parts
    length = lengths[0]
    pre_gain = norm_gains[0, 0:1]
    post_gain = norm_gains[0, 1:2]
    scale = lax.dynamic_slice_in_dim(task_weights, x_index, 1)

    b = x_index // 2
    a = (x_index % 2) ^ b

    def block_a(h1, h2):
        return jnp.where(h1 == 0, 3 * h2, 1 + h2)

    def block_b(h1, h2):
        return jnp.where(h1 == 0, h2, 3 - h2)

    zero = jnp.zeros_like(a)
    plan = jnp.stack(
        [
            block_a(1 - a, 0),
            block_a(1 - a, 1),
            block_a(a, 1 - b),
            1 - b,
            x_index,
            b,
            zero,
            zero,
            block_b(1 - b, 0),
            block_b(1 - b, 1),
            block_b(b, 1 - a),
            1 - a,
            x_index,
            a,
            zero,
            zero,
        ]
    ).astype(jnp.int32)
    scalars = jnp.stack(
        [x_index, core, length, section_index, mp_index // chips, mp_index, 2 * chips]
    ).astype(jnp.int32)

    def quarters(array):
        array = array[0, 0]
        return array.reshape(4, array.shape[0] // 4, array.shape[1])

    def cut_rows(ref, block, row, sub):
        return ref.at[block, pl.ds(row, sub), :]

    def cut_columns(start):
        def cut(ref, block, row, sub):
            at = pl.multiple_of(block * (width // 4), 128)
            return ref.at[pl.ds(start + row, sub), pl.ds(at, width // 4)]

        return cut

    qkv_sources = (
        ((quarters(query_weight),), (quarters(query_fisher),), width // 4, (256,), cut_rows),
        (
            (quarters(key_weight), quarters(value_weight)),
            (quarters(key_fisher), quarters(value_fisher)),
            width // 4,
            (128, 128),
            cut_rows,
        ),
    )
    out_sources = tuple(
        (
            (output_weight[0, 0],),
            (output_fisher[0, 0],),
            128,
            (width // 4,),
            cut_columns(start),
        )
        for start in (0, 128)
    )

    part_rows = 2 * rows * chips
    positions = (
        part_rows * jnp.arange(parts, dtype=jnp.int32)[:, None, None]
        + 2 * rows * jnp.arange(chips, dtype=jnp.int32)[None, :, None]
        + core * rows
        + jnp.arange(rows, dtype=jnp.int32)[None, None, :]
    ).reshape(parts, -1)
    frequency = 10000.0 ** (-2.0 * jnp.arange(HEAD_DIM // 2, dtype=F32) / HEAD_DIM)
    angles = positions.astype(F32)[:, :, None] * frequency[None, None, :]
    cosine = jnp.cos(angles)
    sine = jnp.sin(angles)

    def spread(array):
        pieces = array.reshape(chips, rows, width)
        moved = lax.all_to_all(pieces, "mp", 0, 0, tiled=True, axis_index_groups=groups)
        return moved.reshape(chips * rows, width)

    straight = [(m, 2 * m) for m in range(chips)]
    straight += [(m, 2 * (m - chips) + 1) for m in range(chips, 2 * chips)]
    crossed = [(m, 2 * m + 1) for m in range(chips)]
    crossed += [(m, 2 * (m - chips)) for m in range(chips, 2 * chips)]

    def over_mp(array, pairs):
        return lax.ppermute(array, "mp", pairs)

    def projected(t, normed):
        queries, kv = project(scalars, t, normed, qkv_own, qkv_peer, cosine, sine)
        return queries, (kv, exchanged(kv, "mp", 1))

    with jax.named_scope("merge"):
        out_sent, out_got = first_halves(plan, scale, out_sources)
        plan, _ = lax.optimization_barrier((plan, out_sent))
        qkv_sent, qkv_got = first_halves(plan, scale, qkv_sources)
        rows_in, rows_target, _ = lax.optimization_barrier(
            (hidden_in[0], layer_targets[0, 0], qkv_sent)
        )
        one, other = dealing(scalars, rows_in, rows_target)
        one, other = over_mp(one, straight), over_mp(other, crossed)
        first, states = entered(scalars, pre_gain, one, other, None, 0, chips)
        first, cosine, sine = lax.optimization_barrier((first, cosine, sine))
        first = spread(first)
        out_got, first = lax.optimization_barrier((out_got, first))
        out_sent, out_more = second_halves(plan, scale, out_sources, out_got)
        qkv_got = [lax.optimization_barrier((got, out_sent))[0] for got in qkv_got]
        qkv_sent, qkv_more = second_halves(plan, scale, qkv_sources, qkv_got)
        qkv_more, out_more = lax.optimization_barrier((qkv_more, out_more))
        qkv_share = shares(plan, scale, qkv_sources, qkv_got, qkv_more)
        qkv_first = neighbours(qkv_share)
        out_more, _ = lax.optimization_barrier((out_more, qkv_share))
        out_share = shares(plan, scale, out_sources, out_got, out_more)
        out_first = neighbours(out_share)
        share, near, low, high, far = completed(qkv_share, *qkv_first)
        late, low, high = lax.optimization_barrier((out_first, low, high))
        qkv_own = (share, near, low, high, far)
        qkv_peer = of_partner(qkv_own)
        _, _, out_low, out_high, _ = completed(out_share, *late)
        out_own = (out_share, out_first[0], out_low, out_high, out_first[1])
        out_peer = of_partner(out_own)
    with jax.named_scope("layer"):
        queries, kv = projected(0, first)
    outs = []
    before = kv
    for t in range(sections + parts - 1):
        with jax.named_scope("layer"):
            if t > 0:
                incoming = lax.ppermute(
                    outs[-1], "section", [(i, i + 1) for i in range(sections - 1)]
                )
                if t < parts:
                    normed, states = entered(scalars, pre_gain, one, other, incoming, t, chips)
                else:
                    normed, states = normed_copies(incoming, pre_gain, chips), incoming
                before = kv
                queries, kv = projected(t, spread(normed))
            partial = attend(scalars, t, queries, (*before, *kv), out_own, out_peer, rows)
            outs.append(finished(spread(partial), states, post_gain))
    with jax.named_scope("loss"):
        kept, moved, error = left(
            scalars, [outs[h : h + sections] for h in range(parts)], one, other
        )
        error = lax.all_to_all(error, "mp", 0, 0, tiled=True)
        kept = over_mp(kept, [(j, i) for i, j in straight])
        moved = over_mp(moved, [(j, i) for i, j in crossed])
        outputs = rejoined(scalars, kept, moved)
        loss = jnp.sum(error[:, 0, 0]) / (length.astype(F32) * width)
    return (outputs[None, None], loss[None, None])


def solution(mesh):
    in_specs = (
        P("task", "mp", None),
        P("task"),
        P("section", "task", "mp", None),
        P(),
        P("section", None, None),
        P("task", "section", None, "mp"),
        P("task", "section", None, "mp"),
        P("task", "section", None, "mp"),
        P("task", "section", "mp", None),
        P("task", "section", None, "mp"),
        P("task", "section", None, "mp"),
        P("task", "section", None, "mp"),
        P("task", "section", "mp", None),
    )
    out_specs = (P("section", "task", "mp", None), P("section", "task"))
    return jax.shard_map(
        per_device, mesh=mesh, in_specs=in_specs, out_specs=out_specs, check_vma=False
    )
```
